32 devices in a mesh: section: 4 (over y, x), tensor: 8 (over z, core).
Axes of the slice: x: 2, y: 2, z: 4, core: 2. Of those that a mesh axis runs over, the one named last changes fastest.
Arguments:
- hidden_last: bfloat16 [512, 6656], P(None, 'tensor'), may hold values from -6 to 6
- labels: int32 [512], replicated, may hold values from 0 to 31999
- head_weight: bfloat16 [6656, 32000], P(None, 'tensor'), may hold values from -0.21875 to 0.21875
- layer_inputs: bfloat16 [4, 512, 6656], P('section', None, 'tensor'), may hold values from -6 to 6
- weights: bfloat16 [4, 6656, 6656], P('section', 'tensor'), may hold values from -0.078125 to 0.078125
- row_state: float32 [4, 6656], P('section', 'tensor'), may hold values from 1.173753e-06 to 0.000498845
- col_state: float32 [4, 6656], P('section'), may hold values from 1e-08 to 1e-06
Outputs:
- loss: float32 [], replicated
- input_grads: bfloat16 [4, 512, 6656], P('section', None, 'tensor')
- new_weights: bfloat16 [4, 6656, 6656], P('section', 'tensor')
- new_row_state: float32 [4, 6656], P('section', 'tensor')
- new_col_state: float32 [4, 6656], P('section')
The draws below stay inside these ranges and needn't reach their ends.
All inputs are finite; a program needn't handle non-finite values.
Results may differ from the reference program's by a relative error of at most 0.007.
Values may be sent and summed in bfloat16 or wider, within the bound.
A program may use at most 192 MiB of HBM per device.

```python
import math
import jax
import jax.numpy as jnp
from jax import lax

D = 6656
VOCAB = 32000
SECTIONS = 4
TOKENS = 512


def draw_row_state(key, part):
    base_scale = 9.0 / (TOKENS * D)
    end_factor = 30.0
    position = jnp.arange(D, dtype=jnp.float32) / (D - 1)
    rising = jnp.exp(position * math.log(end_factor))
    roughness = jnp.exp(jax.random.uniform(key, (SECTIONS, D), jnp.float32, math.log(0.5), math.log(2.0)))
    return (base_scale * rising[None, :] * roughness).astype(jnp.float32)


def with_ends(result, key, least, largest):
    longest = result.shape.index(max(result.shape))
    spots = []
    for shift in (0, 1):
        where = [jax.random.randint(jax.random.fold_in(key, axis), (), 0, length) for axis, length in enumerate(result.shape)]
        where[longest] = (where[longest] + shift) % result.shape[longest]
        spots.append(tuple(where))
    return result.at[spots[0]].set(least).at[spots[1]].set(largest)


def block_levels(stream_key, shape, cuts, smallest, high):
    factor_of, own = 1.0, jax.random.fold_in(stream_key, 6)
    for dim, shards_of in cuts:
        draws = jnp.exp(jax.random.uniform(jax.random.fold_in(own, dim), (shards_of,), jnp.float32, smallest / len(cuts), high / len(cuts)))
        factor_of = factor_of * jnp.repeat(draws, shape[dim] // shards_of).reshape([-1 if axis == dim else 1 for axis in range(len(shape))])
    return factor_of


def scatter_about(stream_key, dims, deviation, limit, shards=(), kind=jnp.bfloat16):
    gain = block_levels(stream_key, dims, shards, -0.22, 0.18) if shards else 1.0
    drawn = jax.random.normal(stream_key, dims, jnp.float32) * deviation * gain
    return jnp.minimum(jnp.maximum(drawn, -limit), limit).astype(kind)


def setup_inputs(seed: int = 0) -> dict:
    key_of = jax.random.split(jax.random.key(seed), 8)
    return {
        "hidden_last": scatter_about(key_of[0], (TOKENS, D), 1.0, 6.0, ((1, 8),)),
        "labels": with_ends(jax.random.randint(key_of[1], (TOKENS,), 0, VOCAB), jax.random.fold_in(key_of[1], 1), 0, VOCAB - 1).astype(jnp.int32),
        "head_weight": scatter_about(key_of[2], (D, VOCAB), (D // 9) ** -0.5, 0.21875, ((1, 8),)),
        "layer_inputs": scatter_about(key_of[3], (SECTIONS, TOKENS, D), 1.0, 6.0, ((0, 4), (2, 8))),
        "weights": scatter_about(key_of[4], (SECTIONS, D, D), D ** -0.5, 0.078125, ((0, 4), (1, 8))),
        "row_state": draw_row_state(jax.random.fold_in(key_of[7], 71), 0),
        "col_state": jnp.clip(jnp.exp(math.log(9.999999974752427e-07) - 4.6051702 * jax.random.uniform(key_of[6], (SECTIONS, D), jnp.float32) ** block_levels(key_of[6], (SECTIONS, D), ((0, 4),), -0.2, 0.2)), 9.99999993922529e-09, 9.999999974752427e-07),
    }


decay_rate = 0.9
learn_rate = 0.3
tiny_term = 1e-30

def adalomo(gradient, weight, row_prev, col_prev):
    model_width = weight.shape[0]
    squares = gradient * gradient + tiny_term
    row_new = decay_rate * row_prev + (1.0 - decay_rate) * lax.optimization_barrier(jnp.mean(squares, axis=1))
    col_new = decay_rate * col_prev + (1.0 - decay_rate) * lax.optimization_barrier(jnp.mean(squares, axis=0))
    second = row_new[:, None] * col_new[None, :] / jnp.sum(row_new)
    update = gradient / jnp.sqrt(second)
    entries = float(model_width * model_width)
    weight_float = weight.astype(jnp.float32)
    update_rms = jnp.sqrt(jnp.sum(update * update) / entries)
    weight_rms = jnp.sqrt(jnp.sum(weight_float * weight_float) / entries)
    factor = learn_rate * weight_rms / jnp.maximum(1.0, update_rms)
    return ((weight_float - factor * update).astype(jnp.bfloat16), row_new, col_new)

def reference(hidden_last, labels, head_weight, layer_inputs, weights, row_state, col_state):
    all_rows = labels.shape[0]
    logits = jnp.dot(hidden_last, head_weight, preferred_element_type=jnp.float32)
    exponent = jnp.exp(logits)
    label_hit = labels[:, None] == jnp.arange(head_weight.shape[1], dtype=jnp.int32)[None, :]
    denominator = lax.optimization_barrier(jnp.sum(exponent, axis=1))
    picked = lax.optimization_barrier(jnp.sum(jnp.where(label_hit, logits, jnp.zeros_like(logits)), axis=1))
    loss = jnp.sum(jnp.log(denominator) - picked) / all_rows
    logit_grad = ((exponent / denominator[:, None] - label_hit.astype(jnp.float32)) / all_rows).astype(jnp.bfloat16)
    carried = jnp.dot(logit_grad, head_weight.T, preferred_element_type=jnp.float32).astype(jnp.bfloat16)
    grads_list, weight_list, row_list, col_list = ([], [], [], [])
    for layer_index in reversed(range(weights.shape[0])):
        weight = weights[layer_index]
        saved = layer_inputs[layer_index]
        backward = jnp.dot(carried, weight.T, preferred_element_type=jnp.float32)
        input_grad = (carried.astype(jnp.float32) + backward).astype(jnp.bfloat16)
        gradient = jnp.dot(saved.T, carried, preferred_element_type=jnp.float32)
        new_weight, row_new, col_new = adalomo(gradient, weight, row_state[layer_index], col_state[layer_index])
        grads_list.insert(0, input_grad)
        weight_list.insert(0, new_weight)
        row_list.insert(0, row_new)
        col_list.insert(0, col_new)
        carried = input_grad
    return (loss, jnp.stack(grads_list), jnp.stack(weight_list), jnp.stack(row_list), jnp.stack(col_list))
```

```python
import functools

import jax
import jax.numpy as jnp
from jax import lax
from jax.experimental import pallas as pl
from jax.experimental.pallas import tpu as pltpu
from jax.sharding import PartitionSpec as P

decay_rate = 0.9
learn_rate = 0.3
tiny_term = 1e-30


MESH = pl.DeviceIdType.MESH


def gather_kernel(tensors, x_ref, g_ref, send_ring, recv_ring, send_mate, recv_mate, own_sem):
    me = lax.axis_index("tensor")
    chips = tensors // 2
    chip, core = me // 2, me % 2
    right = lax.rem(chip + 1, chips) * 2 + core
    left = lax.rem(chip + chips - 1, chips) * 2 + core
    mate = chip * 2 + 1 - core
    features = x_ref.shape[0]
    half = features // 2 // 16 * 16
    reach = chips // 2

    barrier = pltpu.get_barrier_semaphore()
    greeted = [mate] + ([right, left] if reach else [])
    for device in greeted:
        pl.semaphore_signal(barrier, inc=1, device_id={"tensor": device}, device_id_type=MESH)
    pl.semaphore_wait(barrier, len(greeted))

    def copy(way, distance, origin, to_mate):
        low, size = 0, features
        if distance and 2 * distance == chips:
            low, size = (0, half) if way == 0 else (half, features - half)
        where = g_ref.at[pl.ds(pl.multiple_of(origin * features + low, 16), size), :]
        own = (distance == 0) if to_mate else (distance == 1)
        slot = 0 if distance == 0 else way * reach + distance - 1 + int(to_mate)
        send, recv = (send_mate, recv_mate) if to_mate else (send_ring, recv_ring)
        target = mate if to_mate else (right if way == 0 else left)
        return pltpu.make_async_remote_copy(
            src_ref=x_ref.at[pl.ds(low, size), :] if own else where, dst_ref=where,
            send_sem=send.at[slot], recv_sem=recv.at[slot],
            device_id={"tensor": target}, device_id_type=MESH,
        )

    def origin_of(way, distance):
        there = chip - distance if way == 0 else chip + distance
        return lax.rem(there + chips, chips) * 2 + core

    sent = []

    def start(*args):
        copy(*args).start()
        sent.append(args)

    own_block = g_ref.at[pl.ds(pl.multiple_of(me * features, 16), features), :]
    keep = pltpu.make_async_copy(x_ref, own_block, own_sem.at[0])
    if reach:
        start(0, 1, me, False)
        start(1, 1, me, False)
    start(0, 0, me, True)
    keep.start()
    for distance in range(1, reach + 1):
        for way in (0, 1):
            origin = origin_of(way, distance)
            copy(way, distance, origin, False).wait_recv()
            if distance < reach:
                start(way, distance + 1, origin, False)
            start(way, distance, origin, True)
    other = 1 - 2 * core
    copy(0, 0, me + other, True).wait_recv()
    for distance in range(1, reach + 1):
        for way in (0, 1):
            copy(way, distance, origin_of(way, distance) + other, True).wait_recv()
    keep.wait()
    for args in sent:
        copy(*args).wait_send()


def gather_rows(x, collective_id):
    tensors = lax.axis_size("tensor")
    ring = max(2 * (tensors // 4), 1)
    vmem = pl.BlockSpec(memory_space=pltpu.VMEM)
    dma = pltpu.SemaphoreType.DMA
    return pl.pallas_call(
        functools.partial(gather_kernel, tensors),
        out_shape=jax.ShapeDtypeStruct((tensors * x.shape[0], x.shape[1]), x.dtype),
        in_specs=[vmem],
        out_specs=vmem,
        scratch_shapes=[dma((ring,)), dma((ring,)), dma((ring + 1,)), dma((ring + 1,)), dma((1,))],
        compiler_params=pltpu.CompilerParams(
            collective_id=collective_id, has_side_effects=True, vmem_limit_bytes=24 * 1024 * 1024
        ),
    )(x)


def scatter_kernel(tensors, x_ref, out_ref, near, stage, far, send_near, recv_near, send_far, recv_far):
    me = lax.axis_index("tensor")
    chips = tensors // 2
    chip, core = me // 2, me % 2
    mate = chip * 2 + 1 - core
    features = out_ref.shape[0]

    barrier = pltpu.get_barrier_semaphore()
    chips_out = [lax.rem(chip + step, chips) for step in range(1, chips)]
    greeted = [mate] + [there * 2 + core for there in chips_out]
    for device in greeted:
        pl.semaphore_signal(barrier, inc=1, device_id={"tensor": device}, device_id_type=MESH)
    pl.semaphore_wait(barrier, len(greeted))

    def rows_of(device):
        return pl.ds(pl.multiple_of(device * features, 16), features)

    def near_copy(there):
        return pltpu.make_async_remote_copy(
            src_ref=x_ref.at[rows_of(there * 2 + 1 - core), :], dst_ref=near.at[there],
            send_sem=send_near.at[there], recv_sem=recv_near.at[there],
            device_id={"tensor": mate}, device_id_type=MESH,
        )

    def far_copy(source, there):
        return pltpu.make_async_remote_copy(
            src_ref=stage.at[there], dst_ref=far.at[source],
            send_sem=send_far.at[there], recv_sem=recv_far.at[source],
            device_id={"tensor": there * 2 + core}, device_id_type=MESH,
        )

    def pair_sum(there):
        near_copy(there).wait_recv()
        mine = x_ref[rows_of(there * 2 + core), :].astype(jnp.float32)
        return mine + near[there].astype(jnp.float32)

    for there in chips_out + [chip]:
        near_copy(there).start()
    for there in chips_out:
        stage[there] = pair_sum(there).astype(stage.dtype)
        far_copy(chip, there).start()
    total = pair_sum(chip)
    for there in chips_out:
        far_copy(there, there).wait_recv()
        total = total + far[there].astype(jnp.float32)
    out_ref[...] = total.astype(out_ref.dtype)
    for there in chips_out + [chip]:
        near_copy(there).wait_send()
    for there in chips_out:
        far_copy(chip, there).wait_send()


def scatter_rows(x, collective_id):
    tensors = lax.axis_size("tensor")
    chips = tensors // 2
    features = x.shape[0] // tensors
    vmem = pl.BlockSpec(memory_space=pltpu.VMEM)
    dma = pltpu.SemaphoreType.DMA
    held = pltpu.VMEM((chips, features, x.shape[1]), x.dtype)
    return pl.pallas_call(
        functools.partial(scatter_kernel, tensors),
        out_shape=jax.ShapeDtypeStruct((features, x.shape[1]), x.dtype),
        in_specs=[vmem],
        out_specs=vmem,
        scratch_shapes=[held, held, held] + [dma((chips,))] * 4,
        compiler_params=pltpu.CompilerParams(
            collective_id=collective_id, has_side_effects=True, vmem_limit_bytes=24 * 1024 * 1024
        ),
    )(x)


def exchange_kernel(tensors, x_ref, out_ref, held, send, recv):
    me = lax.axis_index("tensor")
    barrier = pltpu.get_barrier_semaphore()
    others = [lax.rem(me + step, tensors) for step in range(1, tensors)]
    for other in others:
        pl.semaphore_signal(barrier, inc=1, device_id={"tensor": other}, device_id_type=MESH)
    pl.semaphore_wait(barrier, tensors - 1)

    def copy(source, other):
        return pltpu.make_async_remote_copy(
            src_ref=x_ref, dst_ref=held.at[source], send_sem=send.at[other], recv_sem=recv.at[source],
            device_id={"tensor": other}, device_id_type=MESH,
        )

    for other in others:
        copy(me, other).start()
    held[me] = x_ref[...]
    for other in others:
        copy(other, other).wait_recv()
    out_ref[...] = jnp.sum(held[...], axis=0)
    for other in others:
        copy(me, other).wait_send()


def exchange(x, collective_id):
    tensors = lax.axis_size("tensor")
    vmem = pl.BlockSpec(memory_space=pltpu.VMEM)
    dma = pltpu.SemaphoreType.DMA
    return pl.pallas_call(
        functools.partial(exchange_kernel, tensors),
        out_shape=jax.ShapeDtypeStruct(x.shape, x.dtype),
        in_specs=[vmem],
        out_specs=vmem,
        scratch_shapes=[pltpu.VMEM((tensors,) + x.shape, x.dtype), dma((tensors,)), dma((tensors,))],
        compiler_params=pltpu.CompilerParams(
            collective_id=collective_id, has_side_effects=True, vmem_limit_bytes=24 * 1024 * 1024
        ),
    )(x)


def packed_sum(parts, collective_id):
    flat = jnp.concatenate([jnp.reshape(part, (-1,)) for part in parts])
    rows = -(-flat.shape[0] // 1024) * 8
    flat = jnp.pad(flat, (0, rows * 128 - flat.shape[0])).reshape(rows, 128)
    flat = exchange(flat, collective_id).reshape(-1)
    sums, start = [], 0
    for part in parts:
        sums.append(flat[start : start + part.size].reshape(part.shape))
        start += part.size
    return sums


def step_kernel(
    sections, tensors, count, pack, part_ref, loss_ref, x_ref, row_ref, col_ref, w_ref,
    out_ref, weight_ref, total_ref, row_out, col_out,
    held, carried, grad, acc_ref, row_acc, row_full, loss_buf, vectors, near, pair_sum, spread, final,
    send_x, recv_x, send_z, recv_z, send_mate, recv_mate, send_loss, recv_loss, local_sem, head_sem,
    send_sum, recv_sum, send_far, recv_far,
):
    section = lax.axis_index("section")
    me = lax.axis_index("tensor")
    chips = tensors // 2
    chip, core = me // 2, me % 2
    mate = chip * 2 + 1 - core
    last = sections - 1
    tokens, width = carried.shape
    features = acc_ref.shape[1]
    size = tokens // count
    per = count // sections
    depth = size // pack
    group = vectors.shape[2]
    used = width // group
    joined = 2 if (2 * features) % 128 == 0 else tensors
    span = joined * features

    def rem(a, b):
        return lax.rem(a, b)

    def share_of(step):
        return (last - step // per) * per + rem(step, per)

    def rows_of(step):
        return pl.ds(pl.multiple_of(share_of(step) * size, size), size)

    def packed_of(step):
        return pl.ds(pl.multiple_of(share_of(step) * depth, depth), depth)

    def remote(src, dst, send, recv, device):
        return pltpu.make_async_remote_copy(
            src_ref=src, dst_ref=dst, send_sem=send, recv_sem=recv, device_id=device, device_id_type=MESH
        )

    def block(device, step):
        return held.at[device, packed_of(step), :]

    def line_copy(step, origin, there):
        where = block(origin * 2 + core, step)
        slot = jnp.where(origin == chip, 0, chips) + there
        return remote(where, where, send_z.at[step, slot], recv_z.at[step, origin], {"tensor": there * 2 + core})

    def mate_copy(step, origin, side):
        where = block(origin * 2 + side, step)
        return remote(where, where, send_mate.at[step, origin], recv_mate.at[step, origin], {"tensor": mate})

    def down_copy(step):
        below = jnp.maximum(section - 1, 0)
        return remote(
            out_ref.at[packed_of(step), :], block(me, step), send_x.at[step], recv_x.at[step], {"section": below}
        )

    def head_copy(index):
        step = (last - section) * per + index
        return remote(
            part_ref.at[pl.ds(index * depth, depth), :], block(me, step),
            head_sem.at[index], recv_x.at[step], {"section": last},
        )

    def own_copy(index):
        return pltpu.make_async_copy(
            part_ref.at[pl.ds(index * depth, depth), :], block(me, index), local_sem.at[index]
        )

    def weight_copy():
        return pltpu.make_async_copy(w_ref, weight_ref, local_sem.at[per])

    def loss_copy(source, there):
        return remote(
            loss_ref, loss_buf.at[source], send_loss.at[there], recv_loss.at[source], {"section": there}
        )

    def origin_of(index):
        if index == 0:
            return chip
        near_side = jnp.where(chip * 2 < chips, -1, 1)
        both = jnp.minimum(chip, chips - 1 - chip)
        paired = index <= 2 * both
        distance = jnp.where(paired, (index + 1) // 2, index - both)
        toward_near = paired & (index % 2 == 0)
        return chip + jnp.where(toward_near, near_side, -near_side) * distance

    barrier = pltpu.get_barrier_semaphore()
    greeted = [{"tensor": mate}]
    greeted += [{"tensor": rem(chip + step, chips) * 2 + core} for step in range(1, chips)]
    greeted += [{"section": rem(section + step, sections)} for step in range(1, sections)]
    weight_copy().start()
    for device in greeted:
        pl.semaphore_signal(barrier, inc=1, device_id=device, device_id_type=MESH)
    pl.semaphore_wait(barrier, len(greeted))

    @pl.when(section == last)
    def _():
        for index in range(per):
            own_copy(index).start()

    @pl.when(section != last)
    def _():
        for index in range(per):
            head_copy(index).start()

    for step in range(1, sections):
        loss_copy(section, rem(section + step, sections)).start()

    is_end = (chip == 0) | (chip == chips - 1)

    def launch(step):
        @pl.when((section == last) & (step < per))
        def _():
            own_copy(jnp.minimum(step, per - 1)).wait()

        @pl.when((section != last) | (step >= per))
        def _():
            down_copy(step).wait_recv()

        @pl.when(is_end)
        def _():
            for index in range(1, chips):
                line_copy(step, chip, jnp.where(chip == 0, chips - index, index - 1)).start()

        if chips > 2:
            @pl.when(jnp.logical_not(is_end))
            def _():
                line_copy(step, chip, chip + 1).start()
                line_copy(step, chip, chip - 1).start()

        mate_copy(step, chip, core).start()

    def forwards(origin):
        onward = jnp.where(origin < chip, chip + 1, chip - 1)
        inner = (origin > 0) & (origin < chips - 1)
        return onward, inner & (onward >= 0) & (onward < chips)

    def assemble(step, first):
        for part in range(pack):
            pieces = []
            for offset in range(joined):
                piece = held[first + offset, packed_of(step), :]
                pieces.append(piece[:, part * features : (part + 1) * features])
            rows = pl.ds(pl.multiple_of(share_of(step) * size + part * depth, depth), depth)
            lanes = pl.ds(pl.multiple_of(first * features, 128), span)
            carried[rows, lanes] = jnp.concatenate(pieces, axis=1)

    def product(step, first, fresh):
        lanes = pl.ds(pl.multiple_of(first * features, 128), span)
        value = lax.dot_general(
            carried[rows_of(step), lanes], weight_ref[:, lanes], (((1,), (1,)), ((), ())),
            preferred_element_type=jnp.float32,
        )
        acc_ref[...] = value if fresh else acc_ref[...] + value

    def finish(step, index):
        origin = origin_of(index)
        mate_copy(step, origin, 1 - core).wait_recv()
        if joined == 2:
            assemble(step, origin * 2)
            product(step, origin * 2, index == 0)
        elif index == chips - 1:
            assemble(step, 0)
            product(step, 0, True)

    launch(0)
    weight_copy().wait()

    def add_squares():
        def rows_step(index, inner):
            entries = weight_ref[pl.ds(pl.multiple_of(index * 16, 16), 16), :].astype(jnp.float32)
            return inner + jnp.sum(jnp.reshape(entries * entries, (2, 8, width)), axis=0)

        sums = lax.fori_loop(0, features // 16, rows_step, jnp.zeros((8, width), jnp.float32))
        folded = sums[:, :128]
        for start in range(128, width, 128):
            folded = folded + sums[:, start : start + 128]
        vectors[1, pl.ds(used + 1, 1), :] = jnp.broadcast_to(jnp.sum(folded, keepdims=True), (1, group))

    vectors[...] = jnp.zeros_like(vectors)

    @pl.when(section != last)
    def _():
        add_squares()

    half = count // 2
    low = tokens // 2
    cut = width // half

    def advance(step, carry):
        for index in range(1, chips):
            if index == chips - 1:
                @pl.when(step + 1 < count)
                def _():
                    launch(jnp.minimum(step + 1, count - 1))

            origin = origin_of(index)
            line_copy(step, origin, chip).wait_recv()
            onward, wanted = forwards(origin)

            @pl.when(wanted)
            def _():
                line_copy(step, origin, jnp.clip(onward, 0, chips - 1)).start()

            mate_copy(step, origin, core).start()
            finish(step, index - 1)
        finish(step, chips - 1)
        sums = jnp.concatenate([acc_ref[part * depth : (part + 1) * depth, :] for part in range(pack)], axis=1)
        mine = held[me, packed_of(step), :].astype(jnp.float32)
        out_ref[packed_of(step), :] = (mine + sums).astype(out_ref.dtype)

        @pl.when(section > 0)
        def _():
            down_copy(step).start()

        @pl.when(step >= half)
        def _():
            lanes = pl.ds(pl.multiple_of((step - half) * cut, 128), cut)
            grad[:, lanes] = jnp.dot(
                x_ref[:, low:], carried[low:, lanes], preferred_element_type=jnp.float32
            )

        return carry

    lax.fori_loop(0, count, advance, 0)

    @pl.when(section == last)
    def _():
        add_squares()

    row_acc[...] = jnp.zeros_like(row_acc)

    def gather_squares(index, carry):
        lanes = pl.ds(pl.multiple_of(index * group, 128), group)
        value = grad[:, lanes] + jnp.dot(
            x_ref[:, :low], carried[:low, lanes], preferred_element_type=jnp.float32
        )
        grad[:, lanes] = value
        squares = value * value + tiny_term
        folded = squares[:, :128]
        for start in range(128, group, 128):
            folded = folded + squares[:, start : start + 128]
        row_acc[...] = row_acc[...] + folded
        vectors[0, pl.ds(index, 1), :] = jnp.sum(squares, axis=0, keepdims=True)
        return carry

    lax.fori_loop(0, used, gather_squares, 0)
    sums = jnp.sum(row_acc[...], axis=1, keepdims=True)
    fresh_row = decay_rate * row_ref[...] + (1.0 - decay_rate) * (sums / width)
    row_out[...] = fresh_row
    vectors[1, pl.ds(used, 1), :] = jnp.broadcast_to(jnp.sum(fresh_row, keepdims=True), (1, group))
    row_full[...] = jnp.broadcast_to(1.0 / fresh_row, row_full.shape)

    def gather_scaled(index, carry):
        scaled = []
        for start in range(0, group, 128):
            value = grad[:, pl.ds(pl.multiple_of(index * group + start, 128), 128)]
            scaled.append(jnp.sum(value * value * row_full[...], axis=0, keepdims=True))
        vectors[1, pl.ds(index, 1), :] = jnp.concatenate(scaled, axis=1)
        return carry

    lax.fori_loop(0, used, gather_scaled, 0)

    def mate_sum():
        return remote(vectors.at[1 - core], near, send_sum.at[0], recv_sum.at[0], {"tensor": mate})

    def far_sum(source, there):
        return remote(
            pair_sum, spread.at[source], send_far.at[there], recv_far.at[source], {"tensor": there * 2 + core}
        )

    def mate_total(side):
        return remote(final.at[side], final.at[side], send_sum.at[1], recv_sum.at[1], {"tensor": mate})

    others = [rem(chip + step, chips) for step in range(1, chips)]
    mate_sum().start()
    mate_sum().wait_recv()
    pair_sum[...] = vectors[core] + near[...]
    for there in others:
        far_sum(chip, there).start()
    spread[chip] = pair_sum[...]
    for there in others:
        far_sum(there, there).wait_recv()
    final[core] = jnp.sum(spread[...], axis=0)
    mate_total(core).start()

    total = None
    for step in range(1, sections):
        other = rem(section + step, sections)
        loss_copy(other, other).wait_recv()
    loss_buf[section] = loss_ref[...]
    total_ref[...] = jnp.sum(loss_buf[...], axis=0)

    mate_total(1 - core).wait_recv()

    entries = float(width * width)
    row_total = final[1, used : used + 1, :][:, :1]
    weight_total = final[1, used + 1 : used + 2, :][:, :1]

    def update_columns(index, inner):
        lanes = pl.ds(pl.multiple_of(index * group, 128), group)
        fresh = decay_rate * col_ref[:, lanes] + (1.0 - decay_rate) * (final[0, pl.ds(index, 1), :] / width)
        col_out[:, lanes] = fresh
        return inner + final[1, pl.ds(index, 1), :] / fresh

    scaled = lax.fori_loop(0, used, update_columns, jnp.zeros((1, group), jnp.float32))
    update_total = row_total * jnp.sum(scaled, axis=1, keepdims=True)
    factor = (
        learn_rate * jnp.sqrt(weight_total / entries)
        / jnp.maximum(1.0, jnp.sqrt(update_total / entries))
    )
    row_full[...] = jnp.broadcast_to(
        lax.rsqrt(row_out[...]) * (factor * jnp.sqrt(row_total)), row_full.shape
    )

    def write_weights(index, carry):
        for start in range(0, group, 128):
            lanes = pl.ds(pl.multiple_of(index * group + start, 128), 128)
            change = grad[:, lanes] * (row_full[...] * lax.rsqrt(col_out[:, lanes]))
            weight_ref[:, lanes] = (weight_ref[:, lanes].astype(jnp.float32) - change).astype(weight_ref.dtype)
        return carry

    lax.fori_loop(0, used, write_weights, 0)

    def drain(step, carry):
        @pl.when(section > 0)
        def _():
            down_copy(step).wait_send()

        @pl.when(is_end)
        def _():
            for index in range(1, chips):
                line_copy(step, chip, jnp.where(chip == 0, chips - index, index - 1)).wait_send()

        if chips > 2:
            @pl.when(jnp.logical_not(is_end))
            def _():
                line_copy(step, chip, chip + 1).wait_send()
                line_copy(step, chip, chip - 1).wait_send()

        mate_copy(step, chip, core).wait_send()
        for index in range(1, chips):
            origin = origin_of(index)
            onward, wanted = forwards(origin)

            @pl.when(wanted)
            def _():
                line_copy(step, origin, jnp.clip(onward, 0, chips - 1)).wait_send()

            mate_copy(step, origin, core).wait_send()
        return carry

    lax.fori_loop(0, count, drain, 0)
    for step in range(1, sections):
        loss_copy(section, rem(section + step, sections)).wait_send()

    @pl.when(section != last)
    def _():
        for index in range(per):
            head_copy(index).wait_send()

    mate_sum().wait_send()
    for there in others:
        far_sum(chip, there).wait_send()
    mate_total(core).wait_send()


def step(part, part_loss, saved, local_weight, row_state, col_state):
    sections, tensors = lax.axis_size("section"), lax.axis_size("tensor")
    features, tokens = saved.shape
    width = features * tensors
    chips = tensors // 2
    count = 2 * sections
    size = tokens // count
    pack = 2 if (2 * features) % 128 == 0 and (size // 2) % 16 == 0 else 1
    group = 512 if width % 512 == 0 else 128
    lines = -(-(width // group + 2) // 8) * 8
    part = part.reshape(count // sections, pack, size // pack, features)
    part = jnp.transpose(part, (0, 2, 1, 3)).reshape(tokens // sections // pack, pack * features)
    dma = pltpu.SemaphoreType.DMA
    vmem = pl.BlockSpec(memory_space=pltpu.VMEM)
    single = pltpu.VMEM((lines, group), jnp.float32)
    outputs, weight, total, row_new, col_new = pl.pallas_call(
        functools.partial(step_kernel, sections, tensors, count, pack),
        out_shape=(
            jax.ShapeDtypeStruct((tokens // pack, pack * features), jnp.bfloat16),
            jax.ShapeDtypeStruct((features, width), jnp.bfloat16),
            jax.ShapeDtypeStruct((8, 128), jnp.float32),
            jax.ShapeDtypeStruct((features, 1), jnp.float32),
            jax.ShapeDtypeStruct((1, width), jnp.float32),
        ),
        in_specs=[vmem] * 5 + [pl.BlockSpec(memory_space=pl.ANY)],
        out_specs=(vmem,) * 5,
        scratch_shapes=[
            pltpu.VMEM((tensors, tokens // pack, pack * features), jnp.bfloat16),
            pltpu.VMEM((tokens, width), jnp.bfloat16),
            pltpu.VMEM((features, width), jnp.float32),
            pltpu.VMEM((size, features), jnp.float32),
            pltpu.VMEM((features, 128), jnp.float32),
            pltpu.VMEM((features, 128), jnp.float32),
            pltpu.VMEM((sections, 8, 128), jnp.float32),
            pltpu.VMEM((2, lines, group), jnp.float32),
            single,
            single,
            pltpu.VMEM((chips, lines, group), jnp.float32),
            pltpu.VMEM((2, lines, group), jnp.float32),
            dma((count,)),
            dma((count,)),
            dma((count, 2 * chips)),
            dma((count, chips)),
            dma((count, chips)),
            dma((count, chips)),
            dma((sections,)),
            dma((sections,)),
            dma((count // sections + 1,)),
            dma((count // sections,)),
            dma((2,)),
            dma((2,)),
            dma((chips,)),
            dma((chips,)),
        ],
        compiler_params=pltpu.CompilerParams(
            collective_id=0, has_side_effects=True, vmem_limit_bytes=62 * 1024 * 1024
        ),
    )(part, jnp.full((8, 128), part_loss, jnp.float32), saved, row_state, col_state, local_weight)
    outputs = outputs.reshape(count, size // pack, pack, features)
    outputs = jnp.transpose(outputs, (0, 2, 1, 3)).reshape(tokens, features)
    return outputs, weight, total, row_new, col_new


def body(hidden_last, labels, head_weight, layer_inputs, weights, row_state, col_state):
    section_count = lax.axis_size("section")
    section_index = lax.axis_index("section")
    all_rows = labels.shape[0]
    vocab_local = head_weight.shape[1]
    local_weight = weights[0]
    saved_all = layer_inputs[0]
    columns = lax.axis_index("tensor") * vocab_local + lax.iota(jnp.int32, vocab_local)
    share_rows = all_rows // section_count
    row_start = section_index * share_rows
    hidden_rows = lax.dynamic_slice_in_dim(hidden_last, row_start, share_rows, 0)
    head_slice = head_weight
    logits = lax.dot_general(
        gather_rows(hidden_rows.T, 3),
        head_slice,
        (((0,), (0,)), ((), ())),
        preferred_element_type=jnp.float32,
    )
    exponent = jnp.exp(logits)
    label_hit = (
        lax.dynamic_slice_in_dim(labels, row_start, share_rows, 0)[:, None] == columns[None, :]
    )
    denominator, picked = packed_sum(
        (
            jnp.sum(exponent, axis=1),
            jnp.sum(jnp.where(label_hit, logits, jnp.zeros_like(logits)), axis=1),
        ),
        1,
    )
    losses = jnp.log(denominator) - picked
    logit_grad = (
        (exponent / denominator[:, None] - label_hit.astype(jnp.float32)) / all_rows
    ).astype(jnp.bfloat16)
    head_slice = head_weight
    part_grad = scatter_rows(
        lax.dot_general(
            head_slice, logit_grad, (((1,), (1,)), ((), ())), preferred_element_type=jnp.float32
        ).astype(jnp.bfloat16),
        4,
    )
    part_loss = jnp.sum(losses)
    outputs, new_weight, total, row_new, col_new = step(
        part_grad.T, part_loss, saved_all.T, local_weight, row_state.reshape(-1, 1), col_state
    )
    loss = total[0, 0] / all_rows
    return (loss, outputs[None], new_weight[None], row_new.reshape(1, -1), col_new)


def solution(mesh):
    return jax.shard_map(
        body,
        mesh=mesh,
        in_specs=(
            P(None, "tensor"),
            P(),
            P(None, "tensor"),
            P("section", None, "tensor"),
            P("section", "tensor", None),
            P("section", "tensor"),
            P("section", None),
        ),
        out_specs=(
            P(),
            P("section", None, "tensor"),
            P("section", "tensor", None),
            P("section", "tensor"),
            P("section", None),
        ),
        check_vma=False,
    )
```

```python
import functools

import jax
import jax.numpy as jnp
from jax import lax
from jax.experimental import pallas as pl
from jax.experimental.pallas import tpu as pltpu
from jax.sharding import PartitionSpec as P

decay_rate = 0.9
learn_rate = 0.3
tiny_term = 1e-30


MESH = pl.DeviceIdType.MESH


def gather_kernel(tensors, x_ref, g_ref, send_ring, recv_ring, send_mate, recv_mate, own_sem):
    me = lax.axis_index("tensor")
    chips = tensors // 2
    chip, core = me // 2, me % 2
    right = lax.rem(chip + 1, chips) * 2 + core
    left = lax.rem(chip + chips - 1, chips) * 2 + core
    mate = chip * 2 + 1 - core
    features = x_ref.shape[0]
    half = features // 2 // 16 * 16
    reach = chips // 2

    barrier = pltpu.get_barrier_semaphore()
    greeted = [mate] + ([right, left] if reach else [])
    for device in greeted:
        pl.semaphore_signal(barrier, inc=1, device_id={"tensor": device}, device_id_type=MESH)
    pl.semaphore_wait(barrier, len(greeted))

    def copy(way, distance, origin, to_mate):
        low, size = 0, features
        if distance and 2 * distance == chips:
            low, size = (0, half) if way == 0 else (half, features - half)
        where = g_ref.at[pl.ds(pl.multiple_of(origin * features + low, 16), size), :]
        own = (distance == 0) if to_mate else (distance == 1)
        slot = 0 if distance == 0 else way * reach + distance - 1 + int(to_mate)
        send, recv = (send_mate, recv_mate) if to_mate else (send_ring, recv_ring)
        target = mate if to_mate else (right if way == 0 else left)
        return pltpu.make_async_remote_copy(
            src_ref=x_ref.at[pl.ds(low, size), :] if own else where, dst_ref=where,
            send_sem=send.at[slot], recv_sem=recv.at[slot],
            device_id={"tensor": target}, device_id_type=MESH,
        )

    def origin_of(way, distance):
        there = chip - distance if way == 0 else chip + distance
        return lax.rem(there + chips, chips) * 2 + core

    sent = []

    def start(*args):
        copy(*args).start()
        sent.append(args)

    own_block = g_ref.at[pl.ds(pl.multiple_of(me * features, 16), features), :]
    keep = pltpu.make_async_copy(x_ref, own_block, own_sem.at[0])
    if reach:
        start(0, 1, me, False)
        start(1, 1, me, False)
    start(0, 0, me, True)
    keep.start()
    for distance in range(1, reach + 1):
        for way in (0, 1):
            origin = origin_of(way, distance)
            copy(way, distance, origin, False).wait_recv()
            if distance < reach:
                start(way, distance + 1, origin, False)
            start(way, distance, origin, True)
    other = 1 - 2 * core
    copy(0, 0, me + other, True).wait_recv()
    for distance in range(1, reach + 1):
        for way in (0, 1):
            copy(way, distance, origin_of(way, distance) + other, True).wait_recv()
    keep.wait()
    for args in sent:
        copy(*args).wait_send()


def gather_rows(x, collective_id):
    tensors = lax.axis_size("tensor")
    ring = max(2 * (tensors // 4), 1)
    vmem = pl.BlockSpec(memory_space=pltpu.VMEM)
    dma = pltpu.SemaphoreType.DMA
    return pl.pallas_call(
        functools.partial(gather_kernel, tensors),
        out_shape=jax.ShapeDtypeStruct((tensors * x.shape[0], x.shape[1]), x.dtype),
        in_specs=[vmem],
        out_specs=vmem,
        scratch_shapes=[dma((ring,)), dma((ring,)), dma((ring + 1,)), dma((ring + 1,)), dma((1,))],
        compiler_params=pltpu.CompilerParams(
            collective_id=collective_id, has_side_effects=True, vmem_limit_bytes=24 * 1024 * 1024
        ),
    )(x)


def scatter_kernel(tensors, x_ref, out_ref, near, stage, far, send_near, recv_near, send_far, recv_far):
    me = lax.axis_index("tensor")
    chips = tensors // 2
    chip, core = me // 2, me % 2
    mate = chip * 2 + 1 - core
    features = out_ref.shape[0]

    barrier = pltpu.get_barrier_semaphore()
    chips_out = [lax.rem(chip + step, chips) for step in range(1, chips)]
    greeted = [mate] + [there * 2 + core for there in chips_out]
    for device in greeted:
        pl.semaphore_signal(barrier, inc=1, device_id={"tensor": device}, device_id_type=MESH)
    pl.semaphore_wait(barrier, len(greeted))

    def rows_of(device):
        return pl.ds(pl.multiple_of(device * features, 16), features)

    def near_copy(there):
        return pltpu.make_async_remote_copy(
            src_ref=x_ref.at[rows_of(there * 2 + 1 - core), :], dst_ref=near.at[there],
            send_sem=send_near.at[there], recv_sem=recv_near.at[there],
            device_id={"tensor": mate}, device_id_type=MESH,
        )

    def far_copy(source, there):
        return pltpu.make_async_remote_copy(
            src_ref=stage.at[there], dst_ref=far.at[source],
            send_sem=send_far.at[there], recv_sem=recv_far.at[source],
            device_id={"tensor": there * 2 + core}, device_id_type=MESH,
        )

    def pair_sum(there):
        near_copy(there).wait_recv()
        mine = x_ref[rows_of(there * 2 + core), :].astype(jnp.float32)
        return mine + near[there].astype(jnp.float32)

    for there in chips_out + [chip]:
        near_copy(there).start()
    for there in chips_out:
        stage[there] = pair_sum(there).astype(stage.dtype)
        far_copy(chip, there).start()
    total = pair_sum(chip)
    for there in chips_out:
        far_copy(there, there).wait_recv()
        total = total + far[there].astype(jnp.float32)
    out_ref[...] = total.astype(out_ref.dtype)
    for there in chips_out + [chip]:
        near_copy(there).wait_send()
    for there in chips_out:
        far_copy(chip, there).wait_send()


def scatter_rows(x, collective_id):
    tensors = lax.axis_size("tensor")
    chips = tensors // 2
    features = x.shape[0] // tensors
    vmem = pl.BlockSpec(memory_space=pltpu.VMEM)
    dma = pltpu.SemaphoreType.DMA
    held = pltpu.VMEM((chips, features, x.shape[1]), x.dtype)
    return pl.pallas_call(
        functools.partial(scatter_kernel, tensors),
        out_shape=jax.ShapeDtypeStruct((features, x.shape[1]), x.dtype),
        in_specs=[vmem],
        out_specs=vmem,
        scratch_shapes=[held, held, held] + [dma((chips,))] * 4,
        compiler_params=pltpu.CompilerParams(
            collective_id=collective_id, has_side_effects=True, vmem_limit_bytes=24 * 1024 * 1024
        ),
    )(x)


def exchange_kernel(tensors, x_ref, out_ref, held, send, recv):
    me = lax.axis_index("tensor")
    barrier = pltpu.get_barrier_semaphore()
    others = [lax.rem(me + step, tensors) for step in range(1, tensors)]
    for other in others:
        pl.semaphore_signal(barrier, inc=1, device_id={"tensor": other}, device_id_type=MESH)
    pl.semaphore_wait(barrier, tensors - 1)

    def copy(source, other):
        return pltpu.make_async_remote_copy(
            src_ref=x_ref, dst_ref=held.at[source], send_sem=send.at[other], recv_sem=recv.at[source],
            device_id={"tensor": other}, device_id_type=MESH,
        )

    for other in others:
        copy(me, other).start()
    held[me] = x_ref[...]
    for other in others:
        copy(other, other).wait_recv()
    out_ref[...] = jnp.sum(held[...], axis=0)
    for other in others:
        copy(me, other).wait_send()


def exchange(x, collective_id):
    tensors = lax.axis_size("tensor")
    vmem = pl.BlockSpec(memory_space=pltpu.VMEM)
    dma = pltpu.SemaphoreType.DMA
    return pl.pallas_call(
        functools.partial(exchange_kernel, tensors),
        out_shape=jax.ShapeDtypeStruct(x.shape, x.dtype),
        in_specs=[vmem],
        out_specs=vmem,
        scratch_shapes=[pltpu.VMEM((tensors,) + x.shape, x.dtype), dma((tensors,)), dma((tensors,))],
        compiler_params=pltpu.CompilerParams(
            collective_id=collective_id, has_side_effects=True, vmem_limit_bytes=24 * 1024 * 1024
        ),
    )(x)


def packed_sum(parts, collective_id):
    flat = jnp.concatenate([jnp.reshape(part, (-1,)) for part in parts])
    rows = -(-flat.shape[0] // 1024) * 8
    flat = jnp.pad(flat, (0, rows * 128 - flat.shape[0])).reshape(rows, 128)
    flat = exchange(flat, collective_id).reshape(-1)
    sums, start = [], 0
    for part in parts:
        sums.append(flat[start : start + part.size].reshape(part.shape))
        start += part.size
    return sums


def step_kernel(
    sections, tensors, count, pack, part_ref, loss_ref, x_ref, row_ref, col_ref, w_ref,
    out_ref, grad_out, total_ref, row_out, row_scale, col_out, col_scale,
    weight_ref, stage, held, carried, grad, acc_ref, row_acc, row_full, loss_buf, vectors, near, pair_sum, spread, final,
    send_x, recv_x, send_z, recv_z, send_mate, recv_mate, send_loss, recv_loss, local_sem, head_sem,
    send_sum, recv_sum, send_far, recv_far, stage_sem,
):
    section = lax.axis_index("section")
    me = lax.axis_index("tensor")
    chips = tensors // 2
    chip, core = me // 2, me % 2
    mate = chip * 2 + 1 - core
    last = sections - 1
    tokens, width = carried.shape
    features = acc_ref.shape[1]
    size = tokens // count
    per = count // sections
    depth = size // pack
    group = vectors.shape[2]
    used = width // group
    joined = 2 if (2 * features) % 128 == 0 else tensors
    span = joined * features

    def rem(a, b):
        return lax.rem(a, b)

    def share_of(step):
        return (last - step // per) * per + rem(step, per)

    def rows_of(step):
        return pl.ds(pl.multiple_of(share_of(step) * size, size), size)

    def packed_of(step):
        return pl.ds(pl.multiple_of(share_of(step) * depth, depth), depth)

    def remote(src, dst, send, recv, device):
        return pltpu.make_async_remote_copy(
            src_ref=src, dst_ref=dst, send_sem=send, recv_sem=recv, device_id=device, device_id_type=MESH
        )

    def block(device, step):
        return held.at[device, packed_of(step), :]

    def line_copy(step, origin, there):
        where = block(origin * 2 + core, step)
        slot = jnp.where(origin == chip, 0, chips) + there
        return remote(where, where, send_z.at[step, slot], recv_z.at[step, origin], {"tensor": there * 2 + core})

    def mate_copy(step, origin, side):
        where = block(origin * 2 + side, step)
        return remote(where, where, send_mate.at[step, origin], recv_mate.at[step, origin], {"tensor": mate})

    def down_copy(step):
        below = jnp.maximum(section - 1, 0)
        return remote(
            out_ref.at[packed_of(step), :], block(me, step), send_x.at[step], recv_x.at[step], {"section": below}
        )

    def head_copy(index):
        step = (last - section) * per + index
        return remote(
            part_ref.at[pl.ds(index * depth, depth), :], block(me, step),
            head_sem.at[index], recv_x.at[step], {"section": last},
        )

    def own_copy(index):
        return pltpu.make_async_copy(
            part_ref.at[pl.ds(index * depth, depth), :], block(me, index), local_sem.at[index]
        )

    def weight_copy():
        return pltpu.make_async_copy(w_ref, weight_ref, local_sem.at[per])

    def loss_copy(source, there):
        return remote(
            loss_ref, loss_buf.at[source], send_loss.at[there], recv_loss.at[source], {"section": there}
        )

    def origin_of(index):
        if index == 0:
            return chip
        near_side = jnp.where(chip * 2 < chips, -1, 1)
        both = jnp.minimum(chip, chips - 1 - chip)
        paired = index <= 2 * both
        distance = jnp.where(paired, (index + 1) // 2, index - both)
        toward_near = paired & (index % 2 == 0)
        return chip + jnp.where(toward_near, near_side, -near_side) * distance

    barrier = pltpu.get_barrier_semaphore()
    greeted = [{"tensor": mate}]
    greeted += [{"tensor": rem(chip + step, chips) * 2 + core} for step in range(1, chips)]
    greeted += [{"section": rem(section + step, sections)} for step in range(1, sections)]
    weight_copy().start()
    for device in greeted:
        pl.semaphore_signal(barrier, inc=1, device_id=device, device_id_type=MESH)
    pl.semaphore_wait(barrier, len(greeted))

    @pl.when(section == last)
    def _():
        for index in range(per):
            own_copy(index).start()

    @pl.when(section != last)
    def _():
        for index in range(per):
            head_copy(index).start()

    for step in range(1, sections):
        loss_copy(section, rem(section + step, sections)).start()

    is_end = (chip == 0) | (chip == chips - 1)

    def launch(step):
        @pl.when((section == last) & (step < per))
        def _():
            own_copy(jnp.minimum(step, per - 1)).wait()

        @pl.when((section != last) | (step >= per))
        def _():
            down_copy(step).wait_recv()

        @pl.when(is_end)
        def _():
            for index in range(1, chips):
                line_copy(step, chip, jnp.where(chip == 0, chips - index, index - 1)).start()

        if chips > 2:
            @pl.when(jnp.logical_not(is_end))
            def _():
                line_copy(step, chip, chip + 1).start()
                line_copy(step, chip, chip - 1).start()

        mate_copy(step, chip, core).start()

    def forwards(origin):
        onward = jnp.where(origin < chip, chip + 1, chip - 1)
        inner = (origin > 0) & (origin < chips - 1)
        return onward, inner & (onward >= 0) & (onward < chips)

    def assemble(step, first):
        for part in range(pack):
            pieces = []
            for offset in range(joined):
                piece = held[first + offset, packed_of(step), :]
                pieces.append(piece[:, part * features : (part + 1) * features])
            rows = pl.ds(pl.multiple_of(share_of(step) * size + part * depth, depth), depth)
            lanes = pl.ds(pl.multiple_of(first * features, 128), span)
            carried[rows, lanes] = jnp.concatenate(pieces, axis=1)

    def product(step, first, fresh):
        lanes = pl.ds(pl.multiple_of(first * features, 128), span)
        value = lax.dot_general(
            carried[rows_of(step), lanes], weight_ref[:, lanes], (((1,), (1,)), ((), ())),
            preferred_element_type=jnp.float32,
        )
        acc_ref[...] = value if fresh else acc_ref[...] + value

    def finish(step, index):
        origin = origin_of(index)
        mate_copy(step, origin, 1 - core).wait_recv()
        if joined == 2:
            assemble(step, origin * 2)
            product(step, origin * 2, index == 0)
        elif index == chips - 1:
            assemble(step, 0)
            product(step, 0, True)

    launch(0)
    weight_copy().wait()

    def add_squares():
        def rows_step(index, inner):
            entries = weight_ref[pl.ds(pl.multiple_of(index * 16, 16), 16), :].astype(jnp.float32)
            return inner + jnp.sum(jnp.reshape(entries * entries, (2, 8, width)), axis=0)

        sums = lax.fori_loop(0, features // 16, rows_step, jnp.zeros((8, width), jnp.float32))
        folded = sums[:, :128]
        for start in range(128, width, 128):
            folded = folded + sums[:, start : start + 128]
        vectors[1, pl.ds(used + 1, 1), :] = jnp.broadcast_to(jnp.sum(folded, keepdims=True), (1, group))

    vectors[...] = jnp.zeros_like(vectors)

    @pl.when(section != last)
    def _():
        add_squares()

    half = count // 2
    low = tokens // 2
    cut = width // half

    def advance(step, carry):
        for index in range(1, chips):
            if index == min(2, chips - 1):
                @pl.when(step + 1 < count)
                def _():
                    launch(jnp.minimum(step + 1, count - 1))

            origin = origin_of(index)
            line_copy(step, origin, chip).wait_recv()
            onward, wanted = forwards(origin)

            @pl.when(wanted)
            def _():
                line_copy(step, origin, jnp.clip(onward, 0, chips - 1)).start()

            mate_copy(step, origin, core).start()
            finish(step, index - 1)
        finish(step, chips - 1)
        sums = jnp.concatenate([acc_ref[part * depth : (part + 1) * depth, :] for part in range(pack)], axis=1)
        mine = held[me, packed_of(step), :].astype(jnp.float32)
        out_ref[packed_of(step), :] = (mine + sums).astype(out_ref.dtype)

        @pl.when(section > 0)
        def _():
            down_copy(step).start()

        @pl.when(step >= half)
        def _():
            lanes = pl.ds(pl.multiple_of((step - half) * cut, 128), cut)
            grad[:, lanes] = jnp.dot(
                x_ref[:, low:], carried[low:, lanes], preferred_element_type=jnp.float32
            )

        return carry

    lax.fori_loop(0, count, advance, 0)

    @pl.when(section == last)
    def _():
        add_squares()

    row_acc[...] = jnp.zeros_like(row_acc)

    def stage_copy(index):
        lanes = pl.ds(pl.multiple_of(index * group, 128), group)
        slot = rem(index, 2)
        return pltpu.make_async_copy(stage.at[slot], grad_out.at[:, lanes], stage_sem.at[slot])

    def gather_squares(index, carry):
        lanes = pl.ds(pl.multiple_of(index * group, 128), group)
        value = grad[:, lanes] + jnp.dot(
            x_ref[:, :low], carried[:low, lanes], preferred_element_type=jnp.float32
        )
        grad[:, lanes] = value

        @pl.when(index > 1)
        def _():
            stage_copy(index - 2).wait()

        slot = rem(index, 2)
        inner = jnp.zeros((8, group), jnp.float32)
        for start in range(0, features, 16):
            entries = grad[start : start + 16, lanes]
            stage[slot, start : start + 16, :] = entries.astype(stage.dtype)
            squares = entries * entries + tiny_term
            folded = squares[:, :128]
            for lane in range(128, group, 128):
                folded = folded + squares[:, lane : lane + 128]
            row_acc[start : start + 16, :] = row_acc[start : start + 16, :] + folded
            inner = inner + jnp.sum(jnp.reshape(squares, (2, 8, group)), axis=0)
        vectors[0, pl.ds(index, 1), :] = jnp.sum(inner, axis=0, keepdims=True)
        stage_copy(index).start()
        return carry

    lax.fori_loop(0, used, gather_squares, 0)
    sums = jnp.sum(row_acc[...], axis=1, keepdims=True)
    fresh_row = decay_rate * row_ref[...] + (1.0 - decay_rate) * (sums / width)
    row_out[...] = fresh_row
    vectors[1, pl.ds(used, 1), :] = jnp.broadcast_to(jnp.sum(fresh_row, keepdims=True), (1, group))
    row_full[...] = jnp.broadcast_to(1.0 / fresh_row, row_full.shape)

    def gather_scaled(index, carry):
        lanes = pl.ds(pl.multiple_of(index * group, 128), group)
        inner = jnp.zeros((8, group), jnp.float32)
        for start in range(0, features, 16):
            entries = grad[start : start + 16, lanes]
            shrink = jnp.concatenate([row_full[start : start + 16, :]] * (group // 128), axis=1)
            inner = inner + jnp.sum(jnp.reshape(entries * entries * shrink, (2, 8, group)), axis=0)
        vectors[1, pl.ds(index, 1), :] = jnp.sum(inner, axis=0, keepdims=True)
        return carry

    lax.fori_loop(0, used, gather_scaled, 0)

    def mate_sum():
        return remote(vectors.at[1 - core], near, send_sum.at[0], recv_sum.at[0], {"tensor": mate})

    def far_sum(source, there):
        return remote(
            pair_sum, spread.at[source], send_far.at[there], recv_far.at[source], {"tensor": there * 2 + core}
        )

    def mate_total(side):
        return remote(final.at[side], final.at[side], send_sum.at[1], recv_sum.at[1], {"tensor": mate})

    others = [rem(chip + step, chips) for step in range(1, chips)]
    mate_sum().start()
    mate_sum().wait_recv()
    pair_sum[...] = vectors[core] + near[...]
    for there in others:
        far_sum(chip, there).start()
    spread[chip] = pair_sum[...]
    for there in others:
        far_sum(there, there).wait_recv()
    final[core] = jnp.sum(spread[...], axis=0)
    mate_total(core).start()

    total = None
    for step in range(1, sections):
        other = rem(section + step, sections)
        loss_copy(other, other).wait_recv()
    loss_buf[section] = loss_ref[...]
    total_ref[...] = jnp.sum(loss_buf[...], axis=0)

    mate_total(1 - core).wait_recv()

    entries = float(width * width)
    row_total = final[1, used : used + 1, :][:, :1]
    weight_total = final[1, used + 1 : used + 2, :][:, :1]

    def update_columns(index, inner):
        lanes = pl.ds(pl.multiple_of(index * group, 128), group)
        fresh = decay_rate * col_ref[:, lanes] + (1.0 - decay_rate) * (final[0, pl.ds(index, 1), :] / width)
        col_out[:, lanes] = fresh
        col_scale[:, lanes] = lax.rsqrt(fresh)
        return inner + final[1, pl.ds(index, 1), :] / fresh

    scaled = lax.fori_loop(0, used, update_columns, jnp.zeros((1, group), jnp.float32))
    update_total = row_total * jnp.sum(scaled, axis=1, keepdims=True)
    factor = (
        learn_rate * jnp.sqrt(weight_total / entries)
        / jnp.maximum(1.0, jnp.sqrt(update_total / entries))
    )
    row_scale[...] = lax.rsqrt(row_out[...]) * (factor * jnp.sqrt(row_total))
    for index in (used - 2, used - 1):
        stage_copy(index).wait()

    def drain(step, carry):
        @pl.when(section > 0)
        def _():
            down_copy(step).wait_send()

        @pl.when(is_end)
        def _():
            for index in range(1, chips):
                line_copy(step, chip, jnp.where(chip == 0, chips - index, index - 1)).wait_send()

        if chips > 2:
            @pl.when(jnp.logical_not(is_end))
            def _():
                line_copy(step, chip, chip + 1).wait_send()
                line_copy(step, chip, chip - 1).wait_send()

        mate_copy(step, chip, core).wait_send()
        for index in range(1, chips):
            origin = origin_of(index)
            onward, wanted = forwards(origin)

            @pl.when(wanted)
            def _():
                line_copy(step, origin, jnp.clip(onward, 0, chips - 1)).wait_send()

            mate_copy(step, origin, core).wait_send()
        return carry

    lax.fori_loop(0, count, drain, 0)
    for step in range(1, sections):
        loss_copy(section, rem(section + step, sections)).wait_send()

    @pl.when(section != last)
    def _():
        for index in range(per):
            head_copy(index).wait_send()

    mate_sum().wait_send()
    for there in others:
        far_sum(chip, there).wait_send()
    mate_total(core).wait_send()


def update_kernel(weight_ref, grad_ref, row_ref, col_ref, out_ref):
    rows, width = out_ref.shape
    group = 512 if width % 512 == 0 else 128
    for start in range(0, rows, 16):
        scale = jnp.broadcast_to(row_ref[start : start + 16, :], (16, group))
        for lane in range(0, width, group):
            change = grad_ref[start : start + 16, lane : lane + group].astype(jnp.float32)
            change = change * (scale * col_ref[:, lane : lane + group])
            entries = weight_ref[start : start + 16, lane : lane + group].astype(jnp.float32)
            out_ref[start : start + 16, lane : lane + group] = (entries - change).astype(out_ref.dtype)


def update(weight, grad, row_scale, col_scale):
    features, width = weight.shape
    rows = max(size for size in range(16, 65, 16) if features % size == 0)
    tile = pl.BlockSpec((rows, width), lambda index: (index, 0))
    return pl.pallas_call(
        update_kernel,
        grid=(features // rows,),
        out_shape=jax.ShapeDtypeStruct((features, width), jnp.bfloat16),
        in_specs=[
            tile, tile,
            pl.BlockSpec((rows, 1), lambda index: (index, 0)),
            pl.BlockSpec((1, width), lambda index: (0, 0)),
        ],
        out_specs=tile,
        compiler_params=pltpu.CompilerParams(vmem_limit_bytes=16 * 1024 * 1024),
    )(weight, grad, row_scale, col_scale)


def step(part, part_loss, saved, local_weight, row_state, col_state):
    sections, tensors = lax.axis_size("section"), lax.axis_size("tensor")
    features, tokens = saved.shape
    width = features * tensors
    chips = tensors // 2
    count = 2 * sections
    size = tokens // count
    pack = 2 if (2 * features) % 128 == 0 and (size // 2) % 16 == 0 else 1
    group = 512 if width % 512 == 0 else 128
    lines = -(-(width // group + 2) // 8) * 8
    part = part.reshape(count // sections, pack, size // pack, features)
    part = jnp.transpose(part, (0, 2, 1, 3)).reshape(tokens // sections // pack, pack * features)
    dma = pltpu.SemaphoreType.DMA
    vmem = pl.BlockSpec(memory_space=pltpu.VMEM)
    hbm = pl.BlockSpec(memory_space=pl.ANY)
    single = pltpu.VMEM((lines, group), jnp.float32)
    outputs, grad, total, row_new, row_scale, col_new, col_scale = pl.pallas_call(
        functools.partial(step_kernel, sections, tensors, count, pack),
        out_shape=(
            jax.ShapeDtypeStruct((tokens // pack, pack * features), jnp.bfloat16),
            jax.ShapeDtypeStruct((features, width), jnp.bfloat16),
            jax.ShapeDtypeStruct((8, 128), jnp.float32),
            jax.ShapeDtypeStruct((features, 1), jnp.float32),
            jax.ShapeDtypeStruct((features, 1), jnp.float32),
            jax.ShapeDtypeStruct((1, width), jnp.float32),
            jax.ShapeDtypeStruct((1, width), jnp.float32),
        ),
        in_specs=[vmem] * 5 + [hbm],
        out_specs=(vmem, hbm) + (vmem,) * 5,
        scratch_shapes=[
            pltpu.VMEM((features, width), jnp.bfloat16),
            pltpu.VMEM((2, features, group), jnp.bfloat16),
            pltpu.VMEM((tensors, tokens // pack, pack * features), jnp.bfloat16),
            pltpu.VMEM((tokens, width), jnp.bfloat16),
            pltpu.VMEM((features, width), jnp.float32),
            pltpu.VMEM((size, features), jnp.float32),
            pltpu.VMEM((features, 128), jnp.float32),
            pltpu.VMEM((features, 128), jnp.float32),
            pltpu.VMEM((sections, 8, 128), jnp.float32),
            pltpu.VMEM((2, lines, group), jnp.float32),
            single,
            single,
            pltpu.VMEM((chips, lines, group), jnp.float32),
            pltpu.VMEM((2, lines, group), jnp.float32),
            dma((count,)),
            dma((count,)),
            dma((count, 2 * chips)),
            dma((count, chips)),
            dma((count, chips)),
            dma((count, chips)),
            dma((sections,)),
            dma((sections,)),
            dma((count // sections + 1,)),
            dma((count // sections,)),
            dma((2,)),
            dma((2,)),
            dma((chips,)),
            dma((chips,)),
            dma((2,)),
        ],
        compiler_params=pltpu.CompilerParams(
            collective_id=0, has_side_effects=True, vmem_limit_bytes=57 * 1024 * 1024
        ),
    )(part, jnp.full((8, 128), part_loss, jnp.float32), saved, row_state, col_state, local_weight)
    outputs = outputs.reshape(count, size // pack, pack, features)
    outputs = jnp.transpose(outputs, (0, 2, 1, 3)).reshape(tokens, features)
    weight = update(local_weight, grad, row_scale, col_scale)
    return outputs, weight, total, row_new, col_new


def body(hidden_last, labels, head_weight, layer_inputs, weights, row_state, col_state):
    section_count = lax.axis_size("section")
    section_index = lax.axis_index("section")
    all_rows = labels.shape[0]
    vocab_local = head_weight.shape[1]
    local_weight = weights[0]
    saved_all = layer_inputs[0]
    columns = lax.axis_index("tensor") * vocab_local + lax.iota(jnp.int32, vocab_local)
    share_rows = all_rows // section_count
    row_start = section_index * share_rows
    hidden_rows = lax.dynamic_slice_in_dim(hidden_last, row_start, share_rows, 0)
    head_slice = head_weight
    logits = lax.dot_general(
        gather_rows(hidden_rows.T, 3),
        head_slice,
        (((0,), (0,)), ((), ())),
        preferred_element_type=jnp.float32,
    )
    exponent = jnp.exp(logits)
    label_hit = (
        lax.dynamic_slice_in_dim(labels, row_start, share_rows, 0)[:, None] == columns[None, :]
    )
    denominator, picked = packed_sum(
        (
            jnp.sum(exponent, axis=1),
            jnp.sum(jnp.where(label_hit, logits, jnp.zeros_like(logits)), axis=1),
        ),
        1,
    )
    losses = jnp.log(denominator) - picked
    logit_grad = (
        (exponent / denominator[:, None] - label_hit.astype(jnp.float32)) / all_rows
    ).astype(jnp.bfloat16)
    head_slice = head_weight
    part_grad = scatter_rows(
        lax.dot_general(
            head_slice, logit_grad, (((1,), (1,)), ((), ())), preferred_element_type=jnp.float32
        ).astype(jnp.bfloat16),
        4,
    )
    part_loss = jnp.sum(losses)
    outputs, new_weight, total, row_new, col_new = step(
        part_grad.T, part_loss, saved_all.T, local_weight, row_state.reshape(-1, 1), col_state
    )
    loss = total[0, 0] / all_rows
    return (loss, outputs[None], new_weight[None], row_new.reshape(1, -1), col_new)


def solution(mesh):
    return jax.shard_map(
        body,
        mesh=mesh,
        in_specs=(
            P(None, "tensor"),
            P(),
            P(None, "tensor"),
            P("section", None, "tensor"),
            P("section", "tensor", None),
            P("section", "tensor"),
            P("section", None),
        ),
        out_specs=(
            P(),
            P("section", None, "tensor"),
            P("section", "tensor", None),
            P("section", "tensor"),
            P("section", None),
        ),
        check_vma=False,
    )
```

```python
import functools

import jax
import jax.numpy as jnp
from jax import lax
from jax.experimental import pallas as pl
from jax.experimental.pallas import tpu as pltpu
from jax.sharding import PartitionSpec as P

decay_rate = 0.9
learn_rate = 0.3
tiny_term = 1e-30


MESH = pl.DeviceIdType.MESH


def origin_of(chips, chip, index):
    if index == 0:
        return chip
    near_side = jnp.where(chip * 2 < chips, -1, 1)
    both = jnp.minimum(chip, chips - 1 - chip)
    paired = index <= 2 * both
    distance = jnp.where(paired, (index + 1) // 2, index - both)
    toward_near = paired & (index % 2 == 0)
    return chip + jnp.where(toward_near, near_side, -near_side) * distance


def onward_of(chips, chip, origin):
    onward = jnp.where(origin < chip, chip + 1, chip - 1)
    inner = (origin > 0) & (origin < chips - 1)
    return onward, inner & (onward >= 0) & (onward < chips)


def head_kernel(
    tensors, pack, per, hidden_ref, labels_ref, w_ref, part_ref, loss_ref,
    weight, tokens_ref, logits, slopes, mine, near_out, near, far_out, far, own_sums, sums,
    weight_sem, send_line, recv_line, send_mate, recv_mate, send_sum, recv_sum,
    send_near, recv_near, send_far, recv_far, local_sem,
):
    section = lax.axis_index("section")
    me = lax.axis_index("tensor")
    chips = tensors // 2
    chip, core = me // 2, me % 2
    mate = chip * 2 + 1 - core
    vocab, width = weight.shape
    features = width // tensors
    share = tokens_ref.shape[1]
    all_rows = labels_ref.shape[1]
    joined = 2 if (2 * features) % 128 == 0 else tensors
    groups = tensors // joined
    span = joined * features
    is_end = (chip == 0) | (chip == chips - 1)
    my_tokens = pl.ds(pl.multiple_of(section * share, 128), share)

    def remote(src, dst, send, recv, device):
        return pltpu.make_async_remote_copy(
            src_ref=src, dst_ref=dst, send_sem=send, recv_sem=recv,
            device_id={"tensor": device}, device_id_type=MESH,
        )

    def block(device):
        return tokens_ref.at[pl.ds(pl.multiple_of(device * features, 16), features), :]

    def line_copy(origin, there):
        where = block(origin * 2 + core)
        slot = jnp.where(origin == chip, 0, chips) + there
        return remote(where, where, send_line.at[slot], recv_line.at[origin], there * 2 + core)

    def mate_copy(origin, side):
        where = block(origin * 2 + side)
        return remote(where, where, send_mate.at[origin], recv_mate.at[origin], mate)

    def weight_copy(index):
        first = origin_of(chips, chip, index) * 2 if joined == 2 else 0
        lanes = pl.ds(pl.multiple_of(first * features, 128), span)
        return pltpu.make_async_copy(w_ref.at[:, lanes], weight.at[:, lanes], weight_sem.at[index])

    def own_copy():
        return pltpu.make_async_copy(hidden_ref.at[:, my_tokens], block(me), local_sem.at[0])

    own_copy().start()
    for index in range(groups):
        weight_copy(index).start()

    barrier = pltpu.get_barrier_semaphore()
    others = [lax.rem(me + step, tensors) for step in range(1, tensors)]
    for other in others:
        pl.semaphore_signal(barrier, inc=1, device_id={"tensor": other}, device_id_type=MESH)
    pl.semaphore_wait(barrier, tensors - 1)

    own_copy().wait()

    @pl.when(is_end)
    def _():
        for index in range(1, chips):
            line_copy(chip, jnp.where(chip == 0, index, chips - 1 - index)).start()

    if chips > 2:
        @pl.when(jnp.logical_not(is_end))
        def _():
            line_copy(chip, chip + 1).start()
            line_copy(chip, chip - 1).start()

    mate_copy(chip, core).start()

    tile = max([size for size in range(16, 801, 16) if vocab % size == 0], default=vocab)

    def product(index, fresh):
        first = origin_of(chips, chip, index) * 2 if joined == 2 else 0
        lanes = pl.ds(pl.multiple_of(first * features, 128), span)

        def rows_step(number, carry):
            rows = pl.ds(pl.multiple_of(number * tile, 8), tile)
            value = jnp.dot(weight[rows, lanes], tokens_ref[lanes, :], preferred_element_type=jnp.float32)
            logits[rows, :] = value if fresh else logits[rows, :] + value
            return carry

        lax.fori_loop(0, vocab // tile, rows_step, 0)

    for index in range(chips):
        origin = origin_of(chips, chip, index)
        if index:
            line_copy(origin, chip).wait_recv()
            onward, wanted = onward_of(chips, chip, origin)

            @pl.when(wanted)
            def _():
                line_copy(origin, jnp.clip(onward, 0, chips - 1)).start()

            mate_copy(origin, core).start()
        mate_copy(origin, 1 - core).wait_recv()
        if joined == 2:
            weight_copy(index).wait()
            product(index, index == 0)
        elif index == chips - 1:
            weight_copy(0).wait()
            product(0, True)

    labels = labels_ref[:, my_tokens]
    step_rows = max(size for size in range(8, 201, 8) if vocab % size == 0)

    def sum_step(number, carry):
        total, picked = carry
        rows = pl.ds(pl.multiple_of(number * step_rows, 8), step_rows)
        value = logits[rows, :]
        entries = lax.broadcasted_iota(jnp.int32, value.shape, 0) + (me * vocab + number * step_rows)
        exponent = jnp.exp(value)
        logits[rows, :] = exponent
        chosen = jnp.where(entries == labels, value, jnp.zeros_like(value))
        shape = (step_rows // 8, 8, share)
        return total + jnp.sum(exponent.reshape(shape), axis=0), picked + jnp.sum(chosen.reshape(shape), axis=0)

    zeros = jnp.zeros((8, share), jnp.float32)
    total, picked = lax.fori_loop(0, vocab // step_rows, sum_step, (zeros, zeros))
    own_sums[...] = jnp.concatenate(
        [
            jnp.broadcast_to(jnp.sum(total, axis=0, keepdims=True), (4, share)),
            jnp.broadcast_to(jnp.sum(picked, axis=0, keepdims=True), (4, share)),
        ],
        axis=0,
    )

    def sum_copy(source, other):
        return remote(own_sums, sums.at[source], send_sum.at[other], recv_sum.at[source], other)

    for other in others:
        sum_copy(me, other).start()
    sums[me] = own_sums[...]
    for other in others:
        sum_copy(other, other).wait_recv()
    both = jnp.sum(sums[...], axis=0)
    denominator, picked = both[:1, :], both[4:5, :]
    losses = jnp.sum(jnp.log(denominator) - picked, axis=1, keepdims=True)
    loss_ref[...] = jnp.broadcast_to(losses, loss_ref.shape)

    def slope_of(start, size):
        value = logits[pl.ds(pl.multiple_of(start, 8), size), :]
        entries = lax.broadcasted_iota(jnp.int32, value.shape, 0) + (me * vocab + start)
        hit = (entries == labels).astype(jnp.float32)
        return ((value / denominator - hit) / all_rows).T.astype(slopes.dtype)

    def slope_step(number, carry):
        start = pl.multiple_of(number * 128, 128)
        slopes[:, pl.ds(start, 128)] = slope_of(start, 128)
        return carry

    lax.fori_loop(0, vocab // 128, slope_step, 0)
    if vocab % 128:
        start = vocab // 128 * 128
        slopes[:, start:] = slope_of(start, vocab - start)

    depth = share // per // pack

    def packed(value):
        rows = []
        for index in range(per):
            base = index * pack * depth
            rows.append(
                jnp.concatenate(
                    [value[base + part * depth : base + (part + 1) * depth] for part in range(pack)], axis=1
                )
            )
        return jnp.concatenate(rows, axis=0) if per > 1 else rows[0]

    def near_copy(there):
        return remote(near_out.at[there], near.at[there], send_near.at[there], recv_near.at[there], mate)

    def far_copy(source, there):
        return remote(far_out.at[there], far.at[source], send_far.at[there], recv_far.at[source], there * 2 + core)

    def split(there):
        if joined == 2:
            lanes = pl.ds(pl.multiple_of(there * span, 128), span)
            value = jnp.dot(slopes[...], weight[:, lanes], preferred_element_type=jnp.float32)
            left, right = value[:, :features], value[:, features:]
        else:
            value = jnp.dot(slopes[...], weight[...], preferred_element_type=jnp.float32)
            left = jnp.zeros((share, features), jnp.float32)
            right = left
            for index in range(chips):
                base = index * 2 * features
                left = jnp.where(there == index, value[:, base : base + features], left)
                right = jnp.where(there == index, value[:, base + features : base + 2 * features], right)
        first = core == 0
        return jnp.where(first, left, right), jnp.where(first, right, left)

    def target_of(index):
        return lax.rem(chip + 1 + index, chips)

    def pair_sum(index):
        there = target_of(index)
        near_copy(there).wait_recv()
        return mine[lax.rem(index, 2)] + near[there].astype(jnp.float32)

    def scatter_step(index, carry):
        there = target_of(index)
        kept, given = split(there)
        mine[lax.rem(index, 2)] = packed(kept)
        near_out[there] = packed(given).astype(near_out.dtype)
        near_copy(there).start()

        @pl.when(index > 0)
        def _():
            before = target_of(index - 1)
            far_out[before] = pair_sum(index - 1).astype(far_out.dtype)
            far_copy(chip, before).start()

        return carry

    lax.fori_loop(0, chips, scatter_step, 0)
    result = pair_sum(chips - 1)
    chips_out = [lax.rem(chip + step, chips) for step in range(1, chips)]
    for there in chips_out:
        far_copy(there, there).wait_recv()
        result = result + far[there].astype(jnp.float32)
    part_ref[...] = result.astype(part_ref.dtype)

    @pl.when(is_end)
    def _():
        for index in range(1, chips):
            line_copy(chip, jnp.where(chip == 0, index, chips - 1 - index)).wait_send()

    if chips > 2:
        @pl.when(jnp.logical_not(is_end))
        def _():
            line_copy(chip, chip + 1).wait_send()
            line_copy(chip, chip - 1).wait_send()

    mate_copy(chip, core).wait_send()
    for index in range(1, chips):
        origin = origin_of(chips, chip, index)
        onward, wanted = onward_of(chips, chip, origin)

        @pl.when(wanted)
        def _():
            line_copy(origin, jnp.clip(onward, 0, chips - 1)).wait_send()

        mate_copy(origin, core).wait_send()
    for other in others:
        sum_copy(me, other).wait_send()
    for there in chips_out + [chip]:
        near_copy(there).wait_send()
    for there in chips_out:
        far_copy(chip, there).wait_send()


def head(hidden, labels, head_weight, pack, per):
    sections, tensors = lax.axis_size("section"), lax.axis_size("tensor")
    chips = tensors // 2
    features, tokens = hidden.shape
    vocab, width = head_weight.shape
    share = tokens // sections
    groups = chips if (2 * features) % 128 == 0 else 1
    dma = pltpu.SemaphoreType.DMA
    vmem = pl.BlockSpec(memory_space=pltpu.VMEM)
    hbm = pl.BlockSpec(memory_space=pl.ANY)
    dense = (share // pack, pack * features)
    held = pltpu.VMEM((chips,) + dense, jnp.bfloat16)
    return pl.pallas_call(
        functools.partial(head_kernel, tensors, pack, per),
        out_shape=(
            jax.ShapeDtypeStruct(dense, jnp.bfloat16),
            jax.ShapeDtypeStruct((8, 128), jnp.float32),
        ),
        in_specs=[hbm, vmem, hbm],
        out_specs=(vmem, vmem),
        scratch_shapes=[
            pltpu.VMEM((vocab, width), jnp.bfloat16),
            pltpu.VMEM((width, share), jnp.bfloat16),
            pltpu.VMEM((vocab, share), jnp.float32),
            pltpu.VMEM((share, vocab), jnp.bfloat16),
            pltpu.VMEM((2,) + dense, jnp.float32),
            held, held, held, held,
            pltpu.VMEM((8, share), jnp.float32),
            pltpu.VMEM((tensors, 8, share), jnp.float32),
            dma((groups,)),
            dma((2 * chips,)),
            dma((chips,)),
            dma((chips,)),
            dma((chips,)),
            dma((tensors,)),
            dma((tensors,)),
            dma((chips,)),
            dma((chips,)),
            dma((chips,)),
            dma((chips,)),
            dma((1,)),
        ],
        compiler_params=pltpu.CompilerParams(
            collective_id=1, has_side_effects=True, vmem_limit_bytes=67_000_000
        ),
    )(hidden, labels, head_weight)


def step_kernel(
    sections, tensors, count, pack, part_ref, loss_ref, x_ref, row_ref, col_ref, w_ref,
    out_ref, grad_out, total_ref, row_out, row_scale, col_out, col_scale,
    weight_ref, stage, held, carried, grad, acc_ref, row_acc, row_full, loss_buf, vectors, near, pair_sum, spread, final,
    send_x, recv_x, send_z, recv_z, send_mate, recv_mate, send_loss, recv_loss, local_sem, head_sem,
    send_sum, recv_sum, send_far, recv_far, stage_sem,
):
    section = lax.axis_index("section")
    me = lax.axis_index("tensor")
    chips = tensors // 2
    chip, core = me // 2, me % 2
    mate = chip * 2 + 1 - core
    last = sections - 1
    tokens, width = carried.shape
    features = acc_ref.shape[1]
    size = tokens // count
    per = count // sections
    depth = size // pack
    group = vectors.shape[2]
    used = width // group
    joined = 2 if (2 * features) % 128 == 0 else tensors
    span = joined * features

    def rem(a, b):
        return lax.rem(a, b)

    def share_of(step):
        return (last - step // per) * per + rem(step, per)

    def rows_of(step):
        return pl.ds(pl.multiple_of(share_of(step) * size, size), size)

    def packed_of(step):
        return pl.ds(pl.multiple_of(share_of(step) * depth, depth), depth)

    def remote(src, dst, send, recv, device):
        return pltpu.make_async_remote_copy(
            src_ref=src, dst_ref=dst, send_sem=send, recv_sem=recv, device_id=device, device_id_type=MESH
        )

    def block(device, step):
        return held.at[device, packed_of(step), :]

    def line_copy(step, origin, there):
        where = block(origin * 2 + core, step)
        slot = jnp.where(origin == chip, 0, chips) + there
        return remote(where, where, send_z.at[step, slot], recv_z.at[step, origin], {"tensor": there * 2 + core})

    def mate_copy(step, origin, side):
        where = block(origin * 2 + side, step)
        return remote(where, where, send_mate.at[step, origin], recv_mate.at[step, origin], {"tensor": mate})

    def down_copy(step):
        below = jnp.maximum(section - 1, 0)
        return remote(
            out_ref.at[packed_of(step), :], block(me, step), send_x.at[step], recv_x.at[step], {"section": below}
        )

    def head_copy(index):
        step = (last - section) * per + index
        return remote(
            part_ref.at[pl.ds(index * depth, depth), :], block(me, step),
            head_sem.at[index], recv_x.at[step], {"section": last},
        )

    def own_copy(index):
        return pltpu.make_async_copy(
            part_ref.at[pl.ds(index * depth, depth), :], block(me, index), local_sem.at[index]
        )

    def weight_copy():
        return pltpu.make_async_copy(w_ref, weight_ref, local_sem.at[per])

    def loss_copy(source, there):
        return remote(
            loss_ref, loss_buf.at[source], send_loss.at[there], recv_loss.at[source], {"section": there}
        )

    barrier = pltpu.get_barrier_semaphore()
    greeted = [{"tensor": mate}]
    greeted += [{"tensor": rem(chip + step, chips) * 2 + core} for step in range(1, chips)]
    greeted += [{"section": rem(section + step, sections)} for step in range(1, sections)]
    weight_copy().start()
    for device in greeted:
        pl.semaphore_signal(barrier, inc=1, device_id=device, device_id_type=MESH)
    pl.semaphore_wait(barrier, len(greeted))

    @pl.when(section == last)
    def _():
        for index in range(per):
            own_copy(index).start()

    @pl.when(section != last)
    def _():
        for index in range(per):
            head_copy(index).start()

    for step in range(1, sections):
        loss_copy(section, rem(section + step, sections)).start()

    is_end = (chip == 0) | (chip == chips - 1)

    def launch(step):
        @pl.when((section == last) & (step < per))
        def _():
            own_copy(jnp.minimum(step, per - 1)).wait()

        @pl.when((section != last) | (step >= per))
        def _():
            down_copy(step).wait_recv()

        @pl.when(is_end)
        def _():
            for index in range(1, chips):
                line_copy(step, chip, jnp.where(chip == 0, index, chips - 1 - index)).start()

        if chips > 2:
            @pl.when(jnp.logical_not(is_end))
            def _():
                line_copy(step, chip, chip + 1).start()
                line_copy(step, chip, chip - 1).start()

        mate_copy(step, chip, core).start()

    def assemble(step, first):
        for part in range(pack):
            pieces = []
            for offset in range(joined):
                piece = held[first + offset, packed_of(step), :]
                pieces.append(piece[:, part * features : (part + 1) * features])
            rows = pl.ds(pl.multiple_of(share_of(step) * size + part * depth, depth), depth)
            lanes = pl.ds(pl.multiple_of(first * features, 128), span)
            carried[rows, lanes] = jnp.concatenate(pieces, axis=1)

    def product(step, first, fresh):
        lanes = pl.ds(pl.multiple_of(first * features, 128), span)
        value = lax.dot_general(
            carried[rows_of(step), lanes], weight_ref[:, lanes], (((1,), (1,)), ((), ())),
            preferred_element_type=jnp.float32,
        )
        acc_ref[...] = value if fresh else acc_ref[...] + value

    def finish(step, index):
        origin = origin_of(chips, chip, index)
        mate_copy(step, origin, 1 - core).wait_recv()
        if joined == 2:
            assemble(step, origin * 2)
            product(step, origin * 2, index == 0)
        elif index == chips - 1:
            assemble(step, 0)
            product(step, 0, True)

    launch(0)
    weight_copy().wait()

    def add_squares():
        def rows_step(index, inner):
            entries = weight_ref[pl.ds(pl.multiple_of(index * 16, 16), 16), :].astype(jnp.float32)
            return inner + jnp.sum(jnp.reshape(entries * entries, (2, 8, width)), axis=0)

        sums = lax.fori_loop(0, features // 16, rows_step, jnp.zeros((8, width), jnp.float32))
        folded = sums[:, :128]
        for start in range(128, width, 128):
            folded = folded + sums[:, start : start + 128]
        vectors[1, pl.ds(used + 1, 1), :] = jnp.broadcast_to(jnp.sum(folded, keepdims=True), (1, group))

    vectors[...] = jnp.zeros_like(vectors)

    @pl.when(section != last)
    def _():
        add_squares()

    half = count // 2
    low = tokens // 2
    cut = width // half

    def advance(step, carry):
        for index in range(1, chips):
            if index == min(2, chips - 1):
                @pl.when(step + 1 < count)
                def _():
                    launch(jnp.minimum(step + 1, count - 1))

            origin = origin_of(chips, chip, index)
            line_copy(step, origin, chip).wait_recv()
            onward, wanted = onward_of(chips, chip, origin)

            @pl.when(wanted)
            def _():
                line_copy(step, origin, jnp.clip(onward, 0, chips - 1)).start()

            mate_copy(step, origin, core).start()
            finish(step, index - 1)
        finish(step, chips - 1)
        sums = jnp.concatenate([acc_ref[part * depth : (part + 1) * depth, :] for part in range(pack)], axis=1)
        mine = held[me, packed_of(step), :].astype(jnp.float32)
        out_ref[packed_of(step), :] = (mine + sums).astype(out_ref.dtype)

        @pl.when(section > 0)
        def _():
            down_copy(step).start()

        @pl.when(step >= half)
        def _():
            lanes = pl.ds(pl.multiple_of((step - half) * cut, 128), cut)
            grad[:, lanes] = jnp.dot(
                x_ref[:, low:], carried[low:, lanes], preferred_element_type=jnp.float32
            )

        return carry

    lax.fori_loop(0, count, advance, 0)

    @pl.when(section == last)
    def _():
        add_squares()

    row_acc[...] = jnp.zeros_like(row_acc)

    def stage_copy(index):
        lanes = pl.ds(pl.multiple_of(index * group, 128), group)
        slot = rem(index, 2)
        return pltpu.make_async_copy(stage.at[slot], grad_out.at[:, lanes], stage_sem.at[slot])

    def gather_squares(index, carry):
        lanes = pl.ds(pl.multiple_of(index * group, 128), group)
        value = grad[:, lanes] + jnp.dot(
            x_ref[:, :low], carried[:low, lanes], preferred_element_type=jnp.float32
        )
        grad[:, lanes] = value

        @pl.when(index > 1)
        def _():
            stage_copy(index - 2).wait()

        slot = rem(index, 2)
        inner = jnp.zeros((8, group), jnp.float32)
        for start in range(0, features, 16):
            entries = grad[start : start + 16, lanes]
            stage[slot, start : start + 16, :] = entries.astype(stage.dtype)
            squares = entries * entries + tiny_term
            folded = squares[:, :128]
            for lane in range(128, group, 128):
                folded = folded + squares[:, lane : lane + 128]
            row_acc[start : start + 16, :] = row_acc[start : start + 16, :] + folded
            inner = inner + jnp.sum(jnp.reshape(squares, (2, 8, group)), axis=0)
        vectors[0, pl.ds(index, 1), :] = jnp.sum(inner, axis=0, keepdims=True)
        stage_copy(index).start()
        return carry

    lax.fori_loop(0, used, gather_squares, 0)
    sums = jnp.sum(row_acc[...], axis=1, keepdims=True)
    fresh_row = decay_rate * row_ref[...] + (1.0 - decay_rate) * (sums / width)
    row_out[...] = fresh_row
    vectors[1, pl.ds(used, 1), :] = jnp.broadcast_to(jnp.sum(fresh_row, keepdims=True), (1, group))
    row_full[...] = jnp.broadcast_to(1.0 / fresh_row, row_full.shape)

    def gather_scaled(index, carry):
        lanes = pl.ds(pl.multiple_of(index * group, 128), group)
        inner = jnp.zeros((8, group), jnp.float32)
        for start in range(0, features, 16):
            entries = grad[start : start + 16, lanes]
            shrink = jnp.concatenate([row_full[start : start + 16, :]] * (group // 128), axis=1)
            inner = inner + jnp.sum(jnp.reshape(entries * entries * shrink, (2, 8, group)), axis=0)
        vectors[1, pl.ds(index, 1), :] = jnp.sum(inner, axis=0, keepdims=True)
        return carry

    lax.fori_loop(0, used, gather_scaled, 0)

    def mate_sum():
        return remote(vectors.at[1 - core], near, send_sum.at[0], recv_sum.at[0], {"tensor": mate})

    def far_sum(source, there):
        return remote(
            pair_sum, spread.at[source], send_far.at[there], recv_far.at[source], {"tensor": there * 2 + core}
        )

    def mate_total(side):
        return remote(final.at[side], final.at[side], send_sum.at[1], recv_sum.at[1], {"tensor": mate})

    others = [rem(chip + step, chips) for step in range(1, chips)]
    mate_sum().start()
    mate_sum().wait_recv()
    pair_sum[...] = vectors[core] + near[...]
    for there in others:
        far_sum(chip, there).start()
    spread[chip] = pair_sum[...]
    for there in others:
        far_sum(there, there).wait_recv()
    final[core] = jnp.sum(spread[...], axis=0)
    mate_total(core).start()

    total = None
    for step in range(1, sections):
        other = rem(section + step, sections)
        loss_copy(other, other).wait_recv()
    loss_buf[section] = loss_ref[...]
    total_ref[...] = jnp.sum(loss_buf[...], axis=0)

    mate_total(1 - core).wait_recv()

    entries = float(width * width)
    row_total = final[1, used : used + 1, :][:, :1]
    weight_total = final[1, used + 1 : used + 2, :][:, :1]

    def update_columns(index, inner):
        lanes = pl.ds(pl.multiple_of(index * group, 128), group)
        fresh = decay_rate * col_ref[:, lanes] + (1.0 - decay_rate) * (final[0, pl.ds(index, 1), :] / width)
        col_out[:, lanes] = fresh
        col_scale[:, lanes] = lax.rsqrt(fresh)
        return inner + final[1, pl.ds(index, 1), :] / fresh

    scaled = lax.fori_loop(0, used, update_columns, jnp.zeros((1, group), jnp.float32))
    update_total = row_total * jnp.sum(scaled, axis=1, keepdims=True)
    factor = (
        learn_rate * jnp.sqrt(weight_total / entries)
        / jnp.maximum(1.0, jnp.sqrt(update_total / entries))
    )
    row_scale[...] = lax.rsqrt(row_out[...]) * (factor * jnp.sqrt(row_total))
    for index in (used - 2, used - 1):
        stage_copy(index).wait()

    def drain(step, carry):
        @pl.when(section > 0)
        def _():
            down_copy(step).wait_send()

        @pl.when(is_end)
        def _():
            for index in range(1, chips):
                line_copy(step, chip, jnp.where(chip == 0, index, chips - 1 - index)).wait_send()

        if chips > 2:
            @pl.when(jnp.logical_not(is_end))
            def _():
                line_copy(step, chip, chip + 1).wait_send()
                line_copy(step, chip, chip - 1).wait_send()

        mate_copy(step, chip, core).wait_send()
        for index in range(1, chips):
            origin = origin_of(chips, chip, index)
            onward, wanted = onward_of(chips, chip, origin)

            @pl.when(wanted)
            def _():
                line_copy(step, origin, jnp.clip(onward, 0, chips - 1)).wait_send()

            mate_copy(step, origin, core).wait_send()
        return carry

    lax.fori_loop(0, count, drain, 0)
    for step in range(1, sections):
        loss_copy(section, rem(section + step, sections)).wait_send()

    @pl.when(section != last)
    def _():
        for index in range(per):
            head_copy(index).wait_send()

    mate_sum().wait_send()
    for there in others:
        far_sum(chip, there).wait_send()
    mate_total(core).wait_send()


def update_kernel(
    pack, size, weight_ref, grad_ref, scale_ref, col_ref, carried_ref, row_ref, col_in, total_ref,
    weight_out, carried_out, row_out, col_out, loss_out,
):
    rows, width = weight_out.shape
    group = 512 if width % 512 == 0 else 128

    @pl.when(pl.program_id(0) == 0)
    def _():
        features, tokens = carried_out.shape
        depth = size // pack
        for start in range(0, tokens, 2 * size):
            pieces = []
            for share in (start // size, start // size + 1):
                entries = carried_ref[share * depth : (share + 1) * depth, :].astype(jnp.float32)
                pieces += [entries[:, part * features : (part + 1) * features] for part in range(pack)]
            joined = jnp.concatenate(pieces, axis=0)
            carried_out[:, start : start + 2 * size] = joined.T.astype(carried_out.dtype)
        row_out[...] = jnp.broadcast_to(row_ref[...], (features, 128)).T[:1, :]
        col_out[...] = col_in[...]
        loss_out[...] = total_ref[:1, :1] / tokens

    for start in range(0, rows, 16):
        scale = jnp.broadcast_to(scale_ref[start : start + 16, :], (16, group))
        for lane in range(0, width, group):
            change = grad_ref[start : start + 16, lane : lane + group].astype(jnp.float32)
            change = change * (scale * col_ref[:, lane : lane + group])
            entries = weight_ref[start : start + 16, lane : lane + group].astype(jnp.float32)
            weight_out[start : start + 16, lane : lane + group] = (entries - change).astype(weight_out.dtype)


def update(pack, size, tokens, weight, grad, row_scale, col_scale, outputs, row_new, col_new, total):
    features, width = weight.shape
    rows = max(size for size in range(16, 65, 16) if features % size == 0)
    tile = pl.BlockSpec((rows, width), lambda index: (index, 0))

    def whole(shape):
        return pl.BlockSpec(shape, lambda index: (0, 0))

    return pl.pallas_call(
        functools.partial(update_kernel, pack, size),
        grid=(features // rows,),
        out_shape=(
            jax.ShapeDtypeStruct((features, width), jnp.bfloat16),
            jax.ShapeDtypeStruct((features, tokens), jnp.bfloat16),
            jax.ShapeDtypeStruct((1, features), jnp.float32),
            jax.ShapeDtypeStruct((1, width), jnp.float32),
            jax.ShapeDtypeStruct((1, 1), jnp.float32),
        ),
        in_specs=[
            tile, tile, pl.BlockSpec((rows, 1), lambda index: (index, 0)), whole((1, width)),
            whole(outputs.shape), whole((features, 1)), whole((1, width)), whole((8, 128)),
        ],
        out_specs=(tile, whole((features, tokens)), whole((1, features)), whole((1, width)), whole((1, 1))),
        compiler_params=pltpu.CompilerParams(vmem_limit_bytes=56 * 1024 * 1024),
    )(weight, grad, row_scale, col_scale, outputs, row_new, col_new, total)


def step(part, losses, saved, local_weight, row_state, col_state, pack, count):
    sections, tensors = lax.axis_size("section"), lax.axis_size("tensor")
    features, tokens = saved.shape
    width = features * tensors
    chips = tensors // 2
    size = tokens // count
    group = 512 if width % 512 == 0 else 128
    lines = -(-(width // group + 2) // 8) * 8
    dma = pltpu.SemaphoreType.DMA
    vmem = pl.BlockSpec(memory_space=pltpu.VMEM)
    hbm = pl.BlockSpec(memory_space=pl.ANY)
    single = pltpu.VMEM((lines, group), jnp.float32)
    outputs, grad, total, row_new, row_scale, col_new, col_scale = pl.pallas_call(
        functools.partial(step_kernel, sections, tensors, count, pack),
        out_shape=(
            jax.ShapeDtypeStruct((tokens // pack, pack * features), jnp.bfloat16),
            jax.ShapeDtypeStruct((features, width), jnp.bfloat16),
            jax.ShapeDtypeStruct((8, 128), jnp.float32),
            jax.ShapeDtypeStruct((features, 1), jnp.float32),
            jax.ShapeDtypeStruct((features, 1), jnp.float32),
            jax.ShapeDtypeStruct((1, width), jnp.float32),
            jax.ShapeDtypeStruct((1, width), jnp.float32),
        ),
        in_specs=[vmem] * 5 + [hbm],
        out_specs=(vmem, hbm) + (vmem,) * 5,
        scratch_shapes=[
            pltpu.VMEM((features, width), jnp.bfloat16),
            pltpu.VMEM((2, features, group), jnp.bfloat16),
            pltpu.VMEM((tensors, tokens // pack, pack * features), jnp.bfloat16),
            pltpu.VMEM((tokens, width), jnp.bfloat16),
            pltpu.VMEM((features, width), jnp.float32),
            pltpu.VMEM((size, features), jnp.float32),
            pltpu.VMEM((features, 128), jnp.float32),
            pltpu.VMEM((features, 128), jnp.float32),
            pltpu.VMEM((sections, 8, 128), jnp.float32),
            pltpu.VMEM((2, lines, group), jnp.float32),
            single,
            single,
            pltpu.VMEM((chips, lines, group), jnp.float32),
            pltpu.VMEM((2, lines, group), jnp.float32),
            dma((count,)),
            dma((count,)),
            dma((count, 2 * chips)),
            dma((count, chips)),
            dma((count, chips)),
            dma((count, chips)),
            dma((sections,)),
            dma((sections,)),
            dma((count // sections + 1,)),
            dma((count // sections,)),
            dma((2,)),
            dma((2,)),
            dma((chips,)),
            dma((chips,)),
            dma((2,)),
        ],
        compiler_params=pltpu.CompilerParams(
            collective_id=0, has_side_effects=True, vmem_limit_bytes=57 * 1024 * 1024
        ),
    )(part, losses, saved, row_state, col_state, local_weight)
    return update(pack, size, tokens, local_weight, grad, row_scale, col_scale, outputs, row_new, col_new, total)


def body(hidden_last, labels, head_weight, layer_inputs, weights, row_state, col_state):
    sections, tensors = lax.axis_size("section"), lax.axis_size("tensor")
    tokens, features = hidden_last.shape
    count = 2 * sections
    size = tokens // count
    pack = 2 if (2 * features) % 128 == 0 and (size // 2) % 16 == 0 else 1
    part, losses = head(hidden_last.T, labels.reshape(1, -1), head_weight.T, pack, count // sections)
    new_weight, outputs, row_new, col_new, loss = step(
        part, losses, layer_inputs[0].T, weights[0], row_state.reshape(-1, 1), col_state, pack, count
    )
    return (loss[0, 0], outputs.T[None], new_weight[None], row_new, col_new)


def solution(mesh):
    return jax.shard_map(
        body,
        mesh=mesh,
        in_specs=(
            P(None, "tensor"),
            P(),
            P(None, "tensor"),
            P("section", None, "tensor"),
            P("section", "tensor", None),
            P("section", "tensor"),
            P("section", None),
        ),
        out_specs=(
            P(),
            P("section", None, "tensor"),
            P("section", "tensor", None),
            P("section", "tensor"),
            P("section", None),
        ),
        check_vma=False,
    )
```

```python
import functools

import jax
import jax.numpy as jnp
from jax import lax
from jax.experimental import pallas as pl
from jax.experimental.pallas import tpu as pltpu
from jax.sharding import PartitionSpec as P

decay_rate = 0.9
learn_rate = 0.3
tiny_term = 1e-30


MESH = pl.DeviceIdType.MESH


def origin_of(chips, chip, index):
    if index == 0:
        return chip
    near_side = jnp.where(chip * 2 < chips, -1, 1)
    both = jnp.minimum(chip, chips - 1 - chip)
    paired = index <= 2 * both
    distance = jnp.where(paired, (index + 1) // 2, index - both)
    toward_near = paired & (index % 2 == 0)
    return chip + jnp.where(toward_near, near_side, -near_side) * distance


def onward_of(chips, chip, origin):
    onward = jnp.where(origin < chip, chip + 1, chip - 1)
    inner = (origin > 0) & (origin < chips - 1)
    return onward, inner & (onward >= 0) & (onward < chips)


def head_kernel(
    tensors, pack, per, hidden_ref, labels_ref, w_ref, part_ref, loss_ref,
    weight, tokens_ref, logits, slopes, mine, near_out, near, far_out, far, own_sums, sums,
    weight_sem, send_line, recv_line, send_mate, recv_mate, send_sum, recv_sum,
    send_near, recv_near, send_far, recv_far, local_sem,
):
    section = lax.axis_index("section")
    me = lax.axis_index("tensor")
    chips = tensors // 2
    chip, core = me // 2, me % 2
    mate = chip * 2 + 1 - core
    vocab, width = weight.shape
    features = width // tensors
    share = tokens_ref.shape[1]
    all_rows = labels_ref.shape[1]
    joined = 2 if (2 * features) % 128 == 0 else tensors
    groups = tensors // joined
    span = joined * features
    is_end = (chip == 0) | (chip == chips - 1)
    my_tokens = pl.ds(pl.multiple_of(section * share, 128), share)

    def remote(src, dst, send, recv, device):
        return pltpu.make_async_remote_copy(
            src_ref=src, dst_ref=dst, send_sem=send, recv_sem=recv,
            device_id={"tensor": device}, device_id_type=MESH,
        )

    def block(device):
        return tokens_ref.at[pl.ds(pl.multiple_of(device * features, 16), features), :]

    def line_copy(origin, there):
        where = block(origin * 2 + core)
        slot = jnp.where(origin == chip, 0, chips) + there
        return remote(where, where, send_line.at[slot], recv_line.at[origin], there * 2 + core)

    def mate_copy(origin, side):
        where = block(origin * 2 + side)
        return remote(where, where, send_mate.at[origin], recv_mate.at[origin], mate)

    def weight_copy(index):
        first = origin_of(chips, chip, index) * 2 if joined == 2 else 0
        lanes = pl.ds(pl.multiple_of(first * features, 128), span)
        return pltpu.make_async_copy(w_ref.at[:, lanes], weight.at[:, lanes], weight_sem.at[index])

    def own_copy():
        return pltpu.make_async_copy(hidden_ref.at[:, my_tokens], block(me), local_sem.at[0])

    own_copy().start()
    barrier = pltpu.get_barrier_semaphore()
    others = [lax.rem(me + step, tensors) for step in range(1, tensors)]
    for other in others:
        pl.semaphore_signal(barrier, inc=1, device_id={"tensor": other}, device_id_type=MESH)
    pl.semaphore_wait(barrier, tensors - 1)

    own_copy().wait()

    @pl.when(is_end)
    def _():
        for index in range(1, chips):
            line_copy(chip, jnp.where(chip == 0, index, chips - 1 - index)).start()

    if chips > 2:
        @pl.when(jnp.logical_not(is_end))
        def _():
            line_copy(chip, chip + 1).start()
            line_copy(chip, chip - 1).start()

    mate_copy(chip, core).start()
    for index in range(min(groups, 2)):
        weight_copy(index).start()

    tile = max([size for size in range(16, 801, 16) if vocab % size == 0], default=vocab)

    def product(index, fresh):
        first = origin_of(chips, chip, index) * 2 if joined == 2 else 0
        lanes = pl.ds(pl.multiple_of(first * features, 128), span)

        def rows_step(number, carry):
            rows = pl.ds(pl.multiple_of(number * tile, 8), tile)
            value = jnp.dot(weight[rows, lanes], tokens_ref[lanes, :], preferred_element_type=jnp.float32)
            logits[rows, :] = value if fresh else logits[rows, :] + value
            return carry

        lax.fori_loop(0, vocab // tile, rows_step, 0)

    def arrive(index):
        origin = origin_of(chips, chip, index)
        line_copy(origin, chip).wait_recv()
        onward, wanted = onward_of(chips, chip, origin)

        @pl.when(wanted)
        def _():
            line_copy(origin, jnp.clip(onward, 0, chips - 1)).start()

        mate_copy(origin, core).start()
        if index + 1 < groups:
            weight_copy(index + 1).start()

    def consume(index):
        mate_copy(origin_of(chips, chip, index), 1 - core).wait_recv()
        if joined == 2:
            weight_copy(index).wait()
            product(index, index == 0)
        elif index == chips - 1:
            weight_copy(0).wait()
            product(0, True)

    for index in range(1, chips):
        arrive(index)
        if index == 1:
            consume(0)
        consume(index)
    if chips == 1:
        consume(0)

    labels = labels_ref[:, my_tokens]
    step_rows = max(size for size in range(8, 201, 8) if vocab % size == 0)

    def sum_step(number, carry):
        total, picked = carry
        rows = pl.ds(pl.multiple_of(number * step_rows, 8), step_rows)
        value = logits[rows, :]
        entries = lax.broadcasted_iota(jnp.int32, value.shape, 0) + (me * vocab + number * step_rows)
        exponent = jnp.exp(value)
        logits[rows, :] = exponent
        chosen = jnp.where(entries == labels, value, jnp.zeros_like(value))
        shape = (step_rows // 8, 8, share)
        return total + jnp.sum(exponent.reshape(shape), axis=0), picked + jnp.sum(chosen.reshape(shape), axis=0)

    zeros = jnp.zeros((8, share), jnp.float32)
    total, picked = lax.fori_loop(0, vocab // step_rows, sum_step, (zeros, zeros))
    own_sums[...] = jnp.concatenate(
        [
            jnp.broadcast_to(jnp.sum(total, axis=0, keepdims=True), (4, share)),
            jnp.broadcast_to(jnp.sum(picked, axis=0, keepdims=True), (4, share)),
        ],
        axis=0,
    )

    def sum_copy(source, other):
        return remote(own_sums, sums.at[source], send_sum.at[other], recv_sum.at[source], other)

    for other in others:
        sum_copy(me, other).start()
    sums[me] = own_sums[...]
    for other in others:
        sum_copy(other, other).wait_recv()
    both = jnp.sum(sums[...], axis=0)
    denominator, picked = both[:1, :], both[4:5, :]
    losses = jnp.sum(jnp.log(denominator) - picked, axis=1, keepdims=True)
    loss_ref[...] = jnp.broadcast_to(losses, loss_ref.shape)

    def slope_of(start, size):
        value = logits[pl.ds(pl.multiple_of(start, 8), size), :]
        entries = lax.broadcasted_iota(jnp.int32, value.shape, 0) + (me * vocab + start)
        hit = (entries == labels).astype(jnp.float32)
        return ((value / denominator - hit) / all_rows).astype(slopes.dtype).T

    def slope_step(number, carry):
        start = pl.multiple_of(number * 128, 128)
        slopes[:, pl.ds(start, 128)] = slope_of(start, 128)
        return carry

    lax.fori_loop(0, vocab // 128, slope_step, 0)
    if vocab % 128:
        start = vocab // 128 * 128
        slopes[:, start:] = slope_of(start, vocab - start)

    depth = share // per // pack

    def packed(value):
        rows = []
        for index in range(per):
            base = index * pack * depth
            rows.append(
                jnp.concatenate(
                    [value[base + part * depth : base + (part + 1) * depth] for part in range(pack)], axis=1
                )
            )
        return jnp.concatenate(rows, axis=0) if per > 1 else rows[0]

    def near_copy(there):
        return remote(near_out.at[there], near.at[there], send_near.at[there], recv_near.at[there], mate)

    def far_copy(source, there):
        return remote(far_out.at[there], far.at[source], send_far.at[there], recv_far.at[source], there * 2 + core)

    def split(there):
        if joined == 2:
            lanes = pl.ds(pl.multiple_of(there * span, 128), span)
            value = jnp.dot(slopes[...], weight[:, lanes], preferred_element_type=jnp.float32)
            left, right = value[:, :features], value[:, features:]
        else:
            value = jnp.dot(slopes[...], weight[...], preferred_element_type=jnp.float32)
            left = jnp.zeros((share, features), jnp.float32)
            right = left
            for index in range(chips):
                base = index * 2 * features
                left = jnp.where(there == index, value[:, base : base + features], left)
                right = jnp.where(there == index, value[:, base + features : base + 2 * features], right)
        first = core == 0
        return jnp.where(first, left, right), jnp.where(first, right, left)

    def target_of(index):
        return lax.rem(chip + 1 + index, chips)

    def pair_sum(index):
        there = target_of(index)
        near_copy(there).wait_recv()
        return mine[lax.rem(index, 2)] + near[there].astype(jnp.float32)

    def scatter_step(index, carry):
        there = target_of(index)
        kept, given = split(there)
        mine[lax.rem(index, 2)] = packed(kept)
        near_out[there] = packed(given).astype(near_out.dtype)
        near_copy(there).start()

        @pl.when(index > 0)
        def _():
            before = target_of(index - 1)
            far_out[before] = pair_sum(index - 1).astype(far_out.dtype)
            far_copy(chip, before).start()

        return carry

    lax.fori_loop(0, chips, scatter_step, 0)
    result = pair_sum(chips - 1)
    chips_out = [lax.rem(chip + step, chips) for step in range(1, chips)]
    for there in chips_out:
        far_copy(there, there).wait_recv()
        result = result + far[there].astype(jnp.float32)
    part_ref[...] = result.astype(part_ref.dtype)

    @pl.when(is_end)
    def _():
        for index in range(1, chips):
            line_copy(chip, jnp.where(chip == 0, index, chips - 1 - index)).wait_send()

    if chips > 2:
        @pl.when(jnp.logical_not(is_end))
        def _():
            line_copy(chip, chip + 1).wait_send()
            line_copy(chip, chip - 1).wait_send()

    mate_copy(chip, core).wait_send()
    for index in range(1, chips):
        origin = origin_of(chips, chip, index)
        onward, wanted = onward_of(chips, chip, origin)

        @pl.when(wanted)
        def _():
            line_copy(origin, jnp.clip(onward, 0, chips - 1)).wait_send()

        mate_copy(origin, core).wait_send()
    for other in others:
        sum_copy(me, other).wait_send()
    for there in chips_out + [chip]:
        near_copy(there).wait_send()
    for there in chips_out:
        far_copy(chip, there).wait_send()


def head(hidden, labels, head_weight, pack, per):
    sections, tensors = lax.axis_size("section"), lax.axis_size("tensor")
    chips = tensors // 2
    features, tokens = hidden.shape
    vocab, width = head_weight.shape
    share = tokens // sections
    groups = chips if (2 * features) % 128 == 0 else 1
    dma = pltpu.SemaphoreType.DMA
    vmem = pl.BlockSpec(memory_space=pltpu.VMEM)
    hbm = pl.BlockSpec(memory_space=pl.ANY)
    dense = (share // pack, pack * features)
    held = pltpu.VMEM((chips,) + dense, jnp.bfloat16)
    return pl.pallas_call(
        functools.partial(head_kernel, tensors, pack, per),
        out_shape=(
            jax.ShapeDtypeStruct(dense, jnp.bfloat16),
            jax.ShapeDtypeStruct((8, 128), jnp.float32),
        ),
        in_specs=[hbm, vmem, hbm],
        out_specs=(vmem, vmem),
        scratch_shapes=[
            pltpu.VMEM((vocab, width), jnp.bfloat16),
            pltpu.VMEM((width, share), jnp.bfloat16),
            pltpu.VMEM((vocab, share), jnp.float32),
            pltpu.VMEM((share, vocab), jnp.bfloat16),
            pltpu.VMEM((2,) + dense, jnp.float32),
            held, held, held, held,
            pltpu.VMEM((8, share), jnp.float32),
            pltpu.VMEM((tensors, 8, share), jnp.float32),
            dma((groups,)),
            dma((2 * chips,)),
            dma((chips,)),
            dma((chips,)),
            dma((chips,)),
            dma((tensors,)),
            dma((tensors,)),
            dma((chips,)),
            dma((chips,)),
            dma((chips,)),
            dma((chips,)),
            dma((1,)),
        ],
        compiler_params=pltpu.CompilerParams(
            collective_id=1, has_side_effects=True, vmem_limit_bytes=67_000_000
        ),
    )(hidden, labels, head_weight)


def step_kernel(
    sections, tensors, count, pack, part_ref, loss_ref, x_ref, row_ref, col_ref, w_ref,
    out_ref, grad_out, total_ref, row_out, row_scale, col_out, col_scale,
    flipped, stage, held, carried, grad, acc_ref, row_acc, row_full, loss_buf, vectors, near, pair_sum, spread, final,
    send_x, recv_x, send_z, recv_z, send_mate, recv_mate, send_loss, recv_loss, local_sem, head_sem,
    send_sum, recv_sum, send_far, recv_far, stage_sem,
):
    section = lax.axis_index("section")
    me = lax.axis_index("tensor")
    chips = tensors // 2
    chip, core = me // 2, me % 2
    mate = chip * 2 + 1 - core
    last = sections - 1
    tokens, width = carried.shape
    features = acc_ref.shape[1]
    size = tokens // count
    per = count // sections
    depth = size // pack
    group = vectors.shape[2]
    used = width // group
    joined = 2 if (2 * features) % 128 == 0 else tensors
    span = joined * features

    def rem(a, b):
        return lax.rem(a, b)

    def share_of(step):
        return (last - step // per) * per + rem(step, per)

    def rows_of(step):
        return pl.ds(pl.multiple_of(share_of(step) * size, size), size)

    def packed_of(step):
        return pl.ds(pl.multiple_of(share_of(step) * depth, depth), depth)

    def remote(src, dst, send, recv, device):
        return pltpu.make_async_remote_copy(
            src_ref=src, dst_ref=dst, send_sem=send, recv_sem=recv, device_id=device, device_id_type=MESH
        )

    def block(device, step):
        return held.at[device, packed_of(step), :]

    def line_copy(step, origin, there):
        where = block(origin * 2 + core, step)
        slot = jnp.where(origin == chip, 0, chips) + there
        return remote(where, where, send_z.at[step, slot], recv_z.at[step, origin], {"tensor": there * 2 + core})

    def mate_copy(step, origin, side):
        where = block(origin * 2 + side, step)
        return remote(where, where, send_mate.at[step, origin], recv_mate.at[step, origin], {"tensor": mate})

    def down_copy(step):
        below = jnp.maximum(section - 1, 0)
        return remote(
            out_ref.at[packed_of(step), :], block(me, step), send_x.at[step], recv_x.at[step], {"section": below}
        )

    def head_copy(index):
        step = (last - section) * per + index
        return remote(
            part_ref.at[pl.ds(index * depth, depth), :], block(me, step),
            head_sem.at[index], recv_x.at[step], {"section": last},
        )

    def own_copy(index):
        return pltpu.make_async_copy(
            part_ref.at[pl.ds(index * depth, depth), :], block(me, index), local_sem.at[index]
        )

    def weight_copy(index):
        lanes = pl.ds(pl.multiple_of(index * span, 128), span)
        slot = rem(index, 2)
        return pltpu.make_async_copy(w_ref.at[:, lanes], stage.at[slot], local_sem.at[per + slot])

    def loss_copy(source, there):
        return remote(
            loss_ref, loss_buf.at[source], send_loss.at[there], recv_loss.at[source], {"section": there}
        )

    barrier = pltpu.get_barrier_semaphore()
    greeted = [{"tensor": mate}]
    greeted += [{"tensor": rem(chip + step, chips) * 2 + core} for step in range(1, chips)]
    greeted += [{"section": rem(section + step, sections)} for step in range(1, sections)]
    groups = tensors // joined
    for device in greeted:
        pl.semaphore_signal(barrier, inc=1, device_id=device, device_id_type=MESH)
    pl.semaphore_wait(barrier, len(greeted))

    @pl.when(section == last)
    def _():
        for index in range(per):
            own_copy(index).start()

    @pl.when(section != last)
    def _():
        for index in range(per):
            head_copy(index).start()

    for step in range(1, sections):
        loss_copy(section, rem(section + step, sections)).start()

    is_end = (chip == 0) | (chip == chips - 1)
    ahead = 2

    def launch(step):
        @pl.when((section == last) & (step < per))
        def _():
            own_copy(jnp.minimum(step, per - 1)).wait()

        @pl.when((section != last) | (step >= per))
        def _():
            down_copy(step).wait_recv()

        @pl.when(is_end)
        def _():
            for index in range(1, chips):
                line_copy(step, chip, jnp.where(chip == 0, index, chips - 1 - index)).start()

        if chips > 2:
            @pl.when(jnp.logical_not(is_end))
            def _():
                line_copy(step, chip, chip + 1).start()
                line_copy(step, chip, chip - 1).start()

        mate_copy(step, chip, core).start()

    def assemble(step, first):
        for part in range(pack):
            pieces = []
            for offset in range(joined):
                piece = held[first + offset, packed_of(step), :]
                pieces.append(piece[:, part * features : (part + 1) * features])
            rows = pl.ds(pl.multiple_of(share_of(step) * size + part * depth, depth), depth)
            lanes = pl.ds(pl.multiple_of(first * features, 128), span)
            carried[rows, lanes] = jnp.concatenate(pieces, axis=1)

    def product(step, first, fresh):
        lanes = pl.ds(pl.multiple_of(first * features, 128), span)
        value = jnp.dot(carried[rows_of(step), lanes], flipped[lanes, :], preferred_element_type=jnp.float32)
        acc_ref[...] = value if fresh else acc_ref[...] + value

    def finish(step, index):
        origin = origin_of(chips, chip, index)
        mate_copy(step, origin, 1 - core).wait_recv()
        if joined == 2:
            assemble(step, origin * 2)
            product(step, origin * 2, index == 0)
        elif index == chips - 1:
            assemble(step, 0)
            product(step, 0, True)

    @pl.when(section == last)
    def _():
        for index in range(ahead):
            launch(index)

    for index in range(min(groups, 2)):
        weight_copy(index).start()
    vectors[...] = jnp.zeros_like(vectors)

    def flip(index, inner):
        slot = rem(index, 2)
        weight_copy(index).wait()
        lanes = pl.ds(pl.multiple_of(index * span, 128), span)
        flipped[lanes, :] = stage[slot].T
        for start in range(0, features, 16):
            entries = stage[slot, start : start + 16, :].astype(jnp.float32)
            inner = inner + jnp.sum(jnp.reshape(entries * entries, (2, 8, span)), axis=0)

        @pl.when(index + 2 < groups)
        def _():
            weight_copy(index + 2).start()

        return inner

    squares = lax.fori_loop(0, groups, flip, jnp.zeros((8, span), jnp.float32))
    vectors[1, pl.ds(used + 1, 1), :] = jnp.broadcast_to(jnp.sum(squares, keepdims=True), (1, group))

    @pl.when(section != last)
    def _():
        for index in range(ahead):
            launch(index)

    half = count // 2
    low = tokens // 2
    pieces = 4 if half % 4 == 0 and width % 512 == 0 else 1
    stride = half // pieces
    cut = width // pieces

    def advance(step, carry):
        for index in range(1, chips):
            if index == min(2, chips - 1):
                @pl.when(step + ahead < count)
                def _():
                    launch(jnp.minimum(step + ahead, count - 1))

            origin = origin_of(chips, chip, index)
            line_copy(step, origin, chip).wait_recv()
            onward, wanted = onward_of(chips, chip, origin)

            @pl.when(wanted)
            def _():
                line_copy(step, origin, jnp.clip(onward, 0, chips - 1)).start()

            mate_copy(step, origin, core).start()
            finish(step, index - 1)
        finish(step, chips - 1)
        sums = jnp.concatenate([acc_ref[part * depth : (part + 1) * depth, :] for part in range(pack)], axis=1)
        mine = held[me, packed_of(step), :].astype(jnp.float32)
        out_ref[packed_of(step), :] = (mine + sums).astype(out_ref.dtype)

        @pl.when(section > 0)
        def _():
            down_copy(step).start()

        @pl.when((step >= half) & (rem(step, stride) == 0))
        def _():
            lanes = pl.ds(pl.multiple_of((step - half) // stride * cut, 128), cut)
            grad[:, lanes] = jnp.dot(
                x_ref[:, low:], carried[low:, lanes], preferred_element_type=jnp.float32
            )

        return carry

    lax.fori_loop(0, count, advance, 0)

    row_acc[...] = jnp.zeros_like(row_acc)

    def stage_copy(index):
        lanes = pl.ds(pl.multiple_of(index * group, 128), group)
        slot = rem(index, 2)
        return pltpu.make_async_copy(stage.at[slot, :, pl.ds(0, group)], grad_out.at[:, lanes], stage_sem.at[slot])

    def gather_squares(index, carry):
        lanes = pl.ds(pl.multiple_of(index * group, 128), group)
        value = grad[:, lanes] + jnp.dot(
            x_ref[:, :low], carried[:low, lanes], preferred_element_type=jnp.float32
        )
        grad[:, lanes] = value

        @pl.when(index > 1)
        def _():
            stage_copy(index - 2).wait()

        slot = rem(index, 2)
        inner = jnp.zeros((8, group), jnp.float32)
        for start in range(0, features, 16):
            entries = grad[start : start + 16, lanes]
            stage[slot, start : start + 16, :group] = entries.astype(stage.dtype)
            squares = entries * entries + tiny_term
            folded = squares[:, :128]
            for lane in range(128, group, 128):
                folded = folded + squares[:, lane : lane + 128]
            row_acc[start : start + 16, :] = row_acc[start : start + 16, :] + folded
            inner = inner + jnp.sum(jnp.reshape(squares, (2, 8, group)), axis=0)
        vectors[0, pl.ds(index, 1), :] = jnp.sum(inner, axis=0, keepdims=True)
        stage_copy(index).start()
        return carry

    lax.fori_loop(0, used, gather_squares, 0)
    sums = jnp.sum(row_acc[...], axis=1, keepdims=True)
    fresh_row = decay_rate * row_ref[...] + (1.0 - decay_rate) * (sums / width)
    row_out[...] = fresh_row
    vectors[1, pl.ds(used, 1), :] = jnp.broadcast_to(jnp.sum(fresh_row, keepdims=True), (1, group))
    row_full[...] = jnp.broadcast_to(1.0 / fresh_row, row_full.shape)

    def gather_scaled(index, carry):
        lanes = pl.ds(pl.multiple_of(index * group, 128), group)
        inner = jnp.zeros((8, group), jnp.float32)
        for start in range(0, features, 16):
            entries = grad[start : start + 16, lanes]
            shrink = jnp.concatenate([row_full[start : start + 16, :]] * (group // 128), axis=1)
            inner = inner + jnp.sum(jnp.reshape(entries * entries * shrink, (2, 8, group)), axis=0)
        vectors[1, pl.ds(index, 1), :] = jnp.sum(inner, axis=0, keepdims=True)
        return carry

    lax.fori_loop(0, used, gather_scaled, 0)

    def mate_sum():
        return remote(vectors.at[1 - core], near, send_sum.at[0], recv_sum.at[0], {"tensor": mate})

    def far_sum(source, there):
        return remote(
            pair_sum, spread.at[source], send_far.at[there], recv_far.at[source], {"tensor": there * 2 + core}
        )

    def mate_total(side):
        return remote(final.at[side], final.at[side], send_sum.at[1], recv_sum.at[1], {"tensor": mate})

    others = [rem(chip + step, chips) for step in range(1, chips)]
    mate_sum().start()
    mate_sum().wait_recv()
    pair_sum[...] = vectors[core] + near[...]
    for there in others:
        far_sum(chip, there).start()
    spread[chip] = pair_sum[...]
    for there in others:
        far_sum(there, there).wait_recv()
    final[core] = jnp.sum(spread[...], axis=0)
    mate_total(core).start()

    total = None
    for step in range(1, sections):
        other = rem(section + step, sections)
        loss_copy(other, other).wait_recv()
    loss_buf[section] = loss_ref[...]
    total_ref[...] = jnp.sum(loss_buf[...], axis=0)

    mate_total(1 - core).wait_recv()

    entries = float(width * width)
    row_total = final[1, used : used + 1, :][:, :1]
    weight_total = final[1, used + 1 : used + 2, :][:, :1]

    def update_columns(index, inner):
        lanes = pl.ds(pl.multiple_of(index * group, 128), group)
        fresh = decay_rate * col_ref[:, lanes] + (1.0 - decay_rate) * (final[0, pl.ds(index, 1), :] / width)
        col_out[:, lanes] = fresh
        col_scale[:, lanes] = lax.rsqrt(fresh)
        return inner + final[1, pl.ds(index, 1), :] / fresh

    scaled = lax.fori_loop(0, used, update_columns, jnp.zeros((1, group), jnp.float32))
    update_total = row_total * jnp.sum(scaled, axis=1, keepdims=True)
    factor = (
        learn_rate * jnp.sqrt(weight_total / entries)
        / jnp.maximum(1.0, jnp.sqrt(update_total / entries))
    )
    row_scale[...] = lax.rsqrt(row_out[...]) * (factor * jnp.sqrt(row_total))
    for index in (used - 2, used - 1):
        stage_copy(index).wait()

    def drain(step, carry):
        @pl.when(section > 0)
        def _():
            down_copy(step).wait_send()

        @pl.when(is_end)
        def _():
            for index in range(1, chips):
                line_copy(step, chip, jnp.where(chip == 0, index, chips - 1 - index)).wait_send()

        if chips > 2:
            @pl.when(jnp.logical_not(is_end))
            def _():
                line_copy(step, chip, chip + 1).wait_send()
                line_copy(step, chip, chip - 1).wait_send()

        mate_copy(step, chip, core).wait_send()
        for index in range(1, chips):
            origin = origin_of(chips, chip, index)
            onward, wanted = onward_of(chips, chip, origin)

            @pl.when(wanted)
            def _():
                line_copy(step, origin, jnp.clip(onward, 0, chips - 1)).wait_send()

            mate_copy(step, origin, core).wait_send()
        return carry

    lax.fori_loop(0, count, drain, 0)
    for step in range(1, sections):
        loss_copy(section, rem(section + step, sections)).wait_send()

    @pl.when(section != last)
    def _():
        for index in range(per):
            head_copy(index).wait_send()

    mate_sum().wait_send()
    for there in others:
        far_sum(chip, there).wait_send()
    mate_total(core).wait_send()


def update_kernel(
    pack, size, scale_ref, col_ref, carried_ref, row_ref, col_in, total_ref, weight_ref, grad_ref,
    weight_out, carried_out, row_out, col_out, loss_out, entries_buf, grad_buf, weight_sem, grad_sem, out_sem,
):
    count, rows, width = entries_buf.shape
    group = 512 if width % 512 == 0 else 128
    features, tokens = carried_out.shape

    def rows_of(index):
        return pl.ds(pl.multiple_of(index * rows, 16), rows)

    def weight_copy(index):
        return pltpu.make_async_copy(weight_ref.at[rows_of(index), :], entries_buf.at[index], weight_sem.at[index])

    def grad_copy(index):
        return pltpu.make_async_copy(grad_ref.at[rows_of(index), :], grad_buf.at[index], grad_sem.at[index])

    def out_copy(index):
        return pltpu.make_async_copy(entries_buf.at[index], weight_out.at[rows_of(index), :], out_sem.at[index])

    def fetch(index, carry):
        weight_copy(index).start()
        grad_copy(index).start()
        return carry

    lax.fori_loop(0, count, fetch, 0)
    depth = size // pack
    for start in range(0, tokens, 128):
        pieces = []
        for share in range(start // size, (start + 128) // size):
            entries = carried_ref[share * depth : (share + 1) * depth, :].astype(jnp.float32)
            pieces += [entries[:, part * features : (part + 1) * features] for part in range(pack)]
        joined = jnp.concatenate(pieces, axis=0)
        carried_out[:, start : start + 128] = joined.T.astype(carried_out.dtype)
    row_out[...] = jnp.broadcast_to(row_ref[...], (features, 128)).T[:1, :]
    col_out[...] = col_in[...]
    loss_out[...] = total_ref[:1, :1] / tokens

    def change(index, carry):
        weight_copy(index).wait()
        grad_copy(index).wait()
        scales = scale_ref[rows_of(index), :]
        for start in range(0, rows, 16):
            scale = jnp.broadcast_to(scales[start : start + 16, :], (16, group))
            for lane in range(0, width, group):
                lanes = slice(lane, lane + group)
                moved = grad_buf[index, start : start + 16, lanes].astype(jnp.float32)
                moved = moved * (scale * col_ref[:, lanes])
                entries = entries_buf[index, start : start + 16, lanes].astype(jnp.float32)
                entries_buf[index, start : start + 16, lanes] = (entries - moved).astype(entries_buf.dtype)
        out_copy(index).start()
        return carry

    lax.fori_loop(0, count, change, 0)

    def finish(index, carry):
        out_copy(index).wait()
        return carry

    lax.fori_loop(0, count, finish, 0)


def update(pack, size, tokens, weight, grad, row_scale, col_scale, outputs, row_new, col_new, total):
    features, width = weight.shape
    rows = max(size for size in range(16, 65, 16) if features % size == 0)
    count = features // rows
    vmem = pl.BlockSpec(memory_space=pltpu.VMEM)
    hbm = pl.BlockSpec(memory_space=pl.ANY)
    dma = pltpu.SemaphoreType.DMA((count,))
    held = pltpu.VMEM((count, rows, width), jnp.bfloat16)
    return pl.pallas_call(
        functools.partial(update_kernel, pack, size),
        out_shape=(
            jax.ShapeDtypeStruct((features, width), jnp.bfloat16),
            jax.ShapeDtypeStruct((features, tokens), jnp.bfloat16),
            jax.ShapeDtypeStruct((1, features), jnp.float32),
            jax.ShapeDtypeStruct((1, width), jnp.float32),
            jax.ShapeDtypeStruct((1, 1), jnp.float32),
        ),
        in_specs=[vmem] * 6 + [hbm] * 2,
        out_specs=(hbm,) + (vmem,) * 4,
        scratch_shapes=[held, held, dma, dma, dma],
        compiler_params=pltpu.CompilerParams(vmem_limit_bytes=60 * 1024 * 1024),
    )(row_scale, col_scale, outputs, row_new, col_new, total, weight, grad)


def step(part, losses, saved, local_weight, row_state, col_state, pack, count):
    sections, tensors = lax.axis_size("section"), lax.axis_size("tensor")
    features, tokens = saved.shape
    width = features * tensors
    chips = tensors // 2
    size = tokens // count
    group = 512 if width % 512 == 0 else 128
    span = 2 * features if (2 * features) % 128 == 0 else width
    lines = -(-(width // group + 2) // 8) * 8
    dma = pltpu.SemaphoreType.DMA
    vmem = pl.BlockSpec(memory_space=pltpu.VMEM)
    hbm = pl.BlockSpec(memory_space=pl.ANY)
    single = pltpu.VMEM((lines, group), jnp.float32)
    outputs, grad, total, row_new, row_scale, col_new, col_scale = pl.pallas_call(
        functools.partial(step_kernel, sections, tensors, count, pack),
        out_shape=(
            jax.ShapeDtypeStruct((tokens // pack, pack * features), jnp.bfloat16),
            jax.ShapeDtypeStruct((features, width), jnp.bfloat16),
            jax.ShapeDtypeStruct((8, 128), jnp.float32),
            jax.ShapeDtypeStruct((features, 1), jnp.float32),
            jax.ShapeDtypeStruct((features, 1), jnp.float32),
            jax.ShapeDtypeStruct((1, width), jnp.float32),
            jax.ShapeDtypeStruct((1, width), jnp.float32),
        ),
        in_specs=[vmem] * 5 + [hbm],
        out_specs=(vmem, hbm) + (vmem,) * 5,
        scratch_shapes=[
            pltpu.VMEM((width, features), jnp.bfloat16),
            pltpu.VMEM((2, features, span), jnp.bfloat16),
            pltpu.VMEM((tensors, tokens // pack, pack * features), jnp.bfloat16),
            pltpu.VMEM((tokens, width), jnp.bfloat16),
            pltpu.VMEM((features, width), jnp.float32),
            pltpu.VMEM((size, features), jnp.float32),
            pltpu.VMEM((features, 128), jnp.float32),
            pltpu.VMEM((features, 128), jnp.float32),
            pltpu.VMEM((sections, 8, 128), jnp.float32),
            pltpu.VMEM((2, lines, group), jnp.float32),
            single,
            single,
            pltpu.VMEM((chips, lines, group), jnp.float32),
            pltpu.VMEM((2, lines, group), jnp.float32),
            dma((count,)),
            dma((count,)),
            dma((count, 2 * chips)),
            dma((count, chips)),
            dma((count, chips)),
            dma((count, chips)),
            dma((sections,)),
            dma((sections,)),
            dma((count // sections + 2,)),
            dma((count // sections,)),
            dma((2,)),
            dma((2,)),
            dma((chips,)),
            dma((chips,)),
            dma((2,)),
        ],
        compiler_params=pltpu.CompilerParams(
            collective_id=0, has_side_effects=True, vmem_limit_bytes=66_000_000
        ),
    )(part, losses, saved, row_state, col_state, local_weight)
    return update(pack, size, tokens, local_weight, grad, row_scale, col_scale, outputs, row_new, col_new, total)


def body(hidden_last, labels, head_weight, layer_inputs, weights, row_state, col_state):
    sections, tensors = lax.axis_size("section"), lax.axis_size("tensor")
    tokens, features = hidden_last.shape
    count = 4 * sections
    size = tokens // count
    pack = 2 if (2 * features) % 128 == 0 and (size // 2) % 16 == 0 else 1
    part, losses = head(hidden_last.T, labels.reshape(1, -1), head_weight.T, pack, count // sections)
    new_weight, outputs, row_new, col_new, loss = step(
        part, losses, layer_inputs[0].T, weights[0], row_state.reshape(-1, 1), col_state, pack, count
    )
    return (loss[0, 0], outputs.T[None], new_weight[None], row_new, col_new)


def solution(mesh):
    return jax.shard_map(
        body,
        mesh=mesh,
        in_specs=(
            P(None, "tensor"),
            P(),
            P(None, "tensor"),
            P("section", None, "tensor"),
            P("section", "tensor", None),
            P("section", "tensor"),
            P("section", None),
        ),
        out_specs=(
            P(),
            P("section", None, "tensor"),
            P("section", "tensor", None),
            P("section", "tensor"),
            P("section", None),
        ),
        check_vma=False,
    )
```

```python
import functools

import jax
import jax.numpy as jnp
from jax import lax
from jax.experimental import pallas as pl
from jax.experimental.pallas import tpu as pltpu
from jax.sharding import PartitionSpec as P

decay_rate = 0.9
learn_rate = 0.3
tiny_term = 1e-30


MESH = pl.DeviceIdType.MESH


def origin_of(chips, chip, index):
    if index == 0:
        return chip
    near_side = jnp.where(chip * 2 < chips, -1, 1)
    both = jnp.minimum(chip, chips - 1 - chip)
    paired = index <= 2 * both
    distance = jnp.where(paired, (index + 1) // 2, index - both)
    toward_near = paired & (index % 2 == 0)
    return chip + jnp.where(toward_near, near_side, -near_side) * distance


def onward_of(chips, chip, origin):
    onward = jnp.where(origin < chip, chip + 1, chip - 1)
    inner = (origin > 0) & (origin < chips - 1)
    return onward, inner & (onward >= 0) & (onward < chips)


def head_kernel(
    tensors, pack, per, hidden_ref, labels_ref, w_ref, part_ref, loss_ref,
    weight, tokens_ref, logits, slopes, mine, near_out, near, far_out, far, relay, own_sums, sums,
    weight_sem, send_line, recv_line, send_mate, recv_mate, send_sum, recv_sum,
    send_near, recv_near, send_far, recv_far, recv_relay, local_sem,
):
    section = lax.axis_index("section")
    me = lax.axis_index("tensor")
    chips = tensors // 2
    chip, core = me // 2, me % 2
    mate = chip * 2 + 1 - core
    vocab, width = weight.shape
    features = width // tensors
    share = tokens_ref.shape[1]
    all_rows = labels_ref.shape[1]
    joined = 2 if (2 * features) % 128 == 0 else tensors
    groups = tensors // joined
    span = joined * features
    is_end = (chip == 0) | (chip == chips - 1)
    my_tokens = pl.ds(pl.multiple_of(section * share, 128), share)

    def remote(src, dst, send, recv, device):
        return pltpu.make_async_remote_copy(
            src_ref=src, dst_ref=dst, send_sem=send, recv_sem=recv,
            device_id={"tensor": device}, device_id_type=MESH,
        )

    def block(device):
        return tokens_ref.at[pl.ds(pl.multiple_of(device * features, 16), features), :]

    def line_copy(origin, there):
        where = block(origin * 2 + core)
        slot = jnp.where(origin == chip, 0, chips) + there
        return remote(where, where, send_line.at[slot], recv_line.at[origin], there * 2 + core)

    def mate_copy(origin, side):
        where = block(origin * 2 + side)
        return remote(where, where, send_mate.at[origin], recv_mate.at[origin], mate)

    def weight_copy(index):
        first = origin_of(chips, chip, index) * 2 if joined == 2 else 0
        lanes = pl.ds(pl.multiple_of(first * features, 128), span)
        return pltpu.make_async_copy(w_ref.at[:, lanes], weight.at[:, lanes], weight_sem.at[index])

    def own_copy():
        return pltpu.make_async_copy(hidden_ref.at[:, my_tokens], block(me), local_sem.at[0])

    own_copy().start()
    barrier = pltpu.get_barrier_semaphore()
    others = [lax.rem(me + step, tensors) for step in range(1, tensors)]
    for other in others:
        pl.semaphore_signal(barrier, inc=1, device_id={"tensor": other}, device_id_type=MESH)
    pl.semaphore_wait(barrier, tensors - 1)

    own_copy().wait()

    @pl.when(is_end)
    def _():
        for index in range(1, chips):
            line_copy(chip, jnp.where(chip == 0, index, chips - 1 - index)).start()

    if chips > 2:
        @pl.when(jnp.logical_not(is_end))
        def _():
            line_copy(chip, chip + 1).start()
            line_copy(chip, chip - 1).start()

    mate_copy(chip, core).start()
    for index in range(min(groups, 2)):
        weight_copy(index).start()

    tile = max([size for size in range(16, 801, 16) if vocab % size == 0], default=vocab)

    def product(index, fresh):
        first = origin_of(chips, chip, index) * 2 if joined == 2 else 0
        lanes = pl.ds(pl.multiple_of(first * features, 128), span)

        def rows_step(number, carry):
            rows = pl.ds(pl.multiple_of(number * tile, 8), tile)
            value = jnp.dot(weight[rows, lanes], tokens_ref[lanes, :], preferred_element_type=jnp.float32)
            logits[rows, :] = value if fresh else logits[rows, :] + value
            return carry

        lax.fori_loop(0, vocab // tile, rows_step, 0)

    def arrive(index):
        origin = origin_of(chips, chip, index)
        line_copy(origin, chip).wait_recv()
        onward, wanted = onward_of(chips, chip, origin)

        @pl.when(wanted)
        def _():
            line_copy(origin, jnp.clip(onward, 0, chips - 1)).start()

        mate_copy(origin, core).start()
        if index + 1 < groups:
            weight_copy(index + 1).start()

    def consume(index):
        mate_copy(origin_of(chips, chip, index), 1 - core).wait_recv()
        if joined == 2:
            weight_copy(index).wait()
            product(index, index == 0)
        elif index == chips - 1:
            weight_copy(0).wait()
            product(0, True)

    for index in range(1, chips):
        arrive(index)
        if index == 1:
            consume(0)
        consume(index)
    if chips == 1:
        consume(0)

    labels = labels_ref[:, my_tokens]
    step_rows = max(size for size in range(8, 201, 8) if vocab % size == 0)

    def sum_step(number, carry):
        total, picked = carry
        rows = pl.ds(pl.multiple_of(number * step_rows, 8), step_rows)
        value = logits[rows, :]
        entries = lax.broadcasted_iota(jnp.int32, value.shape, 0) + (me * vocab + number * step_rows)
        exponent = jnp.exp(value)
        logits[rows, :] = exponent
        chosen = jnp.where(entries == labels, value, jnp.zeros_like(value))
        shape = (step_rows // 8, 8, share)
        return total + jnp.sum(exponent.reshape(shape), axis=0), picked + jnp.sum(chosen.reshape(shape), axis=0)

    zeros = jnp.zeros((8, share), jnp.float32)
    total, picked = lax.fori_loop(0, vocab // step_rows, sum_step, (zeros, zeros))
    own_sums[...] = jnp.concatenate(
        [
            jnp.broadcast_to(jnp.sum(total, axis=0, keepdims=True), (4, share)),
            jnp.broadcast_to(jnp.sum(picked, axis=0, keepdims=True), (4, share)),
        ],
        axis=0,
    )

    def sum_copy(source, other):
        return remote(own_sums, sums.at[source], send_sum.at[other], recv_sum.at[source], other)

    for other in others:
        sum_copy(me, other).start()
    sums[me] = own_sums[...]
    for other in others:
        sum_copy(other, other).wait_recv()
    both = jnp.sum(sums[...], axis=0)
    denominator, picked = both[:1, :], both[4:5, :]
    losses = jnp.sum(jnp.log(denominator) - picked, axis=1, keepdims=True)
    loss_ref[...] = jnp.broadcast_to(losses, loss_ref.shape)

    def slope_of(start, size):
        value = logits[pl.ds(pl.multiple_of(start, 8), size), :]
        entries = lax.broadcasted_iota(jnp.int32, value.shape, 0) + (me * vocab + start)
        hit = (entries == labels).astype(jnp.float32)
        return ((value / denominator - hit) / all_rows).astype(slopes.dtype).T

    def slope_step(number, carry):
        start = pl.multiple_of(number * 128, 128)
        slopes[:, pl.ds(start, 128)] = slope_of(start, 128)
        return carry

    lax.fori_loop(0, vocab // 128, slope_step, 0)
    if vocab % 128:
        start = vocab // 128 * 128
        slopes[:, start:] = slope_of(start, vocab - start)

    depth = share // per // pack

    def packed(value):
        rows = []
        for index in range(per):
            base = index * pack * depth
            rows.append(
                jnp.concatenate(
                    [value[base + part * depth : base + (part + 1) * depth] for part in range(pack)], axis=1
                )
            )
        return jnp.concatenate(rows, axis=0) if per > 1 else rows[0]

    def near_copy(there):
        return remote(near_out.at[there], near.at[there], send_near.at[there], recv_near.at[there], mate)

    def far_copy(source, there):
        return remote(far_out.at[there], far.at[source], send_far.at[there], recv_far.at[source], there * 2 + core)

    def split(there):
        if joined == 2:
            lanes = pl.ds(pl.multiple_of(there * span, 128), span)
            value = jnp.dot(slopes[...], weight[:, lanes], preferred_element_type=jnp.float32)
            left, right = value[:, :features], value[:, features:]
        else:
            value = jnp.dot(slopes[...], weight[...], preferred_element_type=jnp.float32)
            left = jnp.zeros((share, features), jnp.float32)
            right = left
            for index in range(chips):
                base = index * 2 * features
                left = jnp.where(there == index, value[:, base : base + features], left)
                right = jnp.where(there == index, value[:, base + features : base + 2 * features], right)
        first = core == 0
        return jnp.where(first, left, right), jnp.where(first, right, left)

    relayed = chips == 4
    low = chip < 2
    neighbour = jnp.where(low, 1 - chip, 5 - chip)
    across = 3 - chip

    def target_of(index):
        if not relayed:
            return lax.rem(chip + 1 + index, chips)
        end_order = jnp.where(low, 3 - index, index)
        far_end = jnp.where(low, 4 - index, index - 1)
        middle_order = jnp.where(index == 0, neighbour, jnp.where(index == 3, chip, far_end))
        return jnp.where(is_end, end_order, middle_order)

    def relay_copy(index):
        there = target_of(index)
        return remote(
            far_out.at[there], relay.at[index], send_far.at[there], recv_relay.at[index], neighbour * 2 + core
        )

    def pair_sum(index):
        there = target_of(index)
        near_copy(there).wait_recv()
        return mine[lax.rem(index, 2)] + near[there].astype(jnp.float32)

    def scatter_step(index, carry):
        there = target_of(index)
        kept, given = split(there)
        mine[lax.rem(index, 2)] = packed(kept)
        near_out[there] = packed(given).astype(near_out.dtype)
        near_copy(there).start()

        @pl.when(index > 0)
        def _():
            before = target_of(index - 1)
            if not relayed:
                far_out[before] = pair_sum(index - 1).astype(far_out.dtype)
                far_copy(chip, before).start()
            else:
                total = pair_sum(index - 1)
                slot = jnp.clip(index - 2, 0, 1)

                @pl.when(is_end | (index == 1))
                def _():
                    far_out[before] = total.astype(far_out.dtype)

                @pl.when(jnp.logical_not(is_end) & (index > 1))
                def _():
                    relay_copy(slot).wait_recv()
                    far_out[before] = (total + relay[slot].astype(jnp.float32)).astype(far_out.dtype)

                @pl.when(is_end & (index < 3))
                def _():
                    relay_copy(jnp.minimum(index - 1, 1)).start()

                @pl.when(jnp.logical_not(is_end) | (index == 3))
                def _():
                    far_copy(chip, before).start()

        return carry

    lax.fori_loop(0, chips, scatter_step, 0)
    result = pair_sum(chips - 1)
    chips_out = [lax.rem(chip + step, chips) for step in range(1, chips)]
    sources = chips_out
    if relayed:
        sources = [jnp.where(is_end, 1, neighbour), jnp.where(is_end, 2, across)]
    for there in sources:
        far_copy(there, there).wait_recv()
        result = result + far[there].astype(jnp.float32)
    part_ref[...] = result.astype(part_ref.dtype)

    @pl.when(is_end)
    def _():
        for index in range(1, chips):
            line_copy(chip, jnp.where(chip == 0, index, chips - 1 - index)).wait_send()

    if chips > 2:
        @pl.when(jnp.logical_not(is_end))
        def _():
            line_copy(chip, chip + 1).wait_send()
            line_copy(chip, chip - 1).wait_send()

    mate_copy(chip, core).wait_send()
    for index in range(1, chips):
        origin = origin_of(chips, chip, index)
        onward, wanted = onward_of(chips, chip, origin)

        @pl.when(wanted)
        def _():
            line_copy(origin, jnp.clip(onward, 0, chips - 1)).wait_send()

        mate_copy(origin, core).wait_send()
    for other in others:
        sum_copy(me, other).wait_send()
    for there in chips_out + [chip]:
        near_copy(there).wait_send()
    if not relayed:
        for there in chips_out:
            far_copy(chip, there).wait_send()
    else:
        @pl.when(is_end)
        def _():
            relay_copy(0).wait_send()
            relay_copy(1).wait_send()
            far_copy(chip, neighbour).wait_send()

        @pl.when(jnp.logical_not(is_end))
        def _():
            for index in range(3):
                far_copy(chip, target_of(index)).wait_send()


def head(hidden, labels, head_weight, pack, per):
    sections, tensors = lax.axis_size("section"), lax.axis_size("tensor")
    chips = tensors // 2
    features, tokens = hidden.shape
    vocab, width = head_weight.shape
    share = tokens // sections
    groups = chips if (2 * features) % 128 == 0 else 1
    dma = pltpu.SemaphoreType.DMA
    vmem = pl.BlockSpec(memory_space=pltpu.VMEM)
    hbm = pl.BlockSpec(memory_space=pl.ANY)
    dense = (share // pack, pack * features)
    held = pltpu.VMEM((chips,) + dense, jnp.bfloat16)
    return pl.pallas_call(
        functools.partial(head_kernel, tensors, pack, per),
        out_shape=(
            jax.ShapeDtypeStruct(dense, jnp.bfloat16),
            jax.ShapeDtypeStruct((8, 128), jnp.float32),
        ),
        in_specs=[hbm, vmem, hbm],
        out_specs=(vmem, vmem),
        scratch_shapes=[
            pltpu.VMEM((vocab, width), jnp.bfloat16),
            pltpu.VMEM((width, share), jnp.bfloat16),
            pltpu.VMEM((vocab, share), jnp.float32),
            pltpu.VMEM((share, vocab), jnp.bfloat16),
            pltpu.VMEM((2,) + dense, jnp.float32),
            held, held, held, held,
            pltpu.VMEM((2,) + dense, jnp.bfloat16),
            pltpu.VMEM((8, share), jnp.float32),
            pltpu.VMEM((tensors, 8, share), jnp.float32),
            dma((groups,)),
            dma((2 * chips,)),
            dma((chips,)),
            dma((chips,)),
            dma((chips,)),
            dma((tensors,)),
            dma((tensors,)),
            dma((chips,)),
            dma((chips,)),
            dma((chips,)),
            dma((chips,)),
            dma((2,)),
            dma((1,)),
        ],
        compiler_params=pltpu.CompilerParams(
            collective_id=1, has_side_effects=True, vmem_limit_bytes=67_000_000
        ),
    )(hidden, labels, head_weight)


def step_kernel(
    sections, tensors, count, pack, part_ref, loss_ref, x_ref, row_ref, col_ref, w_ref,
    out_ref, grad_out, total_ref, row_out, row_scale, col_out, col_scale,
    flipped, stage, held, carried, grad, acc_ref, row_acc, row_full, loss_buf, vectors, near, pair_sum, spread, final,
    send_x, recv_x, send_z, recv_z, send_mate, recv_mate, send_loss, recv_loss, local_sem, head_sem,
    send_sum, recv_sum, send_far, recv_far, stage_sem,
):
    section = lax.axis_index("section")
    me = lax.axis_index("tensor")
    chips = tensors // 2
    chip, core = me // 2, me % 2
    mate = chip * 2 + 1 - core
    last = sections - 1
    tokens, width = carried.shape
    features = acc_ref.shape[1]
    size = tokens // count
    per = count // sections
    depth = size // pack
    group = vectors.shape[2]
    used = width // group
    joined = 2 if (2 * features) % 128 == 0 else tensors
    span = joined * features

    def rem(a, b):
        return lax.rem(a, b)

    def share_of(step):
        return (last - step // per) * per + rem(step, per)

    def rows_of(step):
        return pl.ds(pl.multiple_of(share_of(step) * size, size), size)

    def packed_of(step):
        return pl.ds(pl.multiple_of(share_of(step) * depth, depth), depth)

    def remote(src, dst, send, recv, device):
        return pltpu.make_async_remote_copy(
            src_ref=src, dst_ref=dst, send_sem=send, recv_sem=recv, device_id=device, device_id_type=MESH
        )

    def block(device, step):
        return held.at[device, packed_of(step), :]

    def line_copy(step, origin, there):
        where = block(origin * 2 + core, step)
        slot = jnp.where(origin == chip, 0, chips) + there
        return remote(where, where, send_z.at[step, slot], recv_z.at[step, origin], {"tensor": there * 2 + core})

    def mate_copy(step, origin, side):
        where = block(origin * 2 + side, step)
        return remote(where, where, send_mate.at[step, origin], recv_mate.at[step, origin], {"tensor": mate})

    def down_copy(step):
        below = jnp.maximum(section - 1, 0)
        return remote(
            out_ref.at[packed_of(step), :], block(me, step), send_x.at[step], recv_x.at[step], {"section": below}
        )

    def head_copy(index):
        step = (last - section) * per + index
        return remote(
            part_ref.at[pl.ds(index * depth, depth), :], block(me, step),
            head_sem.at[index], recv_x.at[step], {"section": last},
        )

    def own_copy(index):
        return pltpu.make_async_copy(
            part_ref.at[pl.ds(index * depth, depth), :], block(me, index), local_sem.at[index]
        )

    def weight_copy(index):
        lanes = pl.ds(pl.multiple_of(index * span, 128), span)
        slot = rem(index, 2)
        return pltpu.make_async_copy(w_ref.at[:, lanes], stage.at[slot], local_sem.at[per + slot])

    def loss_copy(source, there):
        return remote(
            loss_ref, loss_buf.at[source], send_loss.at[there], recv_loss.at[source], {"section": there}
        )

    barrier = pltpu.get_barrier_semaphore()
    greeted = [{"tensor": mate}]
    greeted += [{"tensor": rem(chip + step, chips) * 2 + core} for step in range(1, chips)]
    greeted += [{"section": rem(section + step, sections)} for step in range(1, sections)]
    groups = tensors // joined
    for device in greeted:
        pl.semaphore_signal(barrier, inc=1, device_id=device, device_id_type=MESH)
    pl.semaphore_wait(barrier, len(greeted))

    @pl.when(section == last)
    def _():
        for index in range(per):
            own_copy(index).start()

    @pl.when(section != last)
    def _():
        for index in range(per):
            head_copy(index).start()

    for step in range(1, sections):
        loss_copy(section, rem(section + step, sections)).start()

    is_end = (chip == 0) | (chip == chips - 1)
    ahead = 2

    def launch(step):
        @pl.when((section == last) & (step < per))
        def _():
            own_copy(jnp.minimum(step, per - 1)).wait()

        @pl.when((section != last) | (step >= per))
        def _():
            down_copy(step).wait_recv()

        @pl.when(is_end)
        def _():
            for index in range(1, chips):
                line_copy(step, chip, jnp.where(chip == 0, index, chips - 1 - index)).start()

        if chips > 2:
            @pl.when(jnp.logical_not(is_end))
            def _():
                line_copy(step, chip, chip + 1).start()
                line_copy(step, chip, chip - 1).start()

        mate_copy(step, chip, core).start()

    def assemble(step, first):
        for part in range(pack):
            pieces = []
            for offset in range(joined):
                piece = held[first + offset, packed_of(step), :]
                pieces.append(piece[:, part * features : (part + 1) * features])
            rows = pl.ds(pl.multiple_of(share_of(step) * size + part * depth, depth), depth)
            lanes = pl.ds(pl.multiple_of(first * features, 128), span)
            carried[rows, lanes] = jnp.concatenate(pieces, axis=1)

    def product(step, first, fresh):
        lanes = pl.ds(pl.multiple_of(first * features, 128), span)
        value = jnp.dot(carried[rows_of(step), lanes], flipped[lanes, :], preferred_element_type=jnp.float32)
        acc_ref[...] = value if fresh else acc_ref[...] + value

    def finish(step, index):
        origin = origin_of(chips, chip, index)
        mate_copy(step, origin, 1 - core).wait_recv()
        if joined == 2:
            assemble(step, origin * 2)
            product(step, origin * 2, index == 0)
        elif index == chips - 1:
            assemble(step, 0)
            product(step, 0, True)

    @pl.when(section == last)
    def _():
        for index in range(ahead):
            launch(index)

    for index in range(min(groups, 2)):
        weight_copy(index).start()
    vectors[...] = jnp.zeros_like(vectors)

    def flip(index, inner):
        slot = rem(index, 2)
        weight_copy(index).wait()
        lanes = pl.ds(pl.multiple_of(index * span, 128), span)
        flipped[lanes, :] = stage[slot].T
        for start in range(0, features, 16):
            entries = stage[slot, start : start + 16, :].astype(jnp.float32)
            inner = inner + jnp.sum(jnp.reshape(entries * entries, (2, 8, span)), axis=0)

        @pl.when(index + 2 < groups)
        def _():
            weight_copy(index + 2).start()

        return inner

    squares = lax.fori_loop(0, groups, flip, jnp.zeros((8, span), jnp.float32))
    vectors[1, pl.ds(used + 1, 1), :] = jnp.broadcast_to(jnp.sum(squares, keepdims=True), (1, group))

    @pl.when(section != last)
    def _():
        for index in range(ahead):
            launch(index)

    half = count // 2
    low = tokens // 2
    pieces = 4 if half % 4 == 0 and width % 512 == 0 else 1
    stride = half // pieces
    cut = width // pieces

    def advance(step, carry):
        for index in range(1, chips):
            if index == min(2, chips - 1):
                @pl.when(step + ahead < count)
                def _():
                    launch(jnp.minimum(step + ahead, count - 1))

            origin = origin_of(chips, chip, index)
            line_copy(step, origin, chip).wait_recv()
            onward, wanted = onward_of(chips, chip, origin)

            @pl.when(wanted)
            def _():
                line_copy(step, origin, jnp.clip(onward, 0, chips - 1)).start()

            mate_copy(step, origin, core).start()
            finish(step, index - 1)
        finish(step, chips - 1)
        sums = jnp.concatenate([acc_ref[part * depth : (part + 1) * depth, :] for part in range(pack)], axis=1)
        mine = held[me, packed_of(step), :].astype(jnp.float32)
        out_ref[packed_of(step), :] = (mine + sums).astype(out_ref.dtype)

        @pl.when(section > 0)
        def _():
            down_copy(step).start()

        @pl.when((step >= half) & (rem(step, stride) == 0))
        def _():
            lanes = pl.ds(pl.multiple_of((step - half) // stride * cut, 128), cut)
            grad[:, lanes] = jnp.dot(
                x_ref[:, low:], carried[low:, lanes], preferred_element_type=jnp.float32
            )

        return carry

    lax.fori_loop(0, count, advance, 0)

    row_acc[...] = jnp.zeros_like(row_acc)

    def stage_copy(index):
        lanes = pl.ds(pl.multiple_of(index * group, 128), group)
        slot = rem(index, 2)
        return pltpu.make_async_copy(stage.at[slot, :, pl.ds(0, group)], grad_out.at[:, lanes], stage_sem.at[slot])

    def gather_squares(index, carry):
        lanes = pl.ds(pl.multiple_of(index * group, 128), group)
        value = grad[:, lanes] + jnp.dot(
            x_ref[:, :low], carried[:low, lanes], preferred_element_type=jnp.float32
        )
        grad[:, lanes] = value

        @pl.when(index > 1)
        def _():
            stage_copy(index - 2).wait()

        slot = rem(index, 2)
        inner = jnp.zeros((8, group), jnp.float32)
        for start in range(0, features, 16):
            entries = grad[start : start + 16, lanes]
            stage[slot, start : start + 16, :group] = entries.astype(stage.dtype)
            squares = entries * entries + tiny_term
            folded = squares[:, :128]
            for lane in range(128, group, 128):
                folded = folded + squares[:, lane : lane + 128]
            row_acc[start : start + 16, :] = row_acc[start : start + 16, :] + folded
            inner = inner + jnp.sum(jnp.reshape(squares, (2, 8, group)), axis=0)
        vectors[0, pl.ds(index, 1), :] = jnp.sum(inner, axis=0, keepdims=True)
        stage_copy(index).start()
        return carry

    lax.fori_loop(0, used, gather_squares, 0)
    sums = jnp.sum(row_acc[...], axis=1, keepdims=True)
    old_row = jnp.broadcast_to(row_ref[...], (128, features)).T[:, :1]
    fresh_row = decay_rate * old_row + (1.0 - decay_rate) * (sums / width)
    row_out[...] = fresh_row
    vectors[1, pl.ds(used, 1), :] = jnp.broadcast_to(jnp.sum(fresh_row, keepdims=True), (1, group))
    row_full[...] = jnp.broadcast_to(1.0 / fresh_row, row_full.shape)

    def gather_scaled(index, carry):
        lanes = pl.ds(pl.multiple_of(index * group, 128), group)
        inner = jnp.zeros((8, group), jnp.float32)
        for start in range(0, features, 16):
            entries = grad[start : start + 16, lanes]
            shrink = jnp.concatenate([row_full[start : start + 16, :]] * (group // 128), axis=1)
            inner = inner + jnp.sum(jnp.reshape(entries * entries * shrink, (2, 8, group)), axis=0)
        vectors[1, pl.ds(index, 1), :] = jnp.sum(inner, axis=0, keepdims=True)
        return carry

    lax.fori_loop(0, used, gather_scaled, 0)

    def mate_sum():
        return remote(vectors.at[1 - core], near, send_sum.at[0], recv_sum.at[0], {"tensor": mate})

    def far_sum(source, there):
        return remote(
            pair_sum, spread.at[source], send_far.at[there], recv_far.at[source], {"tensor": there * 2 + core}
        )

    def mate_total(side):
        return remote(final.at[side], final.at[side], send_sum.at[1], recv_sum.at[1], {"tensor": mate})

    others = [rem(chip + step, chips) for step in range(1, chips)]
    mate_sum().start()
    mate_sum().wait_recv()
    pair_sum[...] = vectors[core] + near[...]
    for there in others:
        far_sum(chip, there).start()
    spread[chip] = pair_sum[...]
    for there in others:
        far_sum(there, there).wait_recv()
    final[core] = jnp.sum(spread[...], axis=0)
    mate_total(core).start()

    total = None
    for step in range(1, sections):
        other = rem(section + step, sections)
        loss_copy(other, other).wait_recv()
    loss_buf[section] = loss_ref[...]
    total_ref[...] = jnp.sum(loss_buf[...], axis=0)

    mate_total(1 - core).wait_recv()

    entries = float(width * width)
    row_total = final[1, used : used + 1, :][:, :1]
    weight_total = final[1, used + 1 : used + 2, :][:, :1]

    def update_columns(index, inner):
        lanes = pl.ds(pl.multiple_of(index * group, 128), group)
        fresh = decay_rate * col_ref[:, lanes] + (1.0 - decay_rate) * (final[0, pl.ds(index, 1), :] / width)
        col_out[:, lanes] = fresh
        col_scale[:, lanes] = lax.rsqrt(fresh)
        return inner + final[1, pl.ds(index, 1), :] / fresh

    scaled = lax.fori_loop(0, used, update_columns, jnp.zeros((1, group), jnp.float32))
    update_total = row_total * jnp.sum(scaled, axis=1, keepdims=True)
    factor = (
        learn_rate * jnp.sqrt(weight_total / entries)
        / jnp.maximum(1.0, jnp.sqrt(update_total / entries))
    )
    row_scale[...] = lax.rsqrt(row_out[...]) * (factor * jnp.sqrt(row_total))
    for index in (used - 2, used - 1):
        stage_copy(index).wait()

    def drain(step, carry):
        @pl.when(section > 0)
        def _():
            down_copy(step).wait_send()

        @pl.when(is_end)
        def _():
            for index in range(1, chips):
                line_copy(step, chip, jnp.where(chip == 0, index, chips - 1 - index)).wait_send()

        if chips > 2:
            @pl.when(jnp.logical_not(is_end))
            def _():
                line_copy(step, chip, chip + 1).wait_send()
                line_copy(step, chip, chip - 1).wait_send()

        mate_copy(step, chip, core).wait_send()
        for index in range(1, chips):
            origin = origin_of(chips, chip, index)
            onward, wanted = onward_of(chips, chip, origin)

            @pl.when(wanted)
            def _():
                line_copy(step, origin, jnp.clip(onward, 0, chips - 1)).wait_send()

            mate_copy(step, origin, core).wait_send()
        return carry

    lax.fori_loop(0, count, drain, 0)
    for step in range(1, sections):
        loss_copy(section, rem(section + step, sections)).wait_send()

    @pl.when(section != last)
    def _():
        for index in range(per):
            head_copy(index).wait_send()

    mate_sum().wait_send()
    for there in others:
        far_sum(chip, there).wait_send()
    mate_total(core).wait_send()


def update_kernel(
    pack, size, scale_ref, col_ref, carried_ref, row_ref, col_in, total_ref, weight_ref, grad_ref,
    weight_out, carried_out, row_out, col_out, loss_out, entries_buf, grad_buf, weight_sem, grad_sem, out_sem,
):
    count, rows, width = entries_buf.shape
    group = 512 if width % 512 == 0 else 128
    features, tokens = carried_out.shape

    def rows_of(index):
        return pl.ds(pl.multiple_of(index * rows, 16), rows)

    def weight_copy(index):
        return pltpu.make_async_copy(weight_ref.at[rows_of(index), :], entries_buf.at[index], weight_sem.at[index])

    def grad_copy(index):
        return pltpu.make_async_copy(grad_ref.at[rows_of(index), :], grad_buf.at[index], grad_sem.at[index])

    def out_copy(index):
        return pltpu.make_async_copy(entries_buf.at[index], weight_out.at[rows_of(index), :], out_sem.at[index])

    def fetch(index, carry):
        weight_copy(index).start()
        grad_copy(index).start()
        return carry

    lax.fori_loop(0, count, fetch, 0)
    depth = size // pack
    for start in range(0, tokens, 128):
        pieces = []
        for share in range(start // size, (start + 128) // size):
            entries = carried_ref[share * depth : (share + 1) * depth, :].astype(jnp.float32)
            pieces += [entries[:, part * features : (part + 1) * features] for part in range(pack)]
        joined = jnp.concatenate(pieces, axis=0)
        carried_out[:, start : start + 128] = joined.T.astype(carried_out.dtype)
    row_out[...] = jnp.broadcast_to(row_ref[...], (features, 128)).T[:1, :]
    col_out[...] = col_in[...]
    loss_out[...] = total_ref[:1, :1] / tokens

    def change(index, carry):
        weight_copy(index).wait()
        grad_copy(index).wait()
        scales = scale_ref[rows_of(index), :]
        for start in range(0, rows, 16):
            scale = jnp.broadcast_to(scales[start : start + 16, :], (16, group))
            for lane in range(0, width, group):
                lanes = slice(lane, lane + group)
                moved = grad_buf[index, start : start + 16, lanes].astype(jnp.float32)
                moved = moved * (scale * col_ref[:, lanes])
                entries = entries_buf[index, start : start + 16, lanes].astype(jnp.float32)
                entries_buf[index, start : start + 16, lanes] = (entries - moved).astype(entries_buf.dtype)
        out_copy(index).start()
        return carry

    lax.fori_loop(0, count, change, 0)

    def finish(index, carry):
        out_copy(index).wait()
        return carry

    lax.fori_loop(0, count, finish, 0)


def update(pack, size, tokens, weight, grad, row_scale, col_scale, outputs, row_new, col_new, total):
    features, width = weight.shape
    rows = max(size for size in range(16, 65, 16) if features % size == 0)
    count = features // rows
    vmem = pl.BlockSpec(memory_space=pltpu.VMEM)
    hbm = pl.BlockSpec(memory_space=pl.ANY)
    dma = pltpu.SemaphoreType.DMA((count,))
    held = pltpu.VMEM((count, rows, width), jnp.bfloat16)
    return pl.pallas_call(
        functools.partial(update_kernel, pack, size),
        out_shape=(
            jax.ShapeDtypeStruct((features, width), jnp.bfloat16),
            jax.ShapeDtypeStruct((features, tokens), jnp.bfloat16),
            jax.ShapeDtypeStruct((1, features), jnp.float32),
            jax.ShapeDtypeStruct((1, width), jnp.float32),
            jax.ShapeDtypeStruct((1, 1), jnp.float32),
        ),
        in_specs=[vmem] * 6 + [hbm] * 2,
        out_specs=(hbm,) + (vmem,) * 4,
        scratch_shapes=[held, held, dma, dma, dma],
        compiler_params=pltpu.CompilerParams(vmem_limit_bytes=60 * 1024 * 1024),
    )(row_scale, col_scale, outputs, row_new, col_new, total, weight, grad)


def step(part, losses, saved, local_weight, row_state, col_state, pack, count):
    sections, tensors = lax.axis_size("section"), lax.axis_size("tensor")
    features, tokens = saved.shape
    width = features * tensors
    chips = tensors // 2
    size = tokens // count
    group = 512 if width % 512 == 0 else 128
    span = 2 * features if (2 * features) % 128 == 0 else width
    lines = -(-(width // group + 2) // 8) * 8
    dma = pltpu.SemaphoreType.DMA
    vmem = pl.BlockSpec(memory_space=pltpu.VMEM)
    hbm = pl.BlockSpec(memory_space=pl.ANY)
    single = pltpu.VMEM((lines, group), jnp.float32)
    outputs, grad, total, row_new, row_scale, col_new, col_scale = pl.pallas_call(
        functools.partial(step_kernel, sections, tensors, count, pack),
        out_shape=(
            jax.ShapeDtypeStruct((tokens // pack, pack * features), jnp.bfloat16),
            jax.ShapeDtypeStruct((features, width), jnp.bfloat16),
            jax.ShapeDtypeStruct((8, 128), jnp.float32),
            jax.ShapeDtypeStruct((features, 1), jnp.float32),
            jax.ShapeDtypeStruct((features, 1), jnp.float32),
            jax.ShapeDtypeStruct((1, width), jnp.float32),
            jax.ShapeDtypeStruct((1, width), jnp.float32),
        ),
        in_specs=[vmem] * 5 + [hbm],
        out_specs=(vmem, hbm) + (vmem,) * 5,
        scratch_shapes=[
            pltpu.VMEM((width, features), jnp.bfloat16),
            pltpu.VMEM((2, features, span), jnp.bfloat16),
            pltpu.VMEM((tensors, tokens // pack, pack * features), jnp.bfloat16),
            pltpu.VMEM((tokens, width), jnp.bfloat16),
            pltpu.VMEM((features, width), jnp.float32),
            pltpu.VMEM((size, features), jnp.float32),
            pltpu.VMEM((features, 128), jnp.float32),
            pltpu.VMEM((features, 128), jnp.float32),
            pltpu.VMEM((sections, 8, 128), jnp.float32),
            pltpu.VMEM((2, lines, group), jnp.float32),
            single,
            single,
            pltpu.VMEM((chips, lines, group), jnp.float32),
            pltpu.VMEM((2, lines, group), jnp.float32),
            dma((count,)),
            dma((count,)),
            dma((count, 2 * chips)),
            dma((count, chips)),
            dma((count, chips)),
            dma((count, chips)),
            dma((sections,)),
            dma((sections,)),
            dma((count // sections + 2,)),
            dma((count // sections,)),
            dma((2,)),
            dma((2,)),
            dma((chips,)),
            dma((chips,)),
            dma((2,)),
        ],
        compiler_params=pltpu.CompilerParams(
            collective_id=0, has_side_effects=True, vmem_limit_bytes=66_000_000
        ),
    )(part, losses, saved, row_state, col_state, local_weight)
    return update(pack, size, tokens, local_weight, grad, row_scale, col_scale, outputs, row_new, col_new, total)


def body(hidden_last, labels, head_weight, layer_inputs, weights, row_state, col_state):
    sections, tensors = lax.axis_size("section"), lax.axis_size("tensor")
    tokens, features = hidden_last.shape
    count = 4 * sections
    size = tokens // count
    pack = 2 if (2 * features) % 128 == 0 and (size // 2) % 16 == 0 else 1
    part, losses = head(hidden_last.T, labels.reshape(1, -1), head_weight.T, pack, count // sections)
    new_weight, outputs, row_new, col_new, loss = step(
        part, losses, layer_inputs[0].T, weights[0], row_state, col_state, pack, count
    )
    return (loss[0, 0], outputs.T[None], new_weight[None], row_new, col_new)


def solution(mesh):
    return jax.shard_map(
        body,
        mesh=mesh,
        in_specs=(
            P(None, "tensor"),
            P(),
            P(None, "tensor"),
            P("section", None, "tensor"),
            P("section", "tensor", None),
            P("section", "tensor"),
            P("section", None),
        ),
        out_specs=(
            P(),
            P("section", None, "tensor"),
            P("section", "tensor", None),
            P("section", "tensor"),
            P("section", None),
        ),
        check_vma=False,
    )
```

```python
import functools

import jax
import jax.numpy as jnp
from jax import lax
from jax.experimental import pallas as pl
from jax.experimental.pallas import tpu as pltpu
from jax.sharding import PartitionSpec as P

decay_rate = 0.9
learn_rate = 0.3
tiny_term = 1e-30


MESH = pl.DeviceIdType.MESH


def origin_of(chips, chip, index):
    if index == 0:
        return chip
    near_side = jnp.where(chip * 2 < chips, -1, 1)
    both = jnp.minimum(chip, chips - 1 - chip)
    paired = index <= 2 * both
    distance = jnp.where(paired, (index + 1) // 2, index - both)
    toward_near = paired & (index % 2 == 0)
    return chip + jnp.where(toward_near, near_side, -near_side) * distance


def onward_of(chips, chip, origin):
    onward = jnp.where(origin < chip, chip + 1, chip - 1)
    inner = (origin > 0) & (origin < chips - 1)
    return onward, inner & (onward >= 0) & (onward < chips)


def head_kernel(
    tensors, pack, per, hidden_ref, labels_ref, w_ref, part_ref, loss_ref,
    weight, tokens_ref, logits, slopes, mine, near_out, near, far_out, far, relay, own_sums, sums,
    weight_sem, send_line, recv_line, send_mate, recv_mate, send_sum, recv_sum,
    send_near, recv_near, send_far, recv_far, recv_relay, local_sem,
):
    section = lax.axis_index("section")
    me = lax.axis_index("tensor")
    chips = tensors // 2
    chip, core = me // 2, me % 2
    mate = chip * 2 + 1 - core
    vocab, width = weight.shape
    features = width // tensors
    share = tokens_ref.shape[1]
    all_rows = labels_ref.shape[1]
    joined = 2 if (2 * features) % 128 == 0 else tensors
    groups = tensors // joined
    span = joined * features
    is_end = (chip == 0) | (chip == chips - 1)
    my_tokens = pl.ds(pl.multiple_of(section * share, 128), share)

    def remote(src, dst, send, recv, device):
        return pltpu.make_async_remote_copy(
            src_ref=src, dst_ref=dst, send_sem=send, recv_sem=recv,
            device_id={"tensor": device}, device_id_type=MESH,
        )

    def block(device):
        return tokens_ref.at[pl.ds(pl.multiple_of(device * features, 16), features), :]

    def line_copy(origin, there):
        where = block(origin * 2 + core)
        slot = jnp.where(origin == chip, 0, chips) + there
        return remote(where, where, send_line.at[slot], recv_line.at[origin], there * 2 + core)

    def mate_copy(origin, side):
        where = block(origin * 2 + side)
        return remote(where, where, send_mate.at[origin], recv_mate.at[origin], mate)

    def weight_copy(index):
        first = origin_of(chips, chip, index) * 2 if joined == 2 else 0
        lanes = pl.ds(pl.multiple_of(first * features, 128), span)
        return pltpu.make_async_copy(w_ref.at[:, lanes], weight.at[:, lanes], weight_sem.at[index])

    def own_copy():
        return pltpu.make_async_copy(hidden_ref.at[:, my_tokens], block(me), local_sem.at[0])

    own_copy().start()
    barrier = pltpu.get_barrier_semaphore()
    others = [lax.rem(me + step, tensors) for step in range(1, tensors)]
    for other in others:
        pl.semaphore_signal(barrier, inc=1, device_id={"tensor": other}, device_id_type=MESH)
    pl.semaphore_wait(barrier, tensors - 1)

    own_copy().wait()

    @pl.when(is_end)
    def _():
        for index in range(1, chips):
            line_copy(chip, jnp.where(chip == 0, index, chips - 1 - index)).start()

    if chips > 2:
        @pl.when(jnp.logical_not(is_end))
        def _():
            line_copy(chip, chip + 1).start()
            line_copy(chip, chip - 1).start()

    mate_copy(chip, core).start()
    for index in range(min(groups, 2)):
        weight_copy(index).start()

    tile = max([size for size in range(16, 801, 16) if vocab % size == 0], default=vocab)

    def product(index, fresh):
        first = origin_of(chips, chip, index) * 2 if joined == 2 else 0
        lanes = pl.ds(pl.multiple_of(first * features, 128), span)

        def rows_step(number, carry):
            rows = pl.ds(pl.multiple_of(number * tile, 8), tile)
            value = jnp.dot(weight[rows, lanes], tokens_ref[lanes, :], preferred_element_type=jnp.float32)
            logits[rows, :] = value if fresh else logits[rows, :] + value
            return carry

        lax.fori_loop(0, vocab // tile, rows_step, 0)

    def arrive(index):
        origin = origin_of(chips, chip, index)
        line_copy(origin, chip).wait_recv()
        onward, wanted = onward_of(chips, chip, origin)

        @pl.when(wanted)
        def _():
            line_copy(origin, jnp.clip(onward, 0, chips - 1)).start()

        mate_copy(origin, core).start()
        if index + 1 < groups:
            weight_copy(index + 1).start()

    def consume(index):
        mate_copy(origin_of(chips, chip, index), 1 - core).wait_recv()
        if joined == 2:
            weight_copy(index).wait()
            product(index, index == 0)
        elif index == chips - 1:
            weight_copy(0).wait()
            product(0, True)

    for index in range(1, chips):
        arrive(index)
        if index == 1:
            consume(0)
        consume(index)
    if chips == 1:
        consume(0)

    labels = labels_ref[:, my_tokens]
    step_rows = max(size for size in range(8, 201, 8) if vocab % size == 0)

    def sum_step(number, carry):
        total, picked = carry
        rows = pl.ds(pl.multiple_of(number * step_rows, 8), step_rows)
        value = logits[rows, :]
        entries = lax.broadcasted_iota(jnp.int32, value.shape, 0) + (me * vocab + number * step_rows)
        exponent = jnp.exp(value)
        logits[rows, :] = exponent
        chosen = jnp.where(entries == labels, value, jnp.zeros_like(value))
        shape = (step_rows // 8, 8, share)
        return total + jnp.sum(exponent.reshape(shape), axis=0), picked + jnp.sum(chosen.reshape(shape), axis=0)

    zeros = jnp.zeros((8, share), jnp.float32)
    total, picked = lax.fori_loop(0, vocab // step_rows, sum_step, (zeros, zeros))
    own_sums[...] = jnp.concatenate(
        [
            jnp.broadcast_to(jnp.sum(total, axis=0, keepdims=True), (4, share)),
            jnp.broadcast_to(jnp.sum(picked, axis=0, keepdims=True), (4, share)),
        ],
        axis=0,
    )

    def sum_copy(source, other):
        return remote(own_sums, sums.at[source], send_sum.at[other], recv_sum.at[source], other)

    for other in others:
        sum_copy(me, other).start()
    sums[me] = own_sums[...]
    for other in others:
        sum_copy(other, other).wait_recv()
    both = jnp.sum(sums[...], axis=0)
    denominator, picked = both[:1, :], both[4:5, :]
    losses = jnp.sum(jnp.log(denominator) - picked, axis=1, keepdims=True)
    loss_ref[...] = jnp.broadcast_to(losses, loss_ref.shape)

    def slope_of(start, size):
        value = logits[pl.ds(pl.multiple_of(start, 8), size), :]
        entries = lax.broadcasted_iota(jnp.int32, value.shape, 0) + (me * vocab + start)
        hit = (entries == labels).astype(jnp.float32)
        return ((value / denominator - hit) / all_rows).astype(slopes.dtype).T

    def slope_step(number, carry):
        start = pl.multiple_of(number * 128, 128)
        slopes[:, pl.ds(start, 128)] = slope_of(start, 128)
        return carry

    lax.fori_loop(0, vocab // 128, slope_step, 0)
    if vocab % 128:
        start = vocab // 128 * 128
        slopes[:, start:] = slope_of(start, vocab - start)

    depth = share // per // pack

    def packed(value):
        rows = []
        for index in range(per):
            base = index * pack * depth
            rows.append(
                jnp.concatenate(
                    [value[base + part * depth : base + (part + 1) * depth] for part in range(pack)], axis=1
                )
            )
        return jnp.concatenate(rows, axis=0) if per > 1 else rows[0]

    def near_copy(there):
        return remote(near_out.at[there], near.at[there], send_near.at[there], recv_near.at[there], mate)

    def far_copy(source, there):
        return remote(far_out.at[there], far.at[source], send_far.at[there], recv_far.at[source], there * 2 + core)

    def split(there):
        if joined == 2:
            lanes = pl.ds(pl.multiple_of(there * span, 128), span)
            value = jnp.dot(slopes[...], weight[:, lanes], preferred_element_type=jnp.float32)
            left, right = value[:, :features], value[:, features:]
        else:
            value = jnp.dot(slopes[...], weight[...], preferred_element_type=jnp.float32)
            left = jnp.zeros((share, features), jnp.float32)
            right = left
            for index in range(chips):
                base = index * 2 * features
                left = jnp.where(there == index, value[:, base : base + features], left)
                right = jnp.where(there == index, value[:, base + features : base + 2 * features], right)
        first = core == 0
        return jnp.where(first, left, right), jnp.where(first, right, left)

    relayed = chips == 4
    low = chip < 2
    neighbour = jnp.where(low, 1 - chip, 5 - chip)
    across = 3 - chip

    def target_of(index):
        if not relayed:
            return lax.rem(chip + 1 + index, chips)
        end_order = jnp.where(low, 3 - index, index)
        far_end = jnp.where(low, 4 - index, index - 1)
        middle_order = jnp.where(index == 0, neighbour, jnp.where(index == 3, chip, far_end))
        return jnp.where(is_end, end_order, middle_order)

    def relay_copy(index):
        there = target_of(index)
        return remote(
            far_out.at[there], relay.at[index], send_far.at[there], recv_relay.at[index], neighbour * 2 + core
        )

    def pair_sum(index):
        there = target_of(index)
        near_copy(there).wait_recv()
        return mine[lax.rem(index, 2)] + near[there].astype(jnp.float32)

    def scatter_step(index, carry):
        there = target_of(index)
        kept, given = split(there)
        mine[lax.rem(index, 2)] = packed(kept)
        near_out[there] = packed(given).astype(near_out.dtype)
        near_copy(there).start()

        @pl.when(index > 0)
        def _():
            before = target_of(index - 1)
            if not relayed:
                far_out[before] = pair_sum(index - 1).astype(far_out.dtype)
                far_copy(chip, before).start()
            else:
                total = pair_sum(index - 1)
                slot = jnp.clip(index - 2, 0, 1)

                @pl.when(is_end | (index == 1))
                def _():
                    far_out[before] = total.astype(far_out.dtype)

                @pl.when(jnp.logical_not(is_end) & (index > 1))
                def _():
                    relay_copy(slot).wait_recv()
                    far_out[before] = (total + relay[slot].astype(jnp.float32)).astype(far_out.dtype)

                @pl.when(is_end & (index < 3))
                def _():
                    relay_copy(jnp.minimum(index - 1, 1)).start()

                @pl.when(jnp.logical_not(is_end) | (index == 3))
                def _():
                    far_copy(chip, before).start()

        return carry

    lax.fori_loop(0, chips, scatter_step, 0)
    result = pair_sum(chips - 1)
    chips_out = [lax.rem(chip + step, chips) for step in range(1, chips)]
    sources = chips_out
    if relayed:
        sources = [jnp.where(is_end, 1, neighbour), jnp.where(is_end, 2, across)]
    for there in sources:
        far_copy(there, there).wait_recv()
        result = result + far[there].astype(jnp.float32)
    part_ref[...] = result.astype(part_ref.dtype)

    @pl.when(is_end)
    def _():
        for index in range(1, chips):
            line_copy(chip, jnp.where(chip == 0, index, chips - 1 - index)).wait_send()

    if chips > 2:
        @pl.when(jnp.logical_not(is_end))
        def _():
            line_copy(chip, chip + 1).wait_send()
            line_copy(chip, chip - 1).wait_send()

    mate_copy(chip, core).wait_send()
    for index in range(1, chips):
        origin = origin_of(chips, chip, index)
        onward, wanted = onward_of(chips, chip, origin)

        @pl.when(wanted)
        def _():
            line_copy(origin, jnp.clip(onward, 0, chips - 1)).wait_send()

        mate_copy(origin, core).wait_send()
    for other in others:
        sum_copy(me, other).wait_send()
    for there in chips_out + [chip]:
        near_copy(there).wait_send()
    if not relayed:
        for there in chips_out:
            far_copy(chip, there).wait_send()
    else:
        @pl.when(is_end)
        def _():
            relay_copy(0).wait_send()
            relay_copy(1).wait_send()
            far_copy(chip, neighbour).wait_send()

        @pl.when(jnp.logical_not(is_end))
        def _():
            for index in range(3):
                far_copy(chip, target_of(index)).wait_send()


def head(hidden, labels, head_weight, pack, per):
    sections, tensors = lax.axis_size("section"), lax.axis_size("tensor")
    chips = tensors // 2
    features, tokens = hidden.shape
    vocab, width = head_weight.shape
    share = tokens // sections
    groups = chips if (2 * features) % 128 == 0 else 1
    dma = pltpu.SemaphoreType.DMA
    vmem = pl.BlockSpec(memory_space=pltpu.VMEM)
    hbm = pl.BlockSpec(memory_space=pl.ANY)
    dense = (share // pack, pack * features)
    held = pltpu.VMEM((chips,) + dense, jnp.bfloat16)
    return pl.pallas_call(
        functools.partial(head_kernel, tensors, pack, per),
        out_shape=(
            jax.ShapeDtypeStruct(dense, jnp.bfloat16),
            jax.ShapeDtypeStruct((8, 128), jnp.float32),
        ),
        in_specs=[hbm, vmem, hbm],
        out_specs=(vmem, vmem),
        scratch_shapes=[
            pltpu.VMEM((vocab, width), jnp.bfloat16),
            pltpu.VMEM((width, share), jnp.bfloat16),
            pltpu.VMEM((vocab, share), jnp.float32),
            pltpu.VMEM((share, vocab), jnp.bfloat16),
            pltpu.VMEM((2,) + dense, jnp.float32),
            held, held, held, held,
            pltpu.VMEM((2,) + dense, jnp.bfloat16),
            pltpu.VMEM((8, share), jnp.float32),
            pltpu.VMEM((tensors, 8, share), jnp.float32),
            dma((groups,)),
            dma((2 * chips,)),
            dma((chips,)),
            dma((chips,)),
            dma((chips,)),
            dma((tensors,)),
            dma((tensors,)),
            dma((chips,)),
            dma((chips,)),
            dma((chips,)),
            dma((chips,)),
            dma((2,)),
            dma((1,)),
        ],
        compiler_params=pltpu.CompilerParams(
            collective_id=1, has_side_effects=True, vmem_limit_bytes=67_000_000
        ),
    )(hidden, labels, head_weight)


def step_kernel(
    sections, tensors, count, pack, part_ref, loss_ref, x_ref, row_ref, col_ref, w_ref,
    out_ref, grad_out, total_ref, row_out, row_scale, col_out, col_scale,
    flipped, stage, held, carried, grad, acc_ref, row_acc, row_full, loss_buf, vectors, near, pair_sum, spread, final,
    send_x, recv_x, send_z, recv_z, send_mate, recv_mate, send_loss, recv_loss, local_sem, head_sem,
    send_sum, recv_sum, send_far, recv_far, stage_sem,
):
    section = lax.axis_index("section")
    me = lax.axis_index("tensor")
    chips = tensors // 2
    chip, core = me // 2, me % 2
    mate = chip * 2 + 1 - core
    last = sections - 1
    tokens, width = carried.shape
    features = acc_ref.shape[1]
    size = tokens // count
    per = count // sections
    depth = size // pack
    group = vectors.shape[2]
    used = width // group
    joined = 2 if (2 * features) % 128 == 0 else tensors
    span = joined * features

    def rem(a, b):
        return lax.rem(a, b)

    def share_of(step):
        return (last - step // per) * per + rem(step, per)

    def rows_of(step):
        return pl.ds(pl.multiple_of(share_of(step) * size, size), size)

    def packed_of(step):
        return pl.ds(pl.multiple_of(share_of(step) * depth, depth), depth)

    def remote(src, dst, send, recv, device):
        return pltpu.make_async_remote_copy(
            src_ref=src, dst_ref=dst, send_sem=send, recv_sem=recv, device_id=device, device_id_type=MESH
        )

    def block(device, step):
        return held.at[device, packed_of(step), :]

    def line_copy(step, origin, there):
        where = block(origin * 2 + core, step)
        slot = jnp.where(origin == chip, 0, chips) + there
        return remote(where, where, send_z.at[step, slot], recv_z.at[step, origin], {"tensor": there * 2 + core})

    def mate_copy(step, origin, side):
        where = block(origin * 2 + side, step)
        return remote(where, where, send_mate.at[step, origin], recv_mate.at[step, origin], {"tensor": mate})

    def down_copy(step):
        below = jnp.maximum(section - 1, 0)
        return remote(
            out_ref.at[packed_of(step), :], block(me, step), send_x.at[step], recv_x.at[step], {"section": below}
        )

    def head_copy(index):
        step = (last - section) * per + index
        return remote(
            part_ref.at[pl.ds(index * depth, depth), :], block(me, step),
            head_sem.at[index], recv_x.at[step], {"section": last},
        )

    def own_copy(index):
        return pltpu.make_async_copy(
            part_ref.at[pl.ds(index * depth, depth), :], block(me, index), local_sem.at[index]
        )

    def weight_copy(index):
        lanes = pl.ds(pl.multiple_of(index * span, 128), span)
        slot = rem(index, 2)
        return pltpu.make_async_copy(w_ref.at[:, lanes], stage.at[slot], local_sem.at[per + slot])

    def loss_copy(source, there):
        return remote(
            loss_ref, loss_buf.at[source], send_loss.at[there], recv_loss.at[source], {"section": there}
        )

    barrier = pltpu.get_barrier_semaphore()
    greeted = [{"tensor": mate}]
    greeted += [{"tensor": rem(chip + step, chips) * 2 + core} for step in range(1, chips)]
    greeted += [{"section": rem(section + step, sections)} for step in range(1, sections)]
    groups = tensors // joined
    for device in greeted:
        pl.semaphore_signal(barrier, inc=1, device_id=device, device_id_type=MESH)
    pl.semaphore_wait(barrier, len(greeted))

    @pl.when(section == last)
    def _():
        for index in range(per):
            own_copy(index).start()

    @pl.when(section != last)
    def _():
        for index in range(per):
            head_copy(index).start()

    for step in range(1, sections):
        loss_copy(section, rem(section + step, sections)).start()

    is_end = (chip == 0) | (chip == chips - 1)
    ahead = 2

    def launch(step):
        @pl.when((section == last) & (step < per))
        def _():
            own_copy(jnp.minimum(step, per - 1)).wait()

        @pl.when((section != last) | (step >= per))
        def _():
            down_copy(step).wait_recv()

        @pl.when(is_end)
        def _():
            for index in range(1, chips):
                line_copy(step, chip, jnp.where(chip == 0, index, chips - 1 - index)).start()

        if chips > 2:
            @pl.when(jnp.logical_not(is_end))
            def _():
                line_copy(step, chip, chip + 1).start()
                line_copy(step, chip, chip - 1).start()

        mate_copy(step, chip, core).start()

    def assemble(step, first):
        for part in range(pack):
            pieces = []
            for offset in range(joined):
                piece = held[first + offset, packed_of(step), :]
                pieces.append(piece[:, part * features : (part + 1) * features])
            rows = pl.ds(pl.multiple_of(share_of(step) * size + part * depth, depth), depth)
            lanes = pl.ds(pl.multiple_of(first * features, 128), span)
            carried[rows, lanes] = jnp.concatenate(pieces, axis=1)

    def product(step, first, fresh):
        lanes = pl.ds(pl.multiple_of(first * features, 128), span)
        value = jnp.dot(carried[rows_of(step), lanes], flipped[lanes, :], preferred_element_type=jnp.float32)
        acc_ref[...] = value if fresh else acc_ref[...] + value

    def finish(step, index):
        origin = origin_of(chips, chip, index)
        mate_copy(step, origin, 1 - core).wait_recv()
        if joined == 2:
            assemble(step, origin * 2)
            product(step, origin * 2, index == 0)
        elif index == chips - 1:
            assemble(step, 0)
            product(step, 0, True)

    @pl.when(section == last)
    def _():
        for index in range(ahead):
            launch(index)

    for index in range(min(groups, 2)):
        weight_copy(index).start()
    vectors[...] = jnp.zeros_like(vectors)

    def flip(index, inner):
        slot = rem(index, 2)
        weight_copy(index).wait()
        lanes = pl.ds(pl.multiple_of(index * span, 128), span)
        flipped[lanes, :] = stage[slot].T
        for start in range(0, features, 16):
            entries = stage[slot, start : start + 16, :].astype(jnp.float32)
            inner = inner + jnp.sum(jnp.reshape(entries * entries, (2, 8, span)), axis=0)

        @pl.when(index + 2 < groups)
        def _():
            weight_copy(index + 2).start()

        return inner

    squares = lax.fori_loop(0, groups, flip, jnp.zeros((8, span), jnp.float32))
    vectors[1, pl.ds(used + 1, 1), :] = jnp.broadcast_to(jnp.sum(squares, keepdims=True), (1, group))

    @pl.when(section != last)
    def _():
        for index in range(ahead):
            launch(index)

    half = count // 2
    low = tokens // 2
    pieces = 4 if half % 4 == 0 and width % 512 == 0 else 1
    stride = half // pieces
    cut = width // pieces

    def advance(step, carry):
        for index in range(1, chips):
            if index == min(2, chips - 1):
                @pl.when(step + ahead < count)
                def _():
                    launch(jnp.minimum(step + ahead, count - 1))

            origin = origin_of(chips, chip, index)
            line_copy(step, origin, chip).wait_recv()
            onward, wanted = onward_of(chips, chip, origin)

            @pl.when(wanted)
            def _():
                line_copy(step, origin, jnp.clip(onward, 0, chips - 1)).start()

            mate_copy(step, origin, core).start()
            finish(step, index - 1)
        finish(step, chips - 1)
        sums = jnp.concatenate([acc_ref[part * depth : (part + 1) * depth, :] for part in range(pack)], axis=1)
        mine = held[me, packed_of(step), :].astype(jnp.float32)
        out_ref[packed_of(step), :] = (mine + sums).astype(out_ref.dtype)

        @pl.when(section > 0)
        def _():
            down_copy(step).start()

        @pl.when((step >= half) & (rem(step, stride) == 0))
        def _():
            lanes = pl.ds(pl.multiple_of((step - half) // stride * cut, 128), cut)
            grad[:, lanes] = jnp.dot(
                x_ref[:, low:], carried[low:, lanes], preferred_element_type=jnp.float32
            )

        return carry

    lax.fori_loop(0, count, advance, 0)

    row_acc[...] = jnp.zeros_like(row_acc)

    def stage_copy(index):
        lanes = pl.ds(pl.multiple_of(index * group, 128), group)
        slot = rem(index, 2)
        return pltpu.make_async_copy(stage.at[slot, :, pl.ds(0, group)], grad_out.at[:, lanes], stage_sem.at[slot])

    def gather_squares(index, carry):
        lanes = pl.ds(pl.multiple_of(index * group, 128), group)
        value = grad[:, lanes] + jnp.dot(
            x_ref[:, :low], carried[:low, lanes], preferred_element_type=jnp.float32
        )
        grad[:, lanes] = value

        @pl.when(index > 1)
        def _():
            stage_copy(index - 2).wait()

        slot = rem(index, 2)
        inner = jnp.zeros((8, group), jnp.float32)
        for start in range(0, features, 16):
            entries = grad[start : start + 16, lanes]
            stage[slot, start : start + 16, :group] = entries.astype(stage.dtype)
            squares = entries * entries + tiny_term
            folded = squares[:, :128]
            for lane in range(128, group, 128):
                folded = folded + squares[:, lane : lane + 128]
            row_acc[start : start + 16, :] = row_acc[start : start + 16, :] + folded
            inner = inner + jnp.sum(jnp.reshape(squares, (2, 8, group)), axis=0)
        vectors[0, pl.ds(index, 1), :] = jnp.sum(inner, axis=0, keepdims=True)
        stage_copy(index).start()
        return carry

    lax.fori_loop(0, used, gather_squares, 0)

    def mate_sum():
        return remote(vectors.at[1 - core], near, send_sum.at[0], recv_sum.at[0], {"tensor": mate})

    def far_sum(source, there):
        return remote(
            pair_sum, spread.at[source], send_far.at[there], recv_far.at[source], {"tensor": there * 2 + core}
        )

    def mate_total(side):
        return remote(final.at[side], final.at[side], send_sum.at[1], recv_sum.at[1], {"tensor": mate})

    others = [rem(chip + step, chips) for step in range(1, chips)]

    def spread_pair():
        mate_sum().wait_recv()
        pair_sum[...] = vectors[core] + near[...]
        for there in others:
            far_sum(chip, there).start()
        spread[chip] = pair_sum[...]

    @pl.when(core == 1)
    def _():
        mate_sum().start()

    sums = jnp.sum(row_acc[...], axis=1, keepdims=True)
    old_row = jnp.broadcast_to(row_ref[...], (128, features)).T[:, :1]
    fresh_row = decay_rate * old_row + (1.0 - decay_rate) * (sums / width)
    row_out[...] = fresh_row
    vectors[1, pl.ds(used, 1), :] = jnp.broadcast_to(jnp.sum(fresh_row, keepdims=True), (1, group))
    row_full[...] = jnp.broadcast_to(1.0 / fresh_row, row_full.shape)

    def gather_scaled(index, carry):
        lanes = pl.ds(pl.multiple_of(index * group, 128), group)
        inner = jnp.zeros((8, group), jnp.float32)
        for start in range(0, features, 16):
            entries = grad[start : start + 16, lanes]
            shrink = jnp.concatenate([row_full[start : start + 16, :]] * (group // 128), axis=1)
            inner = inner + jnp.sum(jnp.reshape(entries * entries * shrink, (2, 8, group)), axis=0)
        vectors[1, pl.ds(index, 1), :] = jnp.sum(inner, axis=0, keepdims=True)
        return carry

    @pl.when(core == 0)
    def _():
        spread_pair()

    lax.fori_loop(0, used, gather_scaled, 0)

    @pl.when(core == 0)
    def _():
        mate_sum().start()

    @pl.when(core == 1)
    def _():
        spread_pair()

    for there in others:
        far_sum(there, there).wait_recv()
    final[core] = jnp.sum(spread[...], axis=0)
    mate_total(core).start()

    total = None
    for step in range(1, sections):
        other = rem(section + step, sections)
        loss_copy(other, other).wait_recv()
    loss_buf[section] = loss_ref[...]
    total_ref[...] = jnp.sum(loss_buf[...], axis=0)

    mate_total(1 - core).wait_recv()

    entries = float(width * width)
    row_total = final[1, used : used + 1, :][:, :1]
    weight_total = final[1, used + 1 : used + 2, :][:, :1]

    def update_columns(index, inner):
        lanes = pl.ds(pl.multiple_of(index * group, 128), group)
        fresh = decay_rate * col_ref[:, lanes] + (1.0 - decay_rate) * (final[0, pl.ds(index, 1), :] / width)
        col_out[:, lanes] = fresh
        col_scale[:, lanes] = lax.rsqrt(fresh)
        return inner + final[1, pl.ds(index, 1), :] / fresh

    scaled = lax.fori_loop(0, used, update_columns, jnp.zeros((1, group), jnp.float32))
    update_total = row_total * jnp.sum(scaled, axis=1, keepdims=True)
    factor = (
        learn_rate * jnp.sqrt(weight_total / entries)
        / jnp.maximum(1.0, jnp.sqrt(update_total / entries))
    )
    row_scale[...] = lax.rsqrt(row_out[...]) * (factor * jnp.sqrt(row_total))
    for index in (used - 2, used - 1):
        stage_copy(index).wait()

    def drain(step, carry):
        @pl.when(section > 0)
        def _():
            down_copy(step).wait_send()

        @pl.when(is_end)
        def _():
            for index in range(1, chips):
                line_copy(step, chip, jnp.where(chip == 0, index, chips - 1 - index)).wait_send()

        if chips > 2:
            @pl.when(jnp.logical_not(is_end))
            def _():
                line_copy(step, chip, chip + 1).wait_send()
                line_copy(step, chip, chip - 1).wait_send()

        mate_copy(step, chip, core).wait_send()
        for index in range(1, chips):
            origin = origin_of(chips, chip, index)
            onward, wanted = onward_of(chips, chip, origin)

            @pl.when(wanted)
            def _():
                line_copy(step, origin, jnp.clip(onward, 0, chips - 1)).wait_send()

            mate_copy(step, origin, core).wait_send()
        return carry

    lax.fori_loop(0, count, drain, 0)
    for step in range(1, sections):
        loss_copy(section, rem(section + step, sections)).wait_send()

    @pl.when(section != last)
    def _():
        for index in range(per):
            head_copy(index).wait_send()

    mate_sum().wait_send()
    for there in others:
        far_sum(chip, there).wait_send()
    mate_total(core).wait_send()


def update_kernel(
    pack, size, scale_ref, col_ref, carried_ref, row_ref, col_in, total_ref, weight_ref, grad_ref,
    weight_out, carried_out, row_out, col_out, loss_out, entries_buf, grad_buf, weight_sem, grad_sem, out_sem,
):
    count, rows, width = entries_buf.shape
    group = 512 if width % 512 == 0 else 128
    features, tokens = carried_out.shape

    def rows_of(index):
        return pl.ds(pl.multiple_of(index * rows, 16), rows)

    def weight_copy(index):
        return pltpu.make_async_copy(weight_ref.at[rows_of(index), :], entries_buf.at[index], weight_sem.at[index])

    def grad_copy(index):
        return pltpu.make_async_copy(grad_ref.at[rows_of(index), :], grad_buf.at[index], grad_sem.at[index])

    def out_copy(index):
        return pltpu.make_async_copy(entries_buf.at[index], weight_out.at[rows_of(index), :], out_sem.at[index])

    def fetch(index, carry):
        weight_copy(index).start()
        grad_copy(index).start()
        return carry

    lax.fori_loop(0, count, fetch, 0)
    depth = size // pack
    for start in range(0, tokens, 128):
        pieces = []
        for share in range(start // size, (start + 128) // size):
            entries = carried_ref[share * depth : (share + 1) * depth, :].astype(jnp.float32)
            pieces += [entries[:, part * features : (part + 1) * features] for part in range(pack)]
        joined = jnp.concatenate(pieces, axis=0)
        carried_out[:, start : start + 128] = joined.T.astype(carried_out.dtype)
    row_out[...] = jnp.broadcast_to(row_ref[...], (features, 128)).T[:1, :]
    col_out[...] = col_in[...]
    loss_out[...] = total_ref[:1, :1] / tokens

    def change(index, carry):
        weight_copy(index).wait()
        grad_copy(index).wait()
        scales = scale_ref[rows_of(index), :]
        for start in range(0, rows, 16):
            scale = jnp.broadcast_to(scales[start : start + 16, :], (16, group))
            for lane in range(0, width, group):
                lanes = slice(lane, lane + group)
                moved = grad_buf[index, start : start + 16, lanes].astype(jnp.float32)
                moved = moved * (scale * col_ref[:, lanes])
                entries = entries_buf[index, start : start + 16, lanes].astype(jnp.float32)
                entries_buf[index, start : start + 16, lanes] = (entries - moved).astype(entries_buf.dtype)
        out_copy(index).start()
        return carry

    lax.fori_loop(0, count, change, 0)

    def finish(index, carry):
        out_copy(index).wait()
        return carry

    lax.fori_loop(0, count, finish, 0)


def update(pack, size, tokens, weight, grad, row_scale, col_scale, outputs, row_new, col_new, total):
    features, width = weight.shape
    rows = max(size for size in range(16, 65, 16) if features % size == 0)
    count = features // rows
    vmem = pl.BlockSpec(memory_space=pltpu.VMEM)
    hbm = pl.BlockSpec(memory_space=pl.ANY)
    dma = pltpu.SemaphoreType.DMA((count,))
    held = pltpu.VMEM((count, rows, width), jnp.bfloat16)
    return pl.pallas_call(
        functools.partial(update_kernel, pack, size),
        out_shape=(
            jax.ShapeDtypeStruct((features, width), jnp.bfloat16),
            jax.ShapeDtypeStruct((features, tokens), jnp.bfloat16),
            jax.ShapeDtypeStruct((1, features), jnp.float32),
            jax.ShapeDtypeStruct((1, width), jnp.float32),
            jax.ShapeDtypeStruct((1, 1), jnp.float32),
        ),
        in_specs=[vmem] * 6 + [hbm] * 2,
        out_specs=(hbm,) + (vmem,) * 4,
        scratch_shapes=[held, held, dma, dma, dma],
        compiler_params=pltpu.CompilerParams(vmem_limit_bytes=60 * 1024 * 1024),
    )(row_scale, col_scale, outputs, row_new, col_new, total, weight, grad)


def step(part, losses, saved, local_weight, row_state, col_state, pack, count):
    sections, tensors = lax.axis_size("section"), lax.axis_size("tensor")
    features, tokens = saved.shape
    width = features * tensors
    chips = tensors // 2
    size = tokens // count
    group = 512 if width % 512 == 0 else 128
    span = 2 * features if (2 * features) % 128 == 0 else width
    lines = -(-(width // group + 2) // 8) * 8
    dma = pltpu.SemaphoreType.DMA
    vmem = pl.BlockSpec(memory_space=pltpu.VMEM)
    hbm = pl.BlockSpec(memory_space=pl.ANY)
    single = pltpu.VMEM((lines, group), jnp.float32)
    outputs, grad, total, row_new, row_scale, col_new, col_scale = pl.pallas_call(
        functools.partial(step_kernel, sections, tensors, count, pack),
        out_shape=(
            jax.ShapeDtypeStruct((tokens // pack, pack * features), jnp.bfloat16),
            jax.ShapeDtypeStruct((features, width), jnp.bfloat16),
            jax.ShapeDtypeStruct((8, 128), jnp.float32),
            jax.ShapeDtypeStruct((features, 1), jnp.float32),
            jax.ShapeDtypeStruct((features, 1), jnp.float32),
            jax.ShapeDtypeStruct((1, width), jnp.float32),
            jax.ShapeDtypeStruct((1, width), jnp.float32),
        ),
        in_specs=[vmem] * 5 + [hbm],
        out_specs=(vmem, hbm) + (vmem,) * 5,
        scratch_shapes=[
            pltpu.VMEM((width, features), jnp.bfloat16),
            pltpu.VMEM((2, features, span), jnp.bfloat16),
            pltpu.VMEM((tensors, tokens // pack, pack * features), jnp.bfloat16),
            pltpu.VMEM((tokens, width), jnp.bfloat16),
            pltpu.VMEM((features, width), jnp.float32),
            pltpu.VMEM((size, features), jnp.float32),
            pltpu.VMEM((features, 128), jnp.float32),
            pltpu.VMEM((features, 128), jnp.float32),
            pltpu.VMEM((sections, 8, 128), jnp.float32),
            pltpu.VMEM((2, lines, group), jnp.float32),
            single,
            single,
            pltpu.VMEM((chips, lines, group), jnp.float32),
            pltpu.VMEM((2, lines, group), jnp.float32),
            dma((count,)),
            dma((count,)),
            dma((count, 2 * chips)),
            dma((count, chips)),
            dma((count, chips)),
            dma((count, chips)),
            dma((sections,)),
            dma((sections,)),
            dma((count // sections + 2,)),
            dma((count // sections,)),
            dma((2,)),
            dma((2,)),
            dma((chips,)),
            dma((chips,)),
            dma((2,)),
        ],
        compiler_params=pltpu.CompilerParams(
            collective_id=0, has_side_effects=True, vmem_limit_bytes=66_000_000
        ),
    )(part, losses, saved, row_state, col_state, local_weight)
    return update(pack, size, tokens, local_weight, grad, row_scale, col_scale, outputs, row_new, col_new, total)


def body(hidden_last, labels, head_weight, layer_inputs, weights, row_state, col_state):
    sections, tensors = lax.axis_size("section"), lax.axis_size("tensor")
    tokens, features = hidden_last.shape
    count = 4 * sections
    size = tokens // count
    pack = 2 if (2 * features) % 128 == 0 and (size // 2) % 16 == 0 else 1
    part, losses = head(hidden_last.T, labels.reshape(1, -1), head_weight.T, pack, count // sections)
    new_weight, outputs, row_new, col_new, loss = step(
        part, losses, layer_inputs[0].T, weights[0], row_state, col_state, pack, count
    )
    return (loss[0, 0], outputs.T[None], new_weight[None], row_new, col_new)


def solution(mesh):
    return jax.shard_map(
        body,
        mesh=mesh,
        in_specs=(
            P(None, "tensor"),
            P(),
            P(None, "tensor"),
            P("section", None, "tensor"),
            P("section", "tensor", None),
            P("section", "tensor"),
            P("section", None),
        ),
        out_specs=(
            P(),
            P("section", None, "tensor"),
            P("section", "tensor", None),
            P("section", "tensor"),
            P("section", None),
        ),
        check_vma=False,
    )
```
